32 devices in a mesh: vseq: 8 (over y, x, core), aseq: 4 (over z).
Axes of the slice: x: 2, y: 2, z: 4, core: 2. Of those that a mesh axis runs over, the one named last changes fastest.
Arguments:
- video_q: bfloat16 [1536, 24, 128], P(('vseq', 'aseq'))
- video_k: bfloat16 [1536, 24, 128], P(('vseq', 'aseq'))
- video_v: bfloat16 [1536, 24, 128], P(('vseq', 'aseq')), may hold values from -6 to 6
- audio_q: bfloat16 [256, 24, 128], P(('vseq', 'aseq'))
- audio_k: bfloat16 [256, 24, 128], P(('vseq', 'aseq'))
- audio_v: bfloat16 [256, 24, 128], P(('vseq', 'aseq')), may hold values from -6 to 6
- video_x: bfloat16 [1536, 3072], P(('vseq', 'aseq')), may hold values from -3 to 3
- audio_x: bfloat16 [256, 3072], P(('vseq', 'aseq')), may hold values from -3 to 3
- video_out_w: bfloat16 [3072, 3072], P('aseq'), may hold values from -0.4375 to 0.4375
- audio_out_w: bfloat16 [3072, 3072], P('aseq'), may hold values from -0.4375 to 0.4375
- video_gate_w: bfloat16 [256, 3072], replicated, may hold values from -0.375 to 0.375
- audio_gate_w: bfloat16 [256, 3072], replicated, may hold values from -0.375 to 0.375
- levels: int32 [8], replicated, may hold values from 0 to 999
- video_pos: int32 [8], replicated, may hold values from 0 to 166, as said below
- audio_pos: int32 [256], P(('vseq', 'aseq')), may hold values from 0 to 197, as said below
Outputs:
- video_out: bfloat16 [1536, 3072], P(('vseq', 'aseq'))
- audio_out: bfloat16 [256, 3072], P(('vseq', 'aseq'))
The draws below stay inside these ranges and needn't reach their ends.
Inputs may be any that keep to these rules, and one draw needn't show every extreme that they name: `video_pos`: the first frame lies at 0; strictly increasing, consecutive frames 16 to 32 apart; the last frame lies at 166. `audio_pos`: non-decreasing; audio token f * 32 has exactly the position video_pos[f], and tokens f * 32 to (f + 1) * 32 - 1 lie before video_pos[f + 1] where that frame exists, and within 31 of video_pos[f].
All inputs are finite; a program needn't handle non-finite values.
Results may differ from the reference program's by a relative error of at most 0.014.
Values may be sent and summed in bfloat16 or wider, within the bound.
A program may use at most 128 MiB of HBM per device.

```python
import math
import jax
import jax.numpy as jnp
from jax import lax

D = 3072
HEADS = 24
HD = 128
TEMB = 256
FRAMES = 8
GRID_W = 32
LEVELS = 1000
INNER = 3072
TV = 1536
TA = 256
FRAME_TOK = 192
SEG = 32


def drawn_rows(key, row_total):
    return jnp.clip(1.4 * jax.random.normal(key, (row_total, HEADS, HD), jnp.float32), -5.0, 5.0)


def draw_video_q(key, part):
    values = drawn_rows(jax.random.fold_in(key, 1), TV)
    return values.astype(jnp.bfloat16)


def draw_video_k(key, part):
    values = drawn_rows(jax.random.fold_in(key, 2), TV)
    return values.astype(jnp.bfloat16)


def draw_audio_q(key, part):
    values = drawn_rows(jax.random.fold_in(key, 3), TA)
    return values.astype(jnp.bfloat16)


def draw_audio_k(key, part):
    values = drawn_rows(jax.random.fold_in(key, 4), TA)
    return values.astype(jnp.bfloat16)


def timeline(key):
    line_key = jax.random.fold_in(key, 777)
    step_index = jnp.arange(FRAMES - 1, dtype=jnp.int32)
    inner_gaps = 16 + 16 * step_index // (FRAMES - 2)
    inner_gaps = jax.random.permutation(jax.random.fold_in(line_key, 1), inner_gaps)
    gaps = jnp.concatenate([inner_gaps, jnp.full((1,), 32, jnp.int32)]).astype(jnp.int32)
    video_places = jnp.cumsum(gaps).astype(jnp.int32) - gaps
    offsets = jax.random.randint(jax.random.fold_in(line_key, 3), (FRAMES, SEG), 0, gaps[:, None], dtype=jnp.int32)
    offsets = jnp.sort(offsets.at[:, 0].set(0), axis=1)
    offsets = offsets.at[:, SEG - 1].set(gaps - 1)
    audio_places = (video_places[:, None] + offsets).reshape(TA)
    return (video_places.astype(jnp.int32), audio_places.astype(jnp.int32))


def draw_video_pos(key, part):
    video_places, audio_places = timeline(key)
    return video_places


def draw_audio_pos(key, part):
    video_places, audio_places = timeline(key)
    return audio_places


def with_ends(array, stream_key, smallest, largest):
    place = [jax.random.randint(jax.random.fold_in(stream_key, axis), (), 0, length) for axis, length in enumerate(array.shape)]
    main_axis = array.shape.index(max(array.shape))
    next_to = place[:main_axis] + [(place[main_axis] + 1) % array.shape[main_axis]] + place[main_axis + 1:]
    return array.at[tuple(place)].set(smallest).at[tuple(next_to)].set(largest)


def steps_of(rng, shape, cuts, least, top_value):
    level, own = 1.0, jax.random.fold_in(rng, 6)
    for position, shards_of in cuts:
        heights = jnp.exp(jax.random.uniform(jax.random.fold_in(own, position), (shards_of,), jnp.float32, least / len(cuts), top_value / len(cuts)))
        level = level * jnp.repeat(heights, shape[position] // shards_of).reshape([-1 if axis == position else 1 for axis in range(len(shape))])
    return level


def noise(own_key, shape, spread, reach, cuts=(), held_as=jnp.bfloat16):
    loudness = steps_of(own_key, shape, cuts, -0.22, 0.18) if cuts else 1.0
    drawn = jax.random.normal(own_key, shape, jnp.float32) * spread * loudness
    return jnp.minimum(jnp.maximum(drawn, -reach), reach).astype(held_as)


def setup_inputs(seed: int = 0) -> dict:
    arg_keys = jax.random.split(jax.random.key(seed), 16)
    return {
        "video_q": draw_video_q(jax.random.fold_in(arg_keys[15], 71), 0),
        "video_k": draw_video_k(jax.random.fold_in(arg_keys[15], 71), 0),
        "video_v": noise(arg_keys[2], (TV, HEADS, HD), 1.0, 6.0, ((0, 32),)),
        "audio_q": draw_audio_q(jax.random.fold_in(arg_keys[15], 71), 0),
        "audio_k": draw_audio_k(jax.random.fold_in(arg_keys[15], 71), 0),
        "audio_v": noise(arg_keys[5], (TA, HEADS, HD), 1.0, 6.0, ((0, 32),)),
        "video_x": noise(arg_keys[6], (TV, D), 0.5, 3.0, ((0, 32),)),
        "audio_x": noise(arg_keys[7], (TA, D), 0.5, 3.0, ((0, 32),)),
        "video_out_w": noise(arg_keys[8], (INNER, D), (INNER // 16) ** -0.5, 0.4375, ((0, 4),)),
        "audio_out_w": noise(arg_keys[9], (INNER, D), (INNER // 16) ** -0.5, 0.4375, ((0, 4),)),
        "video_gate_w": noise(arg_keys[10], (TEMB, D), TEMB ** -0.5, 0.375),
        "audio_gate_w": noise(arg_keys[11], (TEMB, D), TEMB ** -0.5, 0.375),
        "levels": with_ends(jax.random.randint(arg_keys[12], (FRAMES,), 0, LEVELS), jax.random.fold_in(arg_keys[12], 1), 0, LEVELS - 1).astype(jnp.int32),
        "video_pos": draw_video_pos(jax.random.fold_in(arg_keys[15], 71), 0),
        "audio_pos": draw_audio_pos(jax.random.fold_in(arg_keys[15], 71), 0),
    }


flow_shift = 5.0

def rotate(values, place_t, place_h, place_w):
    head_dim = values.shape[-1]
    one_sixth = head_dim // 6
    first_width = head_dim - 4 * one_sixth
    outputs = []
    sections = ((0, first_width, place_t), (first_width, 2 * one_sixth, place_h), (first_width + 2 * one_sixth, 2 * one_sixth, place_w))
    for start_col, width, places in sections:
        half_width = width // 2
        frequency = 10000.0 ** (-(jnp.arange(half_width, dtype=jnp.float32) * 2.0) / width)
        angles = places.astype(jnp.float32)[:, None] * frequency[None, :]
        cos_part = jnp.cos(angles)[:, None, :]
        sine_part = jnp.sin(angles)[:, None, :]
        low_half = values[..., start_col:start_col + half_width]
        high_half = values[..., start_col + half_width:start_col + width]
        outputs.append(low_half * cos_part - high_half * sine_part)
        outputs.append(low_half * sine_part + high_half * cos_part)
    return jnp.concatenate(outputs, axis=-1)

def frame_gates(levels, gate_w):
    level_frac = (levels.astype(jnp.float32) + 1.0) / LEVELS
    timestep = 1000.0 * flow_shift * level_frac / (1.0 + (flow_shift - 1.0) * level_frac)
    half_emb = gate_w.shape[0] // 2
    frequency = jnp.exp(-math.log(10000.0) * jnp.arange(half_emb, dtype=jnp.float32) / half_emb)
    angles = timestep[:, None] * frequency[None, :]
    embedding = jnp.concatenate([jnp.cos(angles), jnp.sin(angles)], axis=1)
    return jnp.dot(embedding, gate_w.astype(jnp.float32), precision=lax.Precision.HIGHEST, preferred_element_type=jnp.float32)

def attend(queries, keys_all, values_all):
    row_count, head_count, head_dim = queries.shape
    score_scale = 1.0 / math.sqrt(head_dim)
    block_rows = math.gcd(row_count, 512)
    query_heads = jnp.transpose(queries, (1, 0, 2))
    key_heads = jnp.transpose(keys_all, (1, 0, 2))
    value_heads = jnp.transpose(values_all, (1, 0, 2))

    def one_head(triple):
        q_head, k_head, v_head = triple
        q_blocks = q_head.reshape(row_count // block_rows, block_rows, head_dim)

        def one_block(q_block):
            scores = jnp.dot(q_block, k_head.T, preferred_element_type=jnp.float32) * score_scale
            row_max = lax.optimization_barrier(jnp.max(scores, axis=1, keepdims=True))
            weights = jnp.exp(scores - row_max)
            row_sum = lax.optimization_barrier(jnp.sum(weights, axis=1, keepdims=True))
            blended = jnp.dot(weights.astype(jnp.bfloat16), v_head, preferred_element_type=jnp.float32)
            return (blended / row_sum).astype(jnp.bfloat16)
        return lax.map(one_block, q_blocks).reshape(row_count, head_dim)
    result = lax.map(one_head, (query_heads, key_heads, value_heads))
    return jnp.transpose(result, (1, 0, 2)).reshape(row_count, head_count * head_dim)

def reference(video_q, video_k, video_v, audio_q, audio_k, audio_v, video_x, audio_x, video_out_w, audio_out_w, video_gate_w, audio_gate_w, levels, video_pos, audio_pos):
    token_index = jnp.arange(TV, dtype=jnp.int32)
    frame_of = token_index // FRAME_TOK
    within = token_index % FRAME_TOK
    place_t = video_pos[frame_of]
    place_h = within // GRID_W
    place_w = within % GRID_W
    video_query = rotate(video_q.astype(jnp.float32), place_t, place_h, place_w).astype(jnp.bfloat16)
    video_key = rotate(video_k.astype(jnp.float32), place_t, place_h, place_w).astype(jnp.bfloat16)
    audio_frame = lax.optimization_barrier(jnp.sum((video_pos[None, :] <= audio_pos[:, None]).astype(jnp.int32), axis=1)) - 1
    zero_place = jnp.zeros_like(audio_pos)
    audio_query = rotate(audio_q.astype(jnp.float32), audio_pos, zero_place, zero_place).astype(jnp.bfloat16)
    audio_key = rotate(audio_k.astype(jnp.float32), audio_pos, zero_place, zero_place).astype(jnp.bfloat16)
    keys_all = jnp.concatenate([video_key, audio_key], axis=0)
    values_all = jnp.concatenate([video_v, audio_v], axis=0)
    video_attn = attend(video_query, keys_all, values_all)
    audio_attn = attend(audio_query, keys_all, values_all)
    video_gates = frame_gates(levels, video_gate_w)
    audio_gates = frame_gates(levels, audio_gate_w)
    video_proj = jnp.dot(video_attn, video_out_w, preferred_element_type=jnp.float32)
    audio_proj = jnp.dot(audio_attn, audio_out_w, preferred_element_type=jnp.float32)
    video_out = (video_x.astype(jnp.float32) + video_gates[frame_of] * video_proj).astype(jnp.bfloat16)
    audio_out = (audio_x.astype(jnp.float32) + audio_gates[audio_frame] * audio_proj).astype(jnp.bfloat16)
    return (video_out, audio_out)
```

```python
import functools
import math

import jax
import jax.numpy as jnp
import numpy as np
from jax import lax
from jax.experimental import pallas as pl
from jax.experimental.pallas import tpu as pltpu
from jax.sharding import PartitionSpec as P

GRID_W = 32
LEVELS = 1000
flow_shift = 5.0


def rope_tables(head_dim, place_t, place_h, place_w):
    one_sixth = head_dim // 6
    first = head_dim - 4 * one_sixth
    cos_cols, sin_cols = [], []
    for width, places in ((first, place_t), (2 * one_sixth, place_h), (2 * one_sixth, place_w)):
        half = width // 2
        frequency = 10000.0 ** (-(jnp.arange(half, dtype=jnp.float32) * 2.0) / width)
        angles = places.astype(jnp.float32)[:, None] * frequency[None, :]
        cos_part, sin_part = jnp.cos(angles), jnp.sin(angles)
        cos_cols += [cos_part, cos_part]
        sin_cols += [-sin_part, sin_part]
    return jnp.concatenate(cos_cols, axis=1), jnp.concatenate(sin_cols, axis=1)


def swap_matrix(head_dim):
    one_sixth = head_dim // 6
    first = head_dim - 4 * one_sixth
    source = []
    start = 0
    for width in (first, 2 * one_sixth, 2 * one_sixth):
        half = width // 2
        source += list(range(start + half, start + width)) + list(range(start, start + half))
        start += width
    return jnp.asarray(np.arange(head_dim)[:, None] == np.array(source)[None, :], jnp.bfloat16)


def embedding_of(levels, half_emb):
    level_frac = (levels.astype(jnp.float32) + 1.0) / LEVELS
    timestep = 1000.0 * flow_shift * level_frac / (1.0 + (flow_shift - 1.0) * level_frac)
    frequency = jnp.exp(-math.log(10000.0) * jnp.arange(half_emb, dtype=jnp.float32) / half_emb)
    angles = timestep[:, None] * frequency[None, :]
    return jnp.concatenate([jnp.cos(angles), jnp.sin(angles)], axis=1)


def gather_kernel(
    A, V, rows, qkv_ref, ev_ref, ea_ref, gwv_ref, gwa_ref, q_out, kv_out, gv_ref, ga_ref, loc_sem, zs, zr, qs, qr, fs, fr
):
    a = lax.axis_index("aseq")
    v = lax.axis_index("vseq")

    def at_z(k):
        return {"aseq": jnp.bitwise_xor(a, k)}

    def at_v(m):
        return {"vseq": jnp.bitwise_xor(v, m)}

    ring = V == 8
    v_peers = (1, 2, 4) if ring else tuple(range(1, V))
    barrier = pltpu.get_barrier_semaphore()
    for k in range(1, A):
        pl.semaphore_signal(barrier, 1, device_id=at_z(k), device_id_type=pl.DeviceIdType.MESH)
    for m in v_peers:
        pl.semaphore_signal(barrier, 1, device_id=at_v(m), device_id_type=pl.DeviceIdType.MESH)
    pl.semaphore_wait(barrier, A - 1 + len(v_peers))

    def spot(m, k, which=None):
        at = (jnp.bitwise_xor(v, m) * A + jnp.bitwise_xor(a, k)) * rows
        at = pl.ds(pl.multiple_of(at, 8), rows)
        if which is None:
            return kv_out.at[:, :, at, :]
        return kv_out.at[pl.ds(which, 1), :, at, :]

    def q_spot():
        return q_out.at[:, pl.ds(pl.multiple_of(a * rows, 8), rows), :]

    def send(src, dst, ssem, rsem, device):
        copy = pltpu.make_async_remote_copy(
            src_ref=src, dst_ref=dst, send_sem=ssem, recv_sem=rsem,
            device_id=device, device_id_type=pl.DeviceIdType.MESH,
        )
        copy.start()
        return copy

    own_kv = pltpu.make_async_copy(qkv_ref.at[a, pl.ds(1, 2)], spot(0, 0), loc_sem.at[0])
    own_kv.start()
    own_q = pltpu.make_async_copy(qkv_ref.at[a, 0], q_spot(), loc_sem.at[1])
    own_q.start()
    order = [1] + list(range(A - 1, 1, -1))
    z_copies, q_copies = {}, {}
    for k in order:
        z_copies[k] = send(
            qkv_ref.at[jnp.bitwise_xor(a, k), pl.ds(1, 2)], spot(0, 0), zs.at[k], zr.at[k], at_z(k)
        )
    sent = []

    def forward(m, k, which, slot, target):
        copy = send(spot(m, k, which), spot(m, k, which), fs.at[slot, k], fr.at[slot, k], at_v(target))
        sent.append(copy)
        return copy

    got = {}

    def stage_z(k):
        if k == 0:
            own_kv.wait()
        else:
            z_copies[k].wait_recv()
        if ring:
            got["x", k] = forward(0, k, None, 0, 2)
            got["y", k] = forward(0, k, None, 1, 4)
            got["c", k] = forward(0, k, None, 2, 1)
        else:
            for m in v_peers:
                got[m, k] = forward(0, k, None, m, m)

    def stage_xy(k):
        got["x", k].wait_recv()
        got["dk", k] = forward(2, k, 0, 3, 4)
        got["cx", k] = forward(2, k, None, 4, 1)
        got["y", k].wait_recv()
        got["dv", k] = forward(4, k, 1, 5, 2)
        got["cy", k] = forward(4, k, None, 6, 1)

    def stage_d(k):
        got["dk", k].wait_recv()
        got["cdk", k] = forward(6, k, 0, 7, 1)
        got["dv", k].wait_recv()
        got["cdv", k] = forward(6, k, 1, 8, 1)

    stages = [0] + order
    for step in range(A + 2):
        if step < A:
            stage_z(stages[step])
        if step == 0:
            for k in order:
                q_copies[k] = send(
                    qkv_ref.at[jnp.bitwise_xor(a, k), 0], q_spot(), qs.at[k], qr.at[k], at_z(k)
                )
            for e_ref, w_ref, g_ref in ((ev_ref, gwv_ref, gv_ref), (ea_ref, gwa_ref, ga_ref)):
                parts = jnp.dot(e_ref[...], w_ref[...], preferred_element_type=jnp.float32)
                n = g_ref.shape[0]
                g_ref[...] = parts[:n] + parts[n : 2 * n] + parts[2 * n :]
        if ring:
            if 1 <= step < A + 1:
                stage_xy(stages[step - 1])
            if 2 <= step:
                stage_d(stages[step - 2])
    for k in range(A):
        if ring:
            for name in ("c", "cx", "cy", "cdk", "cdv"):
                got[name, k].wait_recv()
        else:
            for m in v_peers:
                got[m, k].wait_recv()
    own_q.wait()
    for k in order:
        q_copies[k].wait()
        z_copies[k].wait_send()
    for copy in sent:
        copy.wait_send()


def gather(qkv, ev, ea, gwv, gwa, A, V):
    _, _, heads, rows, hd = qkv.shape
    slots = 9 if V == 8 else V
    return pl.pallas_call(
        functools.partial(gather_kernel, A, V, rows),
        out_shape=(
            jax.ShapeDtypeStruct((heads, A * rows, hd), qkv.dtype),
            jax.ShapeDtypeStruct((2, heads, V * A * rows, hd), qkv.dtype),
            jax.ShapeDtypeStruct((ev.shape[0] // 3, gwv.shape[1]), jnp.float32),
            jax.ShapeDtypeStruct((ea.shape[0] // 3, gwa.shape[1]), jnp.float32),
        ),
        in_specs=[pl.BlockSpec(memory_space=pl.ANY)] + [pl.BlockSpec(memory_space=pltpu.VMEM)] * 4,
        out_specs=(pl.BlockSpec(memory_space=pl.ANY),) * 2
        + (pl.BlockSpec(memory_space=pltpu.VMEM),) * 2,
        scratch_shapes=[
            pltpu.SemaphoreType.DMA((2,)),
            pltpu.SemaphoreType.DMA((A,)),
            pltpu.SemaphoreType.DMA((A,)),
            pltpu.SemaphoreType.DMA((A,)),
            pltpu.SemaphoreType.DMA((A,)),
            pltpu.SemaphoreType.DMA((slots, A)),
            pltpu.SemaphoreType.DMA((slots, A)),
        ],
        compiler_params=pltpu.CompilerParams(collective_id=0, has_side_effects=True),
        name="gather_heads",
    )(qkv, ev, ea, gwv, gwa)


def attend_kernel(A, vrows, arows, step_keys, q_ref, kv_ref, v_ref, vo_ref, ao_ref):
    q = q_ref[0]
    keys = kv_ref.shape[2]
    scale = math.log2(math.e) / math.sqrt(q.shape[1])
    top, total, acc = None, None, None
    for start in range(0, keys, step_keys):
        k = kv_ref[0, 0, pl.ds(start, step_keys), :]
        vv = v_ref[0, 0, pl.ds(start, step_keys), :]
        s = lax.dot_general(q, k, (((1,), (1,)), ((), ())), preferred_element_type=jnp.float32)
        new_top = jnp.max(s, axis=1, keepdims=True)
        if top is not None:
            new_top = jnp.maximum(new_top, top)
        w = jnp.exp2((s - new_top) * scale)
        part = jnp.sum(w, axis=1, keepdims=True)
        mixed = jnp.dot(w.astype(jnp.bfloat16), vv, preferred_element_type=jnp.float32)
        if top is None:
            total, acc = part, mixed
        else:
            f = jnp.exp2((top - new_top) * scale)
            total, acc = total * f + part, acc * f + mixed
        top = new_top
    o = acc / total
    rows = vrows + arows
    for i in range(A):
        vo_ref[pl.ds(i * vrows, vrows), :] = o[i * rows : i * rows + vrows].astype(vo_ref.dtype)
    ao_ref[...] = jnp.concatenate(
        [o[i * rows + vrows : (i + 1) * rows] for i in range(A)], axis=0
    ).astype(ao_ref.dtype)


def attend(q, kv, A, vrows, arows):
    heads, qrows, hd = q.shape
    keys = kv.shape[2]
    step_keys = keys if keys <= 2048 else 1792
    while keys % step_keys:
        step_keys -= 128
    return pl.pallas_call(
        functools.partial(attend_kernel, A, vrows, arows, step_keys),
        grid=(heads,),
        out_shape=(
            jax.ShapeDtypeStruct((A * vrows, heads * hd), q.dtype),
            jax.ShapeDtypeStruct((A * arows, heads * hd), q.dtype),
        ),
        in_specs=[
            pl.BlockSpec((1, qrows, hd), lambda h: (h, 0, 0)),
            pl.BlockSpec((1, 1, keys, hd), lambda h: (0, h, 0, 0)),
            pl.BlockSpec((1, 1, keys, hd), lambda h: (1, h, 0, 0)),
        ],
        out_specs=(
            pl.BlockSpec((A * vrows, hd), lambda h: (0, h)),
            pl.BlockSpec((A * arows, hd), lambda h: (0, h)),
        ),
        compiler_params=pltpu.CompilerParams(dimension_semantics=("arbitrary",)),
        name="attend_heads",
    )(q, kv, kv)


def project_kernel(
    A, nC, cw, vrows, arows,
    va_ref, aa_ref, wv_hbm, wa_hbm, xv_ref, xa_ref, gv_ref, ga_ref,
    vo_ref, ao_ref,
    wv, wa, own, up_in, dn_in, up_out, dn_out, w_sem, us, ur, ds_, dr,
):
    p = lax.axis_index("aseq")
    loads = []
    for c in range(nC):
        cols = pl.ds(c * cw, cw)
        one = pltpu.make_async_copy(wv_hbm.at[:, cols], wv.at[c], w_sem.at[0, c])
        two = pltpu.make_async_copy(wa_hbm.at[:, cols], wa.at[c], w_sem.at[1, c])
        one.start()
        two.start()
        loads.append((one, two))
    above = {"aseq": jnp.minimum(p + 1, A - 1)}
    below = {"aseq": jnp.maximum(p - 1, 0)}
    MESH = pl.DeviceIdType.MESH
    barrier = pltpu.get_barrier_semaphore()

    for k in range(1, A):
        peer = {"aseq": jnp.bitwise_xor(p, k)}
        pl.semaphore_signal(barrier, 1, device_id=peer, device_id_type=MESH)
    pl.semaphore_wait(barrier, A - 1)

    def up_copy(d, c):
        return pltpu.make_async_remote_copy(
            src_ref=up_out.at[d, c], dst_ref=up_in.at[d, c],
            send_sem=us.at[d, c], recv_sem=ur.at[d, c], device_id=above, device_id_type=MESH,
        )

    def dn_copy(d, c):
        return pltpu.make_async_remote_copy(
            src_ref=dn_out.at[d, c], dst_ref=dn_in.at[d, c],
            send_sem=ds_.at[d, c], recv_sem=dr.at[d, c], device_id=below, device_id_type=MESH,
        )

    def multiply(c):
        one, two = loads[c]
        one.wait()
        pv = jnp.dot(va_ref[...], wv[c], preferred_element_type=jnp.float32)
        two.wait()
        pa = jnp.dot(aa_ref[...], wa[c], preferred_element_type=jnp.float32)
        for d in range(A):
            own[d, c, pl.ds(0, vrows), :] = pv[d * vrows : (d + 1) * vrows]
            own[d, c, pl.ds(vrows, arows), :] = pa[d * arows : (d + 1) * arows]

        first_sends(0, c)

    def first_sends(i, c):
        @pl.when(p == 0)
        def _():
            up_out[A - 1 - i, c] = own[A - 1 - i, c].astype(up_out.dtype)
            up_copy(A - 1 - i, c).start()

        @pl.when(p == A - 1)
        def _():
            dn_out[i, c] = own[i, c].astype(dn_out.dtype)
            dn_copy(i, c).start()

    def relay(i, c):
        d = A - 1 - i

        @pl.when((p > 0) & (p < d))
        def _():
            up_copy(d, c).wait_recv()
            up_out[d, c] = (own[d, c] + up_in[d, c].astype(jnp.float32)).astype(up_out.dtype)
            up_copy(d, c).start()

        @pl.when((p < A - 1) & (p > i))
        def _():
            dn_copy(i, c).wait_recv()
            dn_out[i, c] = (own[i, c] + dn_in[i, c].astype(jnp.float32)).astype(dn_out.dtype)
            dn_copy(i, c).start()

    for c in range(nC):
        multiply(c)
    for i in range(1, A - 1):
        for c in range(nC):
            first_sends(i, c)
    for i in range(A - 1):
        for c in range(nC):
            relay(i, c)

    for c in range(nC):
        @pl.when(p > 0)
        def _():
            up_copy(p, c).wait_recv()
            own[p, c] = own[p, c] + up_in[p, c].astype(jnp.float32)

        @pl.when(p < A - 1)
        def _():
            dn_copy(p, c).wait_recv()
            own[p, c] = own[p, c] + dn_in[p, c].astype(jnp.float32)

        cols = pl.ds(c * cw, cw)
        gate = gv_ref[:, cols] if gv_ref.shape[0] == vrows else gv_ref[pl.ds(0, 1), cols]
        vo_ref[:, cols] = (
            xv_ref[:, cols].astype(jnp.float32) + gate * own[p, c, pl.ds(0, vrows), :]
        ).astype(vo_ref.dtype)
        ao_ref[:, cols] = (
            xa_ref[:, cols].astype(jnp.float32) + ga_ref[:, cols] * own[p, c, pl.ds(vrows, arows), :]
        ).astype(ao_ref.dtype)

    for c in range(nC):
        for d in range(A):
            @pl.when(p < d)
            def _():
                up_copy(d, c).wait_send()

            @pl.when(p > d)
            def _():
                dn_copy(d, c).wait_send()


def project(va, aa, wv, wa, xv, xa, gv, ga, A):
    vrows, width = xv.shape
    arows = xa.shape[0]
    inner = wv.shape[0]
    nC = 2
    cw = width // nC
    rows = vrows + arows
    vmem = pl.BlockSpec(memory_space=pltpu.VMEM)
    hbm = pl.BlockSpec(memory_space=pl.ANY)
    wire = pltpu.VMEM((A, nC, rows, cw), jnp.bfloat16)
    return pl.pallas_call(
        functools.partial(project_kernel, A, nC, cw, vrows, arows),
        out_shape=(
            jax.ShapeDtypeStruct(xv.shape, xv.dtype),
            jax.ShapeDtypeStruct(xa.shape, xa.dtype),
        ),
        in_specs=[vmem, vmem, hbm, hbm, vmem, vmem, vmem, vmem],
        out_specs=(vmem, vmem),
        scratch_shapes=[
            pltpu.VMEM((nC, inner, cw), wv.dtype),
            pltpu.VMEM((nC, inner, cw), wa.dtype),
            pltpu.VMEM((A, nC, rows, cw), jnp.float32),
            wire, wire, wire, wire,
            pltpu.SemaphoreType.DMA((2, nC)),
            pltpu.SemaphoreType.DMA((A, nC)),
            pltpu.SemaphoreType.DMA((A, nC)),
            pltpu.SemaphoreType.DMA((A, nC)),
            pltpu.SemaphoreType.DMA((A, nC)),
        ],
        compiler_params=pltpu.CompilerParams(
            collective_id=1, has_side_effects=True, vmem_limit_bytes=60 * 1024 * 1024
        ),
        name="project_sum",
    )(va, aa, wv, wa, xv, xa, gv, ga)


def fused_kernel(
    A, V, n_heads, nC, vrows, arows,
    vq_h, vk_h, vv_h, aq_h, ak_h, av_h, xv_h, xa_h, wv_h, wa_h, gwv_h, gwa_h, lane_h, swap_h,
    levels_ref, video_pos_ref, audio_pos_ref,
    vo_ref, ao_ref,
    raw_v, raw_a, flat, xv, xa, wv, wa, gwv, gwa, lane, swap,
    kvs, qs, kv, q, va, aa, own, up_in, dn_in, up_out, dn_out, gates,
    in_sem, w_sem, zs, zr, qss, qsr, fs, fr, us, ur, ds_, dr,
):
    a = lax.axis_index("aseq")
    v = lax.axis_index("vseq")
    MESH = pl.DeviceIdType.MESH
    rows = vrows + arows
    heads, hd = raw_v.shape[2], raw_v.shape[3]
    group = heads // A
    G = group // n_heads
    cw = wv.shape[2]
    f32, bf16 = jnp.float32, jnp.bfloat16

    def at_z(k):
        return {"aseq": jnp.bitwise_xor(a, k)}

    def at_v(m):
        return {"vseq": jnp.bitwise_xor(v, m)}

    barrier = pltpu.get_barrier_semaphore()
    for k in range(1, A):
        pl.semaphore_signal(barrier, 1, device_id=at_z(k), device_id_type=MESH)
    for m in (1, 2, 4):
        pl.semaphore_signal(barrier, 1, device_id=at_v(m), device_id_type=MESH)

    small = []
    for i, (src, dst) in enumerate(
        (
            (lane_h, lane), (swap_h, swap),
            (vk_h, raw_v.at[1]), (ak_h, raw_a.at[1]),
            (vv_h, raw_v.at[2]), (av_h, raw_a.at[2]),
            (vq_h, raw_v.at[0]), (aq_h, raw_a.at[0]),
            (xv_h, xv), (xa_h, xa), (gwv_h, gwv), (gwa_h, gwa),
        )
    ):
        copy = pltpu.make_async_copy(src, dst, in_sem.at[i])
        copy.start()
        small.append(copy)

    def load(c, which):
        cols = pl.ds(pl.multiple_of(c * cw, 128), cw)
        src, dst = ((wv_h, wv), (wa_h, wa))[which]
        return pltpu.make_async_copy(src.at[:, cols], dst.at[c], w_sem.at[which, c])

    small[0].wait()
    frame = v
    row = lax.broadcasted_iota(jnp.int32, (vrows, hd), 0)
    within = a * vrows + row
    at_h = lax.div(within, GRID_W)
    at_w = within - at_h * GRID_W
    place_t = video_pos_ref[frame].astype(f32)
    freq = lane[pl.ds(0, 1), :]
    sign = lane[pl.ds(1, 1), :]
    is_t, is_h, is_w = (lane[pl.ds(i, 1), :] for i in (2, 3, 4))
    video_place = place_t * is_t + at_h.astype(f32) * is_h + at_w.astype(f32) * is_w
    audio_row = lax.broadcasted_iota(jnp.int32, (arows, hd), 0)
    audio_at = jnp.zeros((arows, hd), f32)
    for i in range(arows):
        audio_at = jnp.where(audio_row == i, audio_pos_ref[i].astype(f32), audio_at)
    angle = jnp.concatenate([video_place, audio_at * is_t], axis=0) * freq
    cos, sin = jnp.cos(angle), jnp.sin(angle) * sign

    own_slot = v * A + a

    def flatten(which):
        n = vrows * heads
        flat[which, pl.ds(0, n), :] = raw_v[which].astype(f32).reshape(n, hd)
        flat[which, pl.ds(n, arows * heads), :] = raw_a[which].astype(f32).reshape(arows * heads, hd)

    def head_of(which, h):
        top = flat[which, pl.ds(h, vrows, stride=heads), :]
        low = flat[which, pl.ds(vrows * heads + h, arows, stride=heads), :]
        return jnp.concatenate([top, low], axis=0)

    def rotated(x):
        other = jnp.dot(x.astype(bf16), swap[...], preferred_element_type=f32)
        return (x * cos + other * sin).astype(bf16)

    def z_copy(g, k):
        part = pl.ds(g * 2 * n_heads, 2 * n_heads)
        return pltpu.make_async_remote_copy(
            src_ref=kvs.at[k - 1, part], dst_ref=kv.at[own_slot, part],
            send_sem=zs.at[g, k], recv_sem=zr.at[g, k], device_id=at_z(k), device_id_type=MESH,
        )

    def q_copy(g, k):
        part = pl.ds(g * n_heads, n_heads)
        return pltpu.make_async_remote_copy(
            src_ref=qs.at[k - 1, part], dst_ref=q.at[a, part],
            send_sem=qss.at[g, k], recv_sem=qsr.at[g, k], device_id=at_z(k), device_id_type=MESH,
        )

    lines = {
        "x": (0, 0, None, 2), "y": (1, 0, None, 4), "c": (2, 0, None, 1),
        "d1": (3, 2, 0, 4), "cx": (4, 2, None, 1), "d2": (5, 4, 1, 2), "cy": (6, 4, None, 1),
        "cd1": (7, 6, 0, 1), "cd2": (8, 6, 1, 1),
    }

    def forward(name, g, k):
        line, m, half, target = lines[name]
        slot = jnp.bitwise_xor(v, m) * A + jnp.bitwise_xor(a, k)
        if half is None:
            part = pl.ds(g * 2 * n_heads, 2 * n_heads)
        else:
            part = pl.ds(g * 2 * n_heads + half * n_heads, n_heads)
        return pltpu.make_async_remote_copy(
            src_ref=kv.at[slot, part], dst_ref=kv.at[slot, part],
            send_sem=fs.at[line, g, k], recv_sem=fr.at[line, g, k],
            device_id=at_v(target), device_id_type=MESH,
        )

    order = [j ^ (j >> 1) for j in range(A)]
    for copy in small[1:6]:
        copy.wait()
    flatten(1)
    flatten(2)
    for g in range(G):
        for k in order[1:] + [0]:
            for i in range(n_heads):
                h = g * n_heads + i
                whole = jnp.bitwise_xor(a, k) * group + h
                key = rotated(head_of(1, whole))
                value = head_of(2, whole).astype(bf16)
                if k:
                    kvs[k - 1, 2 * h] = key
                    kvs[k - 1, 2 * h + 1] = value
                else:
                    kv[own_slot, 2 * h] = key
                    kv[own_slot, 2 * h + 1] = value
        if g == 0:
            pl.semaphore_wait(barrier, A + 2)
            small[6].wait()
            small[7].wait()
            flatten(0)
        for k in order[1:]:
            z_copy(g, k).start()
        if g == 0:
            for name in ("x", "y", "c"):
                forward(name, 0, 0).start()
        for k in order[1:] + [0]:
            for i in range(n_heads):
                h = g * n_heads + i
                query = rotated(head_of(0, jnp.bitwise_xor(a, k) * group + h))
                if k:
                    qs[k - 1, h] = query
                else:
                    q[a, h] = query
        for k in order[1:]:
            q_copy(g, k).start()

    def start_weights(c, carry):
        load(c, 0).start()
        load(c, 1).start()
        return carry

    lax.fori_loop(0, nC, start_weights, 0)

    scale = math.log2(math.e) / math.sqrt(hd)
    halves = 2
    planes = A // halves
    pieces = n_heads * halves

    def attend_piece(g, i):
        h = g * n_heads + i // halves
        r = i % halves
        query = q[pl.ds(r * planes, planes), h].reshape(planes * rows, hd)
        key = kv[:, 2 * h].reshape(V * A * rows, hd)
        value = kv[:, 2 * h + 1].reshape(V * A * rows, hd)
        s = lax.dot_general(query, key, (((1,), (1,)), ((), ())), preferred_element_type=f32)
        top = jnp.max(s, axis=1, keepdims=True)
        w = jnp.exp2((s - top) * scale)
        total = jnp.sum(w, axis=1, keepdims=True)
        o = jnp.dot(w.astype(bf16), value, preferred_element_type=f32) / total
        cols = pl.ds(pl.multiple_of(h * hd, hd), hd)
        va[pl.ds(pl.multiple_of(r * planes * vrows, 16), planes * vrows), cols] = jnp.concatenate(
            [o[p * rows : p * rows + vrows] for p in range(planes)], axis=0
        ).astype(bf16)
        aa[pl.ds(pl.multiple_of(r * planes * arows, 16), planes * arows), cols] = jnp.concatenate(
            [o[p * rows + vrows : (p + 1) * rows] for p in range(planes)], axis=0
        ).astype(bf16)

    S = G * A
    lag_xy, lag_d = 2, 4
    lag = A + lag_d + 1

    def group_and_step(s):
        g = s // A
        j = s % A
        return g, jnp.bitwise_xor(j, j // 2)

    def step(s, carry):
        @pl.when(s < S)
        def _():
            g, k = group_and_step(s)

            @pl.when(k > 0)
            def _():
                z_copy(g, k).wait_recv()

            @pl.when(s > 0)
            def _():
                for name in ("x", "y", "c"):
                    forward(name, g, k).start()

        @pl.when((s >= lag_xy) & (s < S + lag_xy))
        def _():
            g, k = group_and_step(s - lag_xy)
            forward("x", g, k).wait_recv()
            forward("d1", g, k).start()
            forward("cx", g, k).start()
            forward("y", g, k).wait_recv()
            forward("d2", g, k).start()
            forward("cy", g, k).start()

        @pl.when((s >= lag_d) & (s < S + lag_d))
        def _():
            g, k = group_and_step(s - lag_d)
            forward("d1", g, k).wait_recv()
            forward("cd1", g, k).start()
            forward("d2", g, k).wait_recv()
            forward("cd2", g, k).start()

        @pl.when(s >= lag)
        def _():
            g = (s - lag) // A
            i = (s - lag) % A

            @pl.when(i == 0)
            def _():
                for k in range(A):
                    for name in ("c", "cx", "cy", "cd1", "cd2"):
                        forward(name, g, k).wait_recv()
                    if k:
                        q_copy(g, k).wait_recv()

            @pl.when(i < pieces)
            def _():
                attend_piece(g, i)

        return carry

    lax.fori_loop(0, S + lag, step, 0)

    above = {"aseq": jnp.minimum(a + 1, A - 1)}
    below = {"aseq": jnp.maximum(a - 1, 0)}

    def up_copy(d, c):
        return pltpu.make_async_remote_copy(
            src_ref=up_out.at[d, c], dst_ref=up_in.at[d, c],
            send_sem=us.at[d, c], recv_sem=ur.at[d, c], device_id=above, device_id_type=MESH,
        )

    def dn_copy(d, c):
        return pltpu.make_async_remote_copy(
            src_ref=dn_out.at[d, c], dst_ref=dn_in.at[d, c],
            send_sem=ds_.at[d, c], recv_sem=dr.at[d, c], device_id=below, device_id_type=MESH,
        )

    def first_sends(i, c):
        @pl.when(a == 0)
        def _():
            up_out[A - 1 - i, c] = own[A - 1 - i, c].astype(bf16)
            up_copy(A - 1 - i, c).start()

        @pl.when(a == A - 1)
        def _():
            dn_out[i, c] = own[i, c].astype(bf16)
            dn_copy(i, c).start()

    def multiply(c, carry):
        load(c, 0).wait()
        load(c, 1).wait()
        pv = jnp.dot(va[...], wv[c], preferred_element_type=f32)
        pa = jnp.dot(aa[...], wa[c], preferred_element_type=f32)
        for d in range(A):
            own[d, c, pl.ds(0, vrows), :] = pv[d * vrows : (d + 1) * vrows]
            own[d, c, pl.ds(vrows, arows), :] = pa[d * arows : (d + 1) * arows]
        first_sends(0, c)
        return carry

    lax.fori_loop(0, nC, multiply, 0)

    def later_sends(c, carry):
        first_sends(1 + c // nC, c % nC)
        return carry

    lax.fori_loop(0, (A - 2) * nC, later_sends, 0)

    hop = 2

    def relay(t, carry):
        up = t - hop * jnp.maximum(a - 1, 0)
        dn = t - hop * jnp.maximum(A - 2 - a, 0)

        @pl.when((a > 0) & (up >= 0) & (up < (A - 1 - a) * nC))
        def _():
            d, c = A - 1 - up // nC, up % nC
            up_copy(d, c).wait_recv()
            up_out[d, c] = (own[d, c] + up_in[d, c].astype(f32)).astype(bf16)
            up_copy(d, c).start()

        @pl.when((a < A - 1) & (dn >= 0) & (dn < a * nC))
        def _():
            d, c = dn // nC, dn % nC
            dn_copy(d, c).wait_recv()
            dn_out[d, c] = (own[d, c] + dn_in[d, c].astype(f32)).astype(bf16)
            dn_copy(d, c).start()

        return carry

    for copy in small[8:]:
        copy.wait()
    level = (levels_ref[frame] + 1).astype(f32)
    frac = jnp.full((8, hd), level, f32) / LEVELS
    timestep = 1000.0 * flow_shift * frac / (1.0 + (flow_shift - 1.0) * frac)
    half_emb = gwv.shape[0] // 2
    turn = timestep * lane[pl.ds(5, 1), :]
    embedding = jnp.concatenate([jnp.cos(turn), jnp.sin(turn)], axis=1)
    high = embedding.astype(bf16).astype(f32)
    mid = (embedding - high).astype(bf16).astype(f32)
    low = embedding - high - mid
    erow = lax.broadcasted_iota(jnp.int32, embedding.shape, 0)
    split = jnp.where(erow == 0, high, jnp.where(erow == 1, mid, jnp.where(erow == 2, low, 0.0))).astype(bf16)
    for i, w_ref in enumerate((gwv, gwa)):
        parts = jnp.dot(split, w_ref[...], preferred_element_type=f32)
        gates[i] = jnp.broadcast_to(jnp.sum(parts, axis=0, keepdims=True), parts.shape)

    lax.fori_loop(0, (A - 2) * (nC + hop), relay, 0)

    def finish(c, carry):
        @pl.when(a > 0)
        def _():
            up_copy(a, c).wait_recv()
            own[a, c] = own[a, c] + up_in[a, c].astype(f32)

        @pl.when(a < A - 1)
        def _():
            dn_copy(a, c).wait_recv()
            own[a, c] = own[a, c] + dn_in[a, c].astype(f32)

        cols = pl.ds(pl.multiple_of(c * cw, 128), cw)
        vo_ref[:, cols] = (
            xv[:, cols].astype(f32) + gates[0, pl.ds(0, 1), cols] * own[a, c, pl.ds(0, vrows), :]
        ).astype(vo_ref.dtype)
        ao_ref[:, cols] = (
            xa[:, cols].astype(f32) + gates[1, pl.ds(0, 1), cols] * own[a, c, pl.ds(vrows, arows), :]
        ).astype(ao_ref.dtype)
        return carry

    lax.fori_loop(0, nC, finish, 0)

    def drain(s, carry):
        g, k = group_and_step(s)
        for name in lines:
            forward(name, g, k).wait_send()

        @pl.when(k > 0)
        def _():
            z_copy(g, k).wait_send()
            q_copy(g, k).wait_send()

        return carry

    lax.fori_loop(0, S, drain, 0)

    def drain_sums(c, carry):
        for d in range(A):
            @pl.when(a < d)
            def _():
                up_copy(d, c).wait_send()

            @pl.when(a > d)
            def _():
                dn_copy(d, c).wait_send()

        return carry

    lax.fori_loop(0, nC, drain_sums, 0)


def lane_table(hd, half_emb):
    one_sixth = hd // 6
    first = hd - 4 * one_sixth
    table = np.zeros((8, hd), np.float64)
    start = 0
    for i, width in enumerate((first, 2 * one_sixth, 2 * one_sixth)):
        half = width // 2
        frequency = 10000.0 ** (-(np.arange(half) * 2.0) / width)
        table[0, start : start + width] = np.concatenate([frequency, frequency])
        table[1, start : start + width] = np.repeat([-1.0, 1.0], half)
        table[2 + i, start : start + width] = 1.0
        start += width
    table[5, :half_emb] = np.exp(-math.log(10000.0) * np.arange(half_emb) / half_emb)
    return jnp.asarray(table, jnp.float32)


def store_kernel(v_ref, a_ref, vo_ref, ao_ref, sem):
    one = pltpu.make_async_copy(v_ref, vo_ref, sem.at[0])
    two = pltpu.make_async_copy(a_ref, ao_ref, sem.at[1])
    one.start()
    two.start()
    one.wait()
    two.wait()


def fused(
    video_q, video_k, video_v, audio_q, audio_k, audio_v, video_x, audio_x,
    video_out_w, audio_out_w, video_gate_w, audio_gate_w, levels, video_pos, audio_pos, A, V,
):
    vrows, heads, hd = video_q.shape
    arows = audio_q.shape[0]
    rows = vrows + arows
    group = heads // A
    inner, width = video_out_w.shape
    n_heads = 2
    G = group // n_heads
    nC = 6
    cw = width // nC
    bf16, f32 = jnp.bfloat16, jnp.float32
    anywhere = pl.BlockSpec(memory_space=pl.ANY)
    vmem = pl.BlockSpec(memory_space=pltpu.VMEM)
    smem = pl.BlockSpec(memory_space=pltpu.SMEM)
    wire = pltpu.VMEM((A, nC, rows, cw), bf16)
    dma = pltpu.SemaphoreType.DMA
    temb = video_gate_w.shape[0]
    vo, ao = pl.pallas_call(
        functools.partial(fused_kernel, A, V, n_heads, nC, vrows, arows),
        out_shape=(pltpu.VMEM(video_x.shape, video_x.dtype), pltpu.VMEM(audio_x.shape, audio_x.dtype)),
        in_specs=[anywhere] * 14 + [smem] * 3,
        out_specs=(vmem, vmem),
        scratch_shapes=[
            pltpu.VMEM((3, vrows, heads, hd), bf16),
            pltpu.VMEM((3, arows, heads, hd), bf16),
            pltpu.VMEM((3, rows * heads, hd), f32),
            pltpu.VMEM(video_x.shape, bf16),
            pltpu.VMEM(audio_x.shape, bf16),
            pltpu.VMEM((nC, inner, cw), bf16),
            pltpu.VMEM((nC, inner, cw), bf16),
            pltpu.VMEM((temb, width), bf16),
            pltpu.VMEM((temb, width), bf16),
            pltpu.VMEM((8, hd), f32),
            pltpu.VMEM((hd, hd), bf16),
            pltpu.VMEM((A - 1, 2 * group, rows, hd), bf16),
            pltpu.VMEM((A - 1, group, rows, hd), bf16),
            pltpu.VMEM((V * A, 2 * group, rows, hd), bf16),
            pltpu.VMEM((A, group, rows, hd), bf16),
            pltpu.VMEM((A * vrows, group * hd), bf16),
            pltpu.VMEM((A * arows, group * hd), bf16),
            pltpu.VMEM((A, nC, rows, cw), f32),
            wire, wire, wire, wire,
            pltpu.VMEM((2, 8, width), f32),
            dma((12,)),
            dma((2, nC)),
            dma((G, A)), dma((G, A)), dma((G, A)), dma((G, A)),
            dma((9, G, A)), dma((9, G, A)),
            dma((A, nC)), dma((A, nC)), dma((A, nC)), dma((A, nC)),
        ],
        compiler_params=pltpu.CompilerParams(
            collective_id=2, has_side_effects=True, vmem_limit_bytes=60 * 1024 * 1024
        ),
        name="fused_attention",
    )(
        video_q, video_k, video_v, audio_q, audio_k, audio_v, video_x, audio_x,
        video_out_w, audio_out_w, video_gate_w, audio_gate_w,
        lane_table(hd, temb // 2), swap_matrix(hd), levels, video_pos, audio_pos,
    )
    return pl.pallas_call(
        store_kernel,
        out_shape=(
            jax.ShapeDtypeStruct(video_x.shape, video_x.dtype),
            jax.ShapeDtypeStruct(audio_x.shape, audio_x.dtype),
        ),
        in_specs=[vmem, vmem],
        out_specs=(anywhere, anywhere),
        scratch_shapes=[dma((2,))],
        name="store_result",
    )(vo, ao)


def local(
    video_q, video_k, video_v, audio_q, audio_k, audio_v, video_x, audio_x,
    video_out_w, audio_out_w, video_gate_w, audio_gate_w, levels, video_pos, audio_pos,
):
    A, V = lax.axis_size("aseq"), lax.axis_size("vseq")
    vrows, heads, hd = video_q.shape
    arows = audio_q.shape[0]
    rows = vrows + arows
    frames = video_pos.shape[0]
    if V == 8 and V == frames and A == 4 and heads % (2 * A) == 0 and hd == video_gate_w.shape[0] // 2:
        return fused(
            video_q, video_k, video_v, audio_q, audio_k, audio_v, video_x, audio_x,
            video_out_w, audio_out_w, video_gate_w, audio_gate_w, levels, video_pos, audio_pos, A, V,
        )
    rank = lax.axis_index(("vseq", "aseq"))
    frame_tokens = vrows * A * V // frames
    token = rank * vrows + jnp.arange(vrows, dtype=jnp.int32)
    frame_of = token // frame_tokens
    within = token % frame_tokens
    frame_ids = jnp.arange(frames, dtype=jnp.int32)
    video_hot = frame_of[:, None] == frame_ids[None, :]
    place_t = jnp.sum(jnp.where(video_hot, video_pos[None, :], 0), axis=1)
    zero = jnp.zeros_like(audio_pos)
    cos, sin = rope_tables(
        hd,
        jnp.concatenate([place_t, audio_pos]),
        jnp.concatenate([within // GRID_W, zero]),
        jnp.concatenate([within % GRID_W, zero]),
    )
    swap = swap_matrix(hd)

    def heads_first(video, audio):
        return jnp.swapaxes(jnp.concatenate([video, audio], axis=0), 0, 1)

    def rotate(x):
        other = jnp.dot(x, swap, preferred_element_type=jnp.float32)
        return (x.astype(jnp.float32) * cos[None] + other * sin[None]).astype(jnp.bfloat16)

    group = heads // A
    qkv = jnp.stack(
        [
            rotate(heads_first(video_q, audio_q)).reshape(A, group, rows, hd),
            rotate(heads_first(video_k, audio_k)).reshape(A, group, rows, hd),
            heads_first(video_v, audio_v).reshape(A, group, rows, hd),
        ],
        axis=1,
    )
    audio_frame = jnp.sum((video_pos[None, :] <= audio_pos[:, None]).astype(jnp.int32), axis=1) - 1
    audio_hot = audio_frame[:, None] == frame_ids[None, :]
    embedding = embedding_of(levels, video_gate_w.shape[0] // 2)

    def split_rows(hot):
        mine = jnp.sum(jnp.where(hot[:, :, None], embedding[None], 0.0), axis=1)
        high = mine.astype(jnp.bfloat16)
        rest = mine - high.astype(jnp.float32)
        mid = rest.astype(jnp.bfloat16)
        low = (rest - mid.astype(jnp.float32)).astype(jnp.bfloat16)
        return jnp.concatenate([high, mid, low], axis=0)

    one_frame = frame_tokens % vrows == 0
    ev = split_rows(video_hot[:8] if one_frame else video_hot)
    ea = split_rows(audio_hot)
    q, kv, gv, ga = gather(qkv, ev, ea, video_gate_w, audio_gate_w, A, V)
    va, aa = attend(q, kv, A, vrows, arows)
    return project(va, aa, video_out_w, audio_out_w, video_x, audio_x, gv, ga, A)


def solution(mesh):
    tokens = P(("vseq", "aseq"), None, None)
    wide = P(("vseq", "aseq"), None)
    return jax.shard_map(
        local,
        mesh=mesh,
        in_specs=(
            tokens, tokens, tokens, tokens, tokens, tokens, wide, wide,
            P("aseq", None), P("aseq", None), P(), P(), P(), P(), P(("vseq", "aseq")),
        ),
        out_specs=(wide, wide),
        check_vma=False,
    )
```

```python
import functools
import math

import jax
import jax.numpy as jnp
import numpy as np
from jax import lax
from jax.experimental import pallas as pl
from jax.experimental.pallas import tpu as pltpu
from jax.sharding import PartitionSpec as P

GRID_W = 32
LEVELS = 1000
flow_shift = 5.0


def rope_tables(head_dim, place_t, place_h, place_w):
    one_sixth = head_dim // 6
    first = head_dim - 4 * one_sixth
    cos_cols, sin_cols = [], []
    for width, places in ((first, place_t), (2 * one_sixth, place_h), (2 * one_sixth, place_w)):
        half = width // 2
        frequency = 10000.0 ** (-(jnp.arange(half, dtype=jnp.float32) * 2.0) / width)
        angles = places.astype(jnp.float32)[:, None] * frequency[None, :]
        cos_part, sin_part = jnp.cos(angles), jnp.sin(angles)
        cos_cols += [cos_part, cos_part]
        sin_cols += [-sin_part, sin_part]
    return jnp.concatenate(cos_cols, axis=1), jnp.concatenate(sin_cols, axis=1)


def swap_matrix(head_dim):
    one_sixth = head_dim // 6
    first = head_dim - 4 * one_sixth
    source = []
    start = 0
    for width in (first, 2 * one_sixth, 2 * one_sixth):
        half = width // 2
        source += list(range(start + half, start + width)) + list(range(start, start + half))
        start += width
    return jnp.asarray(np.arange(head_dim)[:, None] == np.array(source)[None, :], jnp.bfloat16)


def embedding_of(levels, half_emb):
    level_frac = (levels.astype(jnp.float32) + 1.0) / LEVELS
    timestep = 1000.0 * flow_shift * level_frac / (1.0 + (flow_shift - 1.0) * level_frac)
    frequency = jnp.exp(-math.log(10000.0) * jnp.arange(half_emb, dtype=jnp.float32) / half_emb)
    angles = timestep[:, None] * frequency[None, :]
    return jnp.concatenate([jnp.cos(angles), jnp.sin(angles)], axis=1)


def gather_kernel(
    A, V, rows, qkv_ref, ev_ref, ea_ref, gwv_ref, gwa_ref, q_out, kv_out, gv_ref, ga_ref, loc_sem, zs, zr, qs, qr, fs, fr
):
    a = lax.axis_index("aseq")
    v = lax.axis_index("vseq")

    def at_z(k):
        return {"aseq": jnp.bitwise_xor(a, k)}

    def at_v(m):
        return {"vseq": jnp.bitwise_xor(v, m)}

    ring = V == 8
    v_peers = (1, 2, 4) if ring else tuple(range(1, V))
    barrier = pltpu.get_barrier_semaphore()
    for k in range(1, A):
        pl.semaphore_signal(barrier, 1, device_id=at_z(k), device_id_type=pl.DeviceIdType.MESH)
    for m in v_peers:
        pl.semaphore_signal(barrier, 1, device_id=at_v(m), device_id_type=pl.DeviceIdType.MESH)
    pl.semaphore_wait(barrier, A - 1 + len(v_peers))

    def spot(m, k, which=None):
        at = (jnp.bitwise_xor(v, m) * A + jnp.bitwise_xor(a, k)) * rows
        at = pl.ds(pl.multiple_of(at, 8), rows)
        if which is None:
            return kv_out.at[:, :, at, :]
        return kv_out.at[pl.ds(which, 1), :, at, :]

    def q_spot():
        return q_out.at[:, pl.ds(pl.multiple_of(a * rows, 8), rows), :]

    def send(src, dst, ssem, rsem, device):
        copy = pltpu.make_async_remote_copy(
            src_ref=src, dst_ref=dst, send_sem=ssem, recv_sem=rsem,
            device_id=device, device_id_type=pl.DeviceIdType.MESH,
        )
        copy.start()
        return copy

    own_kv = pltpu.make_async_copy(qkv_ref.at[a, pl.ds(1, 2)], spot(0, 0), loc_sem.at[0])
    own_kv.start()
    own_q = pltpu.make_async_copy(qkv_ref.at[a, 0], q_spot(), loc_sem.at[1])
    own_q.start()
    order = [1] + list(range(A - 1, 1, -1))
    z_copies, q_copies = {}, {}
    for k in order:
        z_copies[k] = send(
            qkv_ref.at[jnp.bitwise_xor(a, k), pl.ds(1, 2)], spot(0, 0), zs.at[k], zr.at[k], at_z(k)
        )
    sent = []

    def forward(m, k, which, slot, target):
        copy = send(spot(m, k, which), spot(m, k, which), fs.at[slot, k], fr.at[slot, k], at_v(target))
        sent.append(copy)
        return copy

    got = {}

    def stage_z(k):
        if k == 0:
            own_kv.wait()
        else:
            z_copies[k].wait_recv()
        if ring:
            got["x", k] = forward(0, k, None, 0, 2)
            got["y", k] = forward(0, k, None, 1, 4)
            got["c", k] = forward(0, k, None, 2, 1)
        else:
            for m in v_peers:
                got[m, k] = forward(0, k, None, m, m)

    def stage_xy(k):
        got["x", k].wait_recv()
        got["dk", k] = forward(2, k, 0, 3, 4)
        got["cx", k] = forward(2, k, None, 4, 1)
        got["y", k].wait_recv()
        got["dv", k] = forward(4, k, 1, 5, 2)
        got["cy", k] = forward(4, k, None, 6, 1)

    def stage_d(k):
        got["dk", k].wait_recv()
        got["cdk", k] = forward(6, k, 0, 7, 1)
        got["dv", k].wait_recv()
        got["cdv", k] = forward(6, k, 1, 8, 1)

    stages = [0] + order
    for step in range(A + 2):
        if step < A:
            stage_z(stages[step])
        if step == 0:
            for k in order:
                q_copies[k] = send(
                    qkv_ref.at[jnp.bitwise_xor(a, k), 0], q_spot(), qs.at[k], qr.at[k], at_z(k)
                )
            for e_ref, w_ref, g_ref in ((ev_ref, gwv_ref, gv_ref), (ea_ref, gwa_ref, ga_ref)):
                parts = jnp.dot(e_ref[...], w_ref[...], preferred_element_type=jnp.float32)
                n = g_ref.shape[0]
                g_ref[...] = parts[:n] + parts[n : 2 * n] + parts[2 * n :]
        if ring:
            if 1 <= step < A + 1:
                stage_xy(stages[step - 1])
            if 2 <= step:
                stage_d(stages[step - 2])
    for k in range(A):
        if ring:
            for name in ("c", "cx", "cy", "cdk", "cdv"):
                got[name, k].wait_recv()
        else:
            for m in v_peers:
                got[m, k].wait_recv()
    own_q.wait()
    for k in order:
        q_copies[k].wait()
        z_copies[k].wait_send()
    for copy in sent:
        copy.wait_send()


def gather(qkv, ev, ea, gwv, gwa, A, V):
    _, _, heads, rows, hd = qkv.shape
    slots = 9 if V == 8 else V
    return pl.pallas_call(
        functools.partial(gather_kernel, A, V, rows),
        out_shape=(
            jax.ShapeDtypeStruct((heads, A * rows, hd), qkv.dtype),
            jax.ShapeDtypeStruct((2, heads, V * A * rows, hd), qkv.dtype),
            jax.ShapeDtypeStruct((ev.shape[0] // 3, gwv.shape[1]), jnp.float32),
            jax.ShapeDtypeStruct((ea.shape[0] // 3, gwa.shape[1]), jnp.float32),
        ),
        in_specs=[pl.BlockSpec(memory_space=pl.ANY)] + [pl.BlockSpec(memory_space=pltpu.VMEM)] * 4,
        out_specs=(pl.BlockSpec(memory_space=pl.ANY),) * 2
        + (pl.BlockSpec(memory_space=pltpu.VMEM),) * 2,
        scratch_shapes=[
            pltpu.SemaphoreType.DMA((2,)),
            pltpu.SemaphoreType.DMA((A,)),
            pltpu.SemaphoreType.DMA((A,)),
            pltpu.SemaphoreType.DMA((A,)),
            pltpu.SemaphoreType.DMA((A,)),
            pltpu.SemaphoreType.DMA((slots, A)),
            pltpu.SemaphoreType.DMA((slots, A)),
        ],
        compiler_params=pltpu.CompilerParams(collective_id=0, has_side_effects=True),
        name="gather_heads",
    )(qkv, ev, ea, gwv, gwa)


def attend_kernel(A, vrows, arows, step_keys, q_ref, kv_ref, v_ref, vo_ref, ao_ref):
    q = q_ref[0]
    keys = kv_ref.shape[2]
    scale = math.log2(math.e) / math.sqrt(q.shape[1])
    top, total, acc = None, None, None
    for start in range(0, keys, step_keys):
        k = kv_ref[0, 0, pl.ds(start, step_keys), :]
        vv = v_ref[0, 0, pl.ds(start, step_keys), :]
        s = lax.dot_general(q, k, (((1,), (1,)), ((), ())), preferred_element_type=jnp.float32)
        new_top = jnp.max(s, axis=1, keepdims=True)
        if top is not None:
            new_top = jnp.maximum(new_top, top)
        w = jnp.exp2((s - new_top) * scale)
        part = jnp.sum(w, axis=1, keepdims=True)
        mixed = jnp.dot(w.astype(jnp.bfloat16), vv, preferred_element_type=jnp.float32)
        if top is None:
            total, acc = part, mixed
        else:
            f = jnp.exp2((top - new_top) * scale)
            total, acc = total * f + part, acc * f + mixed
        top = new_top
    o = acc / total
    rows = vrows + arows
    for i in range(A):
        vo_ref[pl.ds(i * vrows, vrows), :] = o[i * rows : i * rows + vrows].astype(vo_ref.dtype)
    ao_ref[...] = jnp.concatenate(
        [o[i * rows + vrows : (i + 1) * rows] for i in range(A)], axis=0
    ).astype(ao_ref.dtype)


def attend(q, kv, A, vrows, arows):
    heads, qrows, hd = q.shape
    keys = kv.shape[2]
    step_keys = keys if keys <= 2048 else 1792
    while keys % step_keys:
        step_keys -= 128
    return pl.pallas_call(
        functools.partial(attend_kernel, A, vrows, arows, step_keys),
        grid=(heads,),
        out_shape=(
            jax.ShapeDtypeStruct((A * vrows, heads * hd), q.dtype),
            jax.ShapeDtypeStruct((A * arows, heads * hd), q.dtype),
        ),
        in_specs=[
            pl.BlockSpec((1, qrows, hd), lambda h: (h, 0, 0)),
            pl.BlockSpec((1, 1, keys, hd), lambda h: (0, h, 0, 0)),
            pl.BlockSpec((1, 1, keys, hd), lambda h: (1, h, 0, 0)),
        ],
        out_specs=(
            pl.BlockSpec((A * vrows, hd), lambda h: (0, h)),
            pl.BlockSpec((A * arows, hd), lambda h: (0, h)),
        ),
        compiler_params=pltpu.CompilerParams(dimension_semantics=("arbitrary",)),
        name="attend_heads",
    )(q, kv, kv)


def project_kernel(
    A, nC, cw, vrows, arows,
    va_ref, aa_ref, wv_hbm, wa_hbm, xv_ref, xa_ref, gv_ref, ga_ref,
    vo_ref, ao_ref,
    wv, wa, own, up_in, dn_in, up_out, dn_out, w_sem, us, ur, ds_, dr,
):
    p = lax.axis_index("aseq")
    loads = []
    for c in range(nC):
        cols = pl.ds(c * cw, cw)
        one = pltpu.make_async_copy(wv_hbm.at[:, cols], wv.at[c], w_sem.at[0, c])
        two = pltpu.make_async_copy(wa_hbm.at[:, cols], wa.at[c], w_sem.at[1, c])
        one.start()
        two.start()
        loads.append((one, two))
    above = {"aseq": jnp.minimum(p + 1, A - 1)}
    below = {"aseq": jnp.maximum(p - 1, 0)}
    MESH = pl.DeviceIdType.MESH
    barrier = pltpu.get_barrier_semaphore()

    for k in range(1, A):
        peer = {"aseq": jnp.bitwise_xor(p, k)}
        pl.semaphore_signal(barrier, 1, device_id=peer, device_id_type=MESH)
    pl.semaphore_wait(barrier, A - 1)

    def up_copy(d, c):
        return pltpu.make_async_remote_copy(
            src_ref=up_out.at[d, c], dst_ref=up_in.at[d, c],
            send_sem=us.at[d, c], recv_sem=ur.at[d, c], device_id=above, device_id_type=MESH,
        )

    def dn_copy(d, c):
        return pltpu.make_async_remote_copy(
            src_ref=dn_out.at[d, c], dst_ref=dn_in.at[d, c],
            send_sem=ds_.at[d, c], recv_sem=dr.at[d, c], device_id=below, device_id_type=MESH,
        )

    def multiply(c):
        one, two = loads[c]
        one.wait()
        pv = jnp.dot(va_ref[...], wv[c], preferred_element_type=jnp.float32)
        two.wait()
        pa = jnp.dot(aa_ref[...], wa[c], preferred_element_type=jnp.float32)
        for d in range(A):
            own[d, c, pl.ds(0, vrows), :] = pv[d * vrows : (d + 1) * vrows]
            own[d, c, pl.ds(vrows, arows), :] = pa[d * arows : (d + 1) * arows]

        first_sends(0, c)

    def first_sends(i, c):
        @pl.when(p == 0)
        def _():
            up_out[A - 1 - i, c] = own[A - 1 - i, c].astype(up_out.dtype)
            up_copy(A - 1 - i, c).start()

        @pl.when(p == A - 1)
        def _():
            dn_out[i, c] = own[i, c].astype(dn_out.dtype)
            dn_copy(i, c).start()

    def relay(i, c):
        d = A - 1 - i

        @pl.when((p > 0) & (p < d))
        def _():
            up_copy(d, c).wait_recv()
            up_out[d, c] = (own[d, c] + up_in[d, c].astype(jnp.float32)).astype(up_out.dtype)
            up_copy(d, c).start()

        @pl.when((p < A - 1) & (p > i))
        def _():
            dn_copy(i, c).wait_recv()
            dn_out[i, c] = (own[i, c] + dn_in[i, c].astype(jnp.float32)).astype(dn_out.dtype)
            dn_copy(i, c).start()

    for c in range(nC):
        multiply(c)
    for i in range(1, A - 1):
        for c in range(nC):
            first_sends(i, c)
    for i in range(A - 1):
        for c in range(nC):
            relay(i, c)

    for c in range(nC):
        @pl.when(p > 0)
        def _():
            up_copy(p, c).wait_recv()
            own[p, c] = own[p, c] + up_in[p, c].astype(jnp.float32)

        @pl.when(p < A - 1)
        def _():
            dn_copy(p, c).wait_recv()
            own[p, c] = own[p, c] + dn_in[p, c].astype(jnp.float32)

        cols = pl.ds(c * cw, cw)
        gate = gv_ref[:, cols] if gv_ref.shape[0] == vrows else gv_ref[pl.ds(0, 1), cols]
        vo_ref[:, cols] = (
            xv_ref[:, cols].astype(jnp.float32) + gate * own[p, c, pl.ds(0, vrows), :]
        ).astype(vo_ref.dtype)
        ao_ref[:, cols] = (
            xa_ref[:, cols].astype(jnp.float32) + ga_ref[:, cols] * own[p, c, pl.ds(vrows, arows), :]
        ).astype(ao_ref.dtype)

    for c in range(nC):
        for d in range(A):
            @pl.when(p < d)
            def _():
                up_copy(d, c).wait_send()

            @pl.when(p > d)
            def _():
                dn_copy(d, c).wait_send()


def project(va, aa, wv, wa, xv, xa, gv, ga, A):
    vrows, width = xv.shape
    arows = xa.shape[0]
    inner = wv.shape[0]
    nC = 2
    cw = width // nC
    rows = vrows + arows
    vmem = pl.BlockSpec(memory_space=pltpu.VMEM)
    hbm = pl.BlockSpec(memory_space=pl.ANY)
    wire = pltpu.VMEM((A, nC, rows, cw), jnp.bfloat16)
    return pl.pallas_call(
        functools.partial(project_kernel, A, nC, cw, vrows, arows),
        out_shape=(
            jax.ShapeDtypeStruct(xv.shape, xv.dtype),
            jax.ShapeDtypeStruct(xa.shape, xa.dtype),
        ),
        in_specs=[vmem, vmem, hbm, hbm, vmem, vmem, vmem, vmem],
        out_specs=(vmem, vmem),
        scratch_shapes=[
            pltpu.VMEM((nC, inner, cw), wv.dtype),
            pltpu.VMEM((nC, inner, cw), wa.dtype),
            pltpu.VMEM((A, nC, rows, cw), jnp.float32),
            wire, wire, wire, wire,
            pltpu.SemaphoreType.DMA((2, nC)),
            pltpu.SemaphoreType.DMA((A, nC)),
            pltpu.SemaphoreType.DMA((A, nC)),
            pltpu.SemaphoreType.DMA((A, nC)),
            pltpu.SemaphoreType.DMA((A, nC)),
        ],
        compiler_params=pltpu.CompilerParams(
            collective_id=1, has_side_effects=True, vmem_limit_bytes=60 * 1024 * 1024
        ),
        name="project_sum",
    )(va, aa, wv, wa, xv, xa, gv, ga)


def fused_kernel(
    A, V, n_heads, nC, vrows, arows,
    vq_h, vk_h, vv_h, aq_h, ak_h, av_h, xv_h, xa_h, wv_h, wa_h, gwv_h, gwa_h, lane_h, swap_h,
    levels_h, video_pos_h, audio_pos_h,
    vo_ref, ao_ref,
    levels_ref, video_pos_ref, audio_pos_ref, raw_v, raw_a, flat, xv, xa, wv, wa, gwv, gwa, lane, swap,
    kvs, qs, kv, q, va, aa, own, up_in, dn_in, up_out, dn_out, gates,
    best, total, mixed,
    in_sem, sent, z_got, q_got, xy_got, d_got, core_got, sum_got,
):
    a = lax.axis_index("aseq")
    v = lax.axis_index("vseq")
    MESH = pl.DeviceIdType.MESH
    rows = vrows + arows
    heads, hd = raw_v.shape[2], raw_v.shape[3]
    group = heads // A
    G = group // n_heads
    cw = own.shape[3]
    f32, bf16 = jnp.float32, jnp.bfloat16

    def at_z(k):
        return {"aseq": jnp.bitwise_xor(a, k)}

    def at_v(m):
        return {"vseq": jnp.bitwise_xor(v, m)}

    barrier = pltpu.get_barrier_semaphore()
    for k in range(1, A):
        pl.semaphore_signal(barrier, 1, device_id=at_z(k), device_id_type=MESH)
    for m in (1, 2, 4):
        pl.semaphore_signal(barrier, 1, device_id=at_v(m), device_id_type=MESH)

    small = []
    for i, (src, dst) in enumerate(
        (
            (lane_h, lane), (swap_h, swap),
            (video_pos_h, video_pos_ref), (audio_pos_h, audio_pos_ref),
            (vk_h, raw_v.at[1]), (ak_h, raw_a.at[1]),
            (vv_h, raw_v.at[2]), (av_h, raw_a.at[2]),
            (vq_h, raw_v.at[0]), (aq_h, raw_a.at[0]),
            (xv_h, xv), (xa_h, xa), (gwv_h, gwv), (gwa_h, gwa), (levels_h, levels_ref),
            (wv_h, wv), (wa_h, wa),
        )
    ):
        small.append(pltpu.make_async_copy(src, dst, in_sem.at[i]))
    early = 10
    for copy in small[:early]:
        copy.start()

    for i in (0, 2, 3):
        small[i].wait()
    frame = v
    row = lax.broadcasted_iota(jnp.int32, (vrows, hd), 0)
    within = a * vrows + row
    at_h = lax.div(within, GRID_W)
    at_w = within - at_h * GRID_W
    place_t = video_pos_ref[frame].astype(f32)
    freq = lane[pl.ds(0, 1), :]
    sign = lane[pl.ds(1, 1), :]
    is_t, is_h, is_w = (lane[pl.ds(i, 1), :] for i in (2, 3, 4))
    video_place = place_t * is_t + at_h.astype(f32) * is_h + at_w.astype(f32) * is_w
    audio_row = lax.broadcasted_iota(jnp.int32, (arows, hd), 0)
    audio_at = jnp.zeros((arows, hd), f32)
    for i in range(arows):
        audio_at = jnp.where(audio_row == i, audio_pos_ref[i].astype(f32), audio_at)
    angle = jnp.concatenate([video_place, audio_at * is_t], axis=0) * freq
    cos, sin = jnp.cos(angle), jnp.sin(angle) * sign

    def flatten(which):
        n = vrows * heads
        flat[which, pl.ds(0, n), :] = raw_v[which].astype(f32).reshape(n, hd)
        flat[which, pl.ds(n, arows * heads), :] = raw_a[which].astype(f32).reshape(arows * heads, hd)

    def head_of(which, h):
        top = flat[which, pl.ds(h, vrows, stride=heads), :]
        low = flat[which, pl.ds(vrows * heads + h, arows, stride=heads), :]
        return jnp.concatenate([top, low], axis=0)

    def rotated(x):
        other = jnp.dot(x.astype(bf16), swap[...], preferred_element_type=f32)
        return (x * cos + other * sin).astype(bf16)

    def z_copy(g, k):
        part = pl.ds(g * 2 * n_heads, 2 * n_heads)
        return pltpu.make_async_remote_copy(
            src_ref=kvs.at[k - 1, part], dst_ref=kv.at[v, a, part],
            send_sem=sent.at[0], recv_sem=z_got.at[g, k], device_id=at_z(k), device_id_type=MESH,
        )

    def q_copy(g, k):
        part = pl.ds(g * n_heads, n_heads)
        return pltpu.make_async_remote_copy(
            src_ref=qs.at[k - 1, part], dst_ref=q.at[a, part],
            send_sem=sent.at[1], recv_sem=q_got.at[g], device_id=at_z(k), device_id_type=MESH,
        )

    lines = {
        "x": (xy_got, 0, None, 2), "y": (xy_got, 0, None, 4), "c": (core_got, 0, None, 1),
        "d1": (d_got, 2, 0, 4), "cx": (core_got, 2, None, 1),
        "d2": (d_got, 4, 1, 2), "cy": (core_got, 4, None, 1),
        "cd1": (core_got, 6, 0, 1), "cd2": (core_got, 6, 1, 1),
    }

    def forward(name, g, k):
        got, m, half, target = lines[name]
        if half is None:
            part = pl.ds(g * 2 * n_heads, 2 * n_heads)
        else:
            part = pl.ds(g * 2 * n_heads + half * n_heads, n_heads)
        slot = kv.at[jnp.bitwise_xor(v, m), jnp.bitwise_xor(a, k), part]
        pltpu.make_async_remote_copy(
            src_ref=slot, dst_ref=slot, send_sem=sent.at[2], recv_sem=got.at[g, k],
            device_id=at_v(target), device_id_type=MESH,
        ).start()

    def wait_for(ref, sem):
        pltpu.make_async_copy(ref, ref, sem).wait()

    def wait_blocks(n, sem):
        wait_for(kv.at[pl.ds(0, n), 0, pl.ds(0, 2 * n_heads)], sem)

    order = [j ^ (j >> 1) for j in range(A)]
    for i in (1, 4, 5, 6, 7):
        small[i].wait()
    flatten(1)
    flatten(2)
    def send_keys(g):
        for k in order[1:] + [0]:
            for i in range(n_heads):
                h = g * n_heads + i
                whole = jnp.bitwise_xor(a, k) * group + h
                key = rotated(head_of(1, whole))
                value = head_of(2, whole).astype(bf16)
                if k:
                    kvs[k - 1, 2 * h] = key
                    kvs[k - 1, 2 * h + 1] = value
                else:
                    kv[v, a, 2 * h] = key
                    kv[v, a, 2 * h + 1] = value
        if g == 0:
            pl.semaphore_wait(barrier, A + 2)
        for k in order[1:]:
            z_copy(g, k).start()
        if g == 0:
            for name in ("x", "y", "c"):
                forward(name, 0, 0)

    def send_queries(g):
        if g == 0:
            small[8].wait()
            small[9].wait()
            flatten(0)
        for k in order[1:] + [0]:
            for i in range(n_heads):
                h = g * n_heads + i
                query = rotated(head_of(0, jnp.bitwise_xor(a, k) * group + h))
                if k:
                    qs[k - 1, h] = query
                else:
                    q[a, h] = query
        for k in order[1:]:
            q_copy(g, k).start()

    send_keys(0)
    send_queries(0)
    for g in range(1, G):
        send_keys(g)
        if g > 1:
            send_queries(g - 1)
    send_queries(G - 1)

    for copy in small[early:]:
        copy.start()

    scale = math.log2(math.e) / math.sqrt(hd)

    def attend(g, k, first, last):
        plane = jnp.bitwise_xor(a, k)

        @pl.when(first)
        def _():
            wait_for(q.at[pl.ds(0, A - 1), pl.ds(0, n_heads)], q_got.at[g])
            best[...] = jnp.full_like(best, -jnp.inf)
            total[...] = jnp.zeros_like(total)
            mixed[...] = jnp.zeros_like(mixed)

        for i in range(n_heads):
            h = g * n_heads + i
            query = q[:, h].reshape(A * rows, hd)
            key = kv[:, plane, 2 * h].reshape(V * rows, hd)
            value = kv[:, plane, 2 * h + 1].reshape(V * rows, hd)
            s = lax.dot_general(query, key, (((1,), (1,)), ((), ())), preferred_element_type=f32)
            before = best[i]
            top = jnp.maximum(before, jnp.max(s, axis=1, keepdims=True))
            w = jnp.exp2((s - top) * scale)
            fade = jnp.exp2((before - top) * scale)
            best[i] = top
            total[i] = total[i] * fade + jnp.sum(w, axis=1, keepdims=True)
            mixed[i] = mixed[i] * fade + jnp.dot(w.astype(bf16), value, preferred_element_type=f32)

        @pl.when(last)
        def _():
            for i in range(n_heads):
                o = mixed[i] / total[i]
                cols = pl.ds(pl.multiple_of((g * n_heads + i) * hd, hd), hd)
                va[:, cols] = jnp.concatenate(
                    [o[p * rows : p * rows + vrows] for p in range(A)], axis=0
                ).astype(bf16)
                aa[:, cols] = jnp.concatenate(
                    [o[p * rows + vrows : (p + 1) * rows] for p in range(A)], axis=0
                ).astype(bf16)

    S = G * A
    lag_xy, lag_d, lag_att = 2, 4, 5

    def group_and_step(s):
        g = s // A
        j = s % A
        return g, jnp.bitwise_xor(j, j // 2)

    def step(s, carry):
        @pl.when(s < S)
        def _():
            g, k = group_and_step(s)

            @pl.when(k > 0)
            def _():
                z_copy(g, k).wait_recv()

            @pl.when(s > 0)
            def _():
                for name in ("x", "y", "c"):
                    forward(name, g, k)

        @pl.when((s >= lag_xy) & (s < S + lag_xy))
        def _():
            g, k = group_and_step(s - lag_xy)
            wait_blocks(2, xy_got.at[g, k])
            for name in ("d1", "d2", "cx", "cy"):
                forward(name, g, k)

        @pl.when((s >= lag_d) & (s < S + lag_d))
        def _():
            g, k = group_and_step(s - lag_d)
            wait_blocks(1, d_got.at[g, k])
            for name in ("cd1", "cd2"):
                forward(name, g, k)

        @pl.when(s >= lag_att)
        def _():
            g, k = group_and_step(s - lag_att)
            wait_blocks(4, core_got.at[g, k])
            j = (s - lag_att) % A
            attend(g, k, j == 0, j == A - 1)

        return carry

    lax.fori_loop(0, S + lag_att, step, 0)

    above = {"aseq": jnp.minimum(a + 1, A - 1)}
    below = {"aseq": jnp.maximum(a - 1, 0)}

    def up_copy(d, c):
        return pltpu.make_async_remote_copy(
            src_ref=up_out.at[d, c], dst_ref=up_in.at[d, c],
            send_sem=sent.at[3], recv_sem=sum_got.at[d + 1, c], device_id=above, device_id_type=MESH,
        )

    def dn_copy(d, c):
        return pltpu.make_async_remote_copy(
            src_ref=dn_out.at[d, c], dst_ref=dn_in.at[d, c],
            send_sem=sent.at[3], recv_sem=sum_got.at[d, c], device_id=below, device_id_type=MESH,
        )

    def first_sends(i, c):
        @pl.when(a == 0)
        def _():
            up_out[A - 1 - i, c] = own[A - 1 - i, c].astype(bf16)
            up_copy(A - 1 - i, c).start()

        @pl.when(a == A - 1)
        def _():
            dn_out[i, c] = own[i, c].astype(bf16)
            dn_copy(i, c).start()

    def multiply(c, carry):
        cols = pl.ds(pl.multiple_of(c * cw, 128), cw)
        pv = jnp.dot(va[...], wv[:, cols], preferred_element_type=f32)
        pa = jnp.dot(aa[...], wa[:, cols], preferred_element_type=f32)
        for d in range(A):
            own[d, c, pl.ds(0, vrows), :] = pv[d * vrows : (d + 1) * vrows]
            own[d, c, pl.ds(vrows, arows), :] = pa[d * arows : (d + 1) * arows]
        first_sends(0, c)
        return carry

    for copy in small[early:]:
        copy.wait()
    lax.fori_loop(0, nC, multiply, 0)

    def later_sends(c, carry):
        first_sends(1 + c // nC, c % nC)
        return carry

    lax.fori_loop(0, (A - 2) * nC, later_sends, 0)

    hop = 2

    def relay(t, carry):
        up = t - hop * jnp.maximum(a - 1, 0)
        dn = t - hop * jnp.maximum(A - 2 - a, 0)

        @pl.when((a > 0) & (up >= 0) & (up < (A - 1 - a) * nC))
        def _():
            d, c = A - 1 - up // nC, up % nC
            up_copy(d, c).wait_recv()
            up_out[d, c] = (own[d, c] + up_in[d, c].astype(f32)).astype(bf16)
            up_copy(d, c).start()

        @pl.when((a < A - 1) & (dn >= 0) & (dn < a * nC))
        def _():
            d, c = dn // nC, dn % nC
            dn_copy(d, c).wait_recv()
            dn_out[d, c] = (own[d, c] + dn_in[d, c].astype(f32)).astype(bf16)
            dn_copy(d, c).start()

        return carry

    level = (levels_ref[frame] + 1).astype(f32)
    frac = jnp.full((8, hd), level, f32) / LEVELS
    timestep = 1000.0 * flow_shift * frac / (1.0 + (flow_shift - 1.0) * frac)
    half_emb = gwv.shape[0] // 2
    turn = timestep * lane[pl.ds(5, 1), :]
    embedding = jnp.concatenate([jnp.cos(turn), jnp.sin(turn)], axis=1)
    high = embedding.astype(bf16).astype(f32)
    mid = (embedding - high).astype(bf16).astype(f32)
    low = embedding - high - mid
    erow = lax.broadcasted_iota(jnp.int32, embedding.shape, 0)
    split = jnp.where(erow == 0, high, jnp.where(erow == 1, mid, jnp.where(erow == 2, low, 0.0))).astype(bf16)
    for i, w_ref in enumerate((gwv, gwa)):
        parts = jnp.dot(split, w_ref[...], preferred_element_type=f32)
        gates[i] = jnp.broadcast_to(jnp.sum(parts, axis=0, keepdims=True), parts.shape)

    lax.fori_loop(0, (A - 2) * (nC + hop), relay, 0)

    def finish(c, carry):
        @pl.when(a > 0)
        def _():
            up_copy(a, c).wait_recv()
            own[a, c] = own[a, c] + up_in[a, c].astype(f32)

        @pl.when(a < A - 1)
        def _():
            dn_copy(a, c).wait_recv()
            own[a, c] = own[a, c] + dn_in[a, c].astype(f32)

        cols = pl.ds(pl.multiple_of(c * cw, 128), cw)
        vo_ref[:, cols] = (
            xv[:, cols].astype(f32) + gates[0, pl.ds(0, 1), cols] * own[a, c, pl.ds(0, vrows), :]
        ).astype(vo_ref.dtype)
        ao_ref[:, cols] = (
            xa[:, cols].astype(f32) + gates[1, pl.ds(0, 1), cols] * own[a, c, pl.ds(vrows, arows), :]
        ).astype(ao_ref.dtype)
        return carry

    lax.fori_loop(0, nC, finish, 0)

    wait_for(kvs, sent.at[0])
    wait_for(qs, sent.at[1])
    wait_for(kv.at[pl.ds(0, 7)], sent.at[2])
    wait_for(up_in.at[pl.ds(0, A - 1)], sent.at[3])


def lane_table(hd, half_emb):
    one_sixth = hd // 6
    first = hd - 4 * one_sixth
    table = np.zeros((8, hd), np.float64)
    start = 0
    for i, width in enumerate((first, 2 * one_sixth, 2 * one_sixth)):
        half = width // 2
        frequency = 10000.0 ** (-(np.arange(half) * 2.0) / width)
        table[0, start : start + width] = np.concatenate([frequency, frequency])
        table[1, start : start + width] = np.repeat([-1.0, 1.0], half)
        table[2 + i, start : start + width] = 1.0
        start += width
    table[5, :half_emb] = np.exp(-math.log(10000.0) * np.arange(half_emb) / half_emb)
    return jnp.asarray(table, jnp.float32)


def store_kernel(v_ref, a_ref, vo_ref, ao_ref, sem):
    one = pltpu.make_async_copy(v_ref, vo_ref, sem.at[0])
    two = pltpu.make_async_copy(a_ref, ao_ref, sem.at[1])
    one.start()
    two.start()
    one.wait()
    two.wait()


def fused(
    video_q, video_k, video_v, audio_q, audio_k, audio_v, video_x, audio_x,
    video_out_w, audio_out_w, video_gate_w, audio_gate_w, levels, video_pos, audio_pos, A, V,
):
    vrows, heads, hd = video_q.shape
    arows = audio_q.shape[0]
    rows = vrows + arows
    group = heads // A
    inner, width = video_out_w.shape
    n_heads = 2
    G = group // n_heads
    nC = 6
    cw = width // nC
    bf16, f32 = jnp.bfloat16, jnp.float32
    anywhere = pl.BlockSpec(memory_space=pl.ANY)
    vmem = pl.BlockSpec(memory_space=pltpu.VMEM)
    wire = pltpu.VMEM((A, nC, rows, cw), bf16)
    dma = pltpu.SemaphoreType.DMA
    temb = video_gate_w.shape[0]
    vo, ao = pl.pallas_call(
        functools.partial(fused_kernel, A, V, n_heads, nC, vrows, arows),
        out_shape=(pltpu.VMEM(video_x.shape, video_x.dtype), pltpu.VMEM(audio_x.shape, audio_x.dtype)),
        in_specs=[anywhere] * 17,
        out_specs=(vmem, vmem),
        scratch_shapes=[
            pltpu.SMEM(levels.shape, levels.dtype),
            pltpu.SMEM(video_pos.shape, video_pos.dtype),
            pltpu.SMEM(audio_pos.shape, audio_pos.dtype),
            pltpu.VMEM((3, vrows, heads, hd), bf16),
            pltpu.VMEM((3, arows, heads, hd), bf16),
            pltpu.VMEM((3, rows * heads, hd), f32),
            pltpu.VMEM(video_x.shape, bf16),
            pltpu.VMEM(audio_x.shape, bf16),
            pltpu.VMEM((inner, width), bf16),
            pltpu.VMEM((inner, width), bf16),
            pltpu.VMEM((temb, width), bf16),
            pltpu.VMEM((temb, width), bf16),
            pltpu.VMEM((8, hd), f32),
            pltpu.VMEM((hd, hd), bf16),
            pltpu.VMEM((A - 1, 2 * group, rows, hd), bf16),
            pltpu.VMEM((A - 1, group, rows, hd), bf16),
            pltpu.VMEM((V, A, 2 * group, rows, hd), bf16),
            pltpu.VMEM((A, group, rows, hd), bf16),
            pltpu.VMEM((A * vrows, group * hd), bf16),
            pltpu.VMEM((A * arows, group * hd), bf16),
            pltpu.VMEM((A, nC, rows, cw), f32),
            wire, wire, wire, wire,
            pltpu.VMEM((2, 8, width), f32),
            pltpu.VMEM((n_heads, A * rows, 1), f32),
            pltpu.VMEM((n_heads, A * rows, 1), f32),
            pltpu.VMEM((n_heads, A * rows, hd), f32),
            dma((17,)), dma((4,)), dma((G, A)), dma((G,)), dma((G, A)), dma((G, A)), dma((G, A)), dma((A + 1, nC)),
        ],
        compiler_params=pltpu.CompilerParams(
            collective_id=2, has_side_effects=True, vmem_limit_bytes=60 * 1024 * 1024
        ),
        name="fused_attention",
    )(
        video_q, video_k, video_v, audio_q, audio_k, audio_v, video_x, audio_x,
        video_out_w, audio_out_w, video_gate_w, audio_gate_w,
        lane_table(hd, temb // 2), swap_matrix(hd), levels, video_pos, audio_pos,
    )
    return pl.pallas_call(
        store_kernel,
        out_shape=(
            jax.ShapeDtypeStruct(video_x.shape, video_x.dtype),
            jax.ShapeDtypeStruct(audio_x.shape, audio_x.dtype),
        ),
        in_specs=[vmem, vmem],
        out_specs=(anywhere, anywhere),
        scratch_shapes=[dma((2,))],
        name="store_result",
    )(pltpu.with_memory_space_constraint(vo, pltpu.VMEM), pltpu.with_memory_space_constraint(ao, pltpu.VMEM))


def local(
    video_q, video_k, video_v, audio_q, audio_k, audio_v, video_x, audio_x,
    video_out_w, audio_out_w, video_gate_w, audio_gate_w, levels, video_pos, audio_pos,
):
    A, V = lax.axis_size("aseq"), lax.axis_size("vseq")
    vrows, heads, hd = video_q.shape
    arows = audio_q.shape[0]
    rows = vrows + arows
    frames = video_pos.shape[0]
    if V == 8 and V == frames and A == 4 and heads % (2 * A) == 0 and hd == video_gate_w.shape[0] // 2:
        return fused(
            video_q, video_k, video_v, audio_q, audio_k, audio_v, video_x, audio_x,
            video_out_w, audio_out_w, video_gate_w, audio_gate_w, levels, video_pos, audio_pos, A, V,
        )
    rank = lax.axis_index(("vseq", "aseq"))
    frame_tokens = vrows * A * V // frames
    token = rank * vrows + jnp.arange(vrows, dtype=jnp.int32)
    frame_of = token // frame_tokens
    within = token % frame_tokens
    frame_ids = jnp.arange(frames, dtype=jnp.int32)
    video_hot = frame_of[:, None] == frame_ids[None, :]
    place_t = jnp.sum(jnp.where(video_hot, video_pos[None, :], 0), axis=1)
    zero = jnp.zeros_like(audio_pos)
    cos, sin = rope_tables(
        hd,
        jnp.concatenate([place_t, audio_pos]),
        jnp.concatenate([within // GRID_W, zero]),
        jnp.concatenate([within % GRID_W, zero]),
    )
    swap = swap_matrix(hd)

    def heads_first(video, audio):
        return jnp.swapaxes(jnp.concatenate([video, audio], axis=0), 0, 1)

    def rotate(x):
        other = jnp.dot(x, swap, preferred_element_type=jnp.float32)
        return (x.astype(jnp.float32) * cos[None] + other * sin[None]).astype(jnp.bfloat16)

    group = heads // A
    qkv = jnp.stack(
        [
            rotate(heads_first(video_q, audio_q)).reshape(A, group, rows, hd),
            rotate(heads_first(video_k, audio_k)).reshape(A, group, rows, hd),
            heads_first(video_v, audio_v).reshape(A, group, rows, hd),
        ],
        axis=1,
    )
    audio_frame = jnp.sum((video_pos[None, :] <= audio_pos[:, None]).astype(jnp.int32), axis=1) - 1
    audio_hot = audio_frame[:, None] == frame_ids[None, :]
    embedding = embedding_of(levels, video_gate_w.shape[0] // 2)

    def split_rows(hot):
        mine = jnp.sum(jnp.where(hot[:, :, None], embedding[None], 0.0), axis=1)
        high = mine.astype(jnp.bfloat16)
        rest = mine - high.astype(jnp.float32)
        mid = rest.astype(jnp.bfloat16)
        low = (rest - mid.astype(jnp.float32)).astype(jnp.bfloat16)
        return jnp.concatenate([high, mid, low], axis=0)

    one_frame = frame_tokens % vrows == 0
    ev = split_rows(video_hot[:8] if one_frame else video_hot)
    ea = split_rows(audio_hot)
    q, kv, gv, ga = gather(qkv, ev, ea, video_gate_w, audio_gate_w, A, V)
    va, aa = attend(q, kv, A, vrows, arows)
    return project(va, aa, video_out_w, audio_out_w, video_x, audio_x, gv, ga, A)


def solution(mesh):
    tokens = P(("vseq", "aseq"), None, None)
    wide = P(("vseq", "aseq"), None)
    return jax.shard_map(
        local,
        mesh=mesh,
        in_specs=(
            tokens, tokens, tokens, tokens, tokens, tokens, wide, wide,
            P("aseq", None), P("aseq", None), P(), P(), P(), P(), P(("vseq", "aseq")),
        ),
        out_specs=(wide, wide),
        check_vma=False,
    )
```

```python
import functools
import math

import jax
import jax.numpy as jnp
import numpy as np
from jax import lax
from jax.experimental import pallas as pl
from jax.experimental.pallas import tpu as pltpu
from jax.sharding import PartitionSpec as P

GRID_W = 32
LEVELS = 1000
flow_shift = 5.0


def rope_tables(head_dim, place_t, place_h, place_w):
    one_sixth = head_dim // 6
    first = head_dim - 4 * one_sixth
    cos_cols, sin_cols = [], []
    for width, places in ((first, place_t), (2 * one_sixth, place_h), (2 * one_sixth, place_w)):
        half = width // 2
        frequency = 10000.0 ** (-(jnp.arange(half, dtype=jnp.float32) * 2.0) / width)
        angles = places.astype(jnp.float32)[:, None] * frequency[None, :]
        cos_part, sin_part = jnp.cos(angles), jnp.sin(angles)
        cos_cols += [cos_part, cos_part]
        sin_cols += [-sin_part, sin_part]
    return jnp.concatenate(cos_cols, axis=1), jnp.concatenate(sin_cols, axis=1)


def swap_matrix(head_dim):
    one_sixth = head_dim // 6
    first = head_dim - 4 * one_sixth
    source = []
    start = 0
    for width in (first, 2 * one_sixth, 2 * one_sixth):
        half = width // 2
        source += list(range(start + half, start + width)) + list(range(start, start + half))
        start += width
    return jnp.asarray(np.arange(head_dim)[:, None] == np.array(source)[None, :], jnp.bfloat16)


def embedding_of(levels, half_emb):
    level_frac = (levels.astype(jnp.float32) + 1.0) / LEVELS
    timestep = 1000.0 * flow_shift * level_frac / (1.0 + (flow_shift - 1.0) * level_frac)
    frequency = jnp.exp(-math.log(10000.0) * jnp.arange(half_emb, dtype=jnp.float32) / half_emb)
    angles = timestep[:, None] * frequency[None, :]
    return jnp.concatenate([jnp.cos(angles), jnp.sin(angles)], axis=1)


def gather_kernel(
    A, V, rows, qkv_ref, ev_ref, ea_ref, gwv_ref, gwa_ref, q_out, kv_out, gv_ref, ga_ref, loc_sem, zs, zr, qs, qr, fs, fr
):
    a = lax.axis_index("aseq")
    v = lax.axis_index("vseq")

    def at_z(k):
        return {"aseq": jnp.bitwise_xor(a, k)}

    def at_v(m):
        return {"vseq": jnp.bitwise_xor(v, m)}

    ring = V == 8
    v_peers = (1, 2, 4) if ring else tuple(range(1, V))
    barrier = pltpu.get_barrier_semaphore()
    for k in range(1, A):
        pl.semaphore_signal(barrier, 1, device_id=at_z(k), device_id_type=pl.DeviceIdType.MESH)
    for m in v_peers:
        pl.semaphore_signal(barrier, 1, device_id=at_v(m), device_id_type=pl.DeviceIdType.MESH)
    pl.semaphore_wait(barrier, A - 1 + len(v_peers))

    def spot(m, k, which=None):
        at = (jnp.bitwise_xor(v, m) * A + jnp.bitwise_xor(a, k)) * rows
        at = pl.ds(pl.multiple_of(at, 8), rows)
        if which is None:
            return kv_out.at[:, :, at, :]
        return kv_out.at[pl.ds(which, 1), :, at, :]

    def q_spot():
        return q_out.at[:, pl.ds(pl.multiple_of(a * rows, 8), rows), :]

    def send(src, dst, ssem, rsem, device):
        copy = pltpu.make_async_remote_copy(
            src_ref=src, dst_ref=dst, send_sem=ssem, recv_sem=rsem,
            device_id=device, device_id_type=pl.DeviceIdType.MESH,
        )
        copy.start()
        return copy

    own_kv = pltpu.make_async_copy(qkv_ref.at[a, pl.ds(1, 2)], spot(0, 0), loc_sem.at[0])
    own_kv.start()
    own_q = pltpu.make_async_copy(qkv_ref.at[a, 0], q_spot(), loc_sem.at[1])
    own_q.start()
    order = [1] + list(range(A - 1, 1, -1))
    z_copies, q_copies = {}, {}
    for k in order:
        z_copies[k] = send(
            qkv_ref.at[jnp.bitwise_xor(a, k), pl.ds(1, 2)], spot(0, 0), zs.at[k], zr.at[k], at_z(k)
        )
    sent = []

    def forward(m, k, which, slot, target):
        copy = send(spot(m, k, which), spot(m, k, which), fs.at[slot, k], fr.at[slot, k], at_v(target))
        sent.append(copy)
        return copy

    got = {}

    def stage_z(k):
        if k == 0:
            own_kv.wait()
        else:
            z_copies[k].wait_recv()
        if ring:
            got["x", k] = forward(0, k, None, 0, 2)
            got["y", k] = forward(0, k, None, 1, 4)
            got["c", k] = forward(0, k, None, 2, 1)
        else:
            for m in v_peers:
                got[m, k] = forward(0, k, None, m, m)

    def stage_xy(k):
        got["x", k].wait_recv()
        got["dk", k] = forward(2, k, 0, 3, 4)
        got["cx", k] = forward(2, k, None, 4, 1)
        got["y", k].wait_recv()
        got["dv", k] = forward(4, k, 1, 5, 2)
        got["cy", k] = forward(4, k, None, 6, 1)

    def stage_d(k):
        got["dk", k].wait_recv()
        got["cdk", k] = forward(6, k, 0, 7, 1)
        got["dv", k].wait_recv()
        got["cdv", k] = forward(6, k, 1, 8, 1)

    stages = [0] + order
    for step in range(A + 2):
        if step < A:
            stage_z(stages[step])
        if step == 0:
            for k in order:
                q_copies[k] = send(
                    qkv_ref.at[jnp.bitwise_xor(a, k), 0], q_spot(), qs.at[k], qr.at[k], at_z(k)
                )
            for e_ref, w_ref, g_ref in ((ev_ref, gwv_ref, gv_ref), (ea_ref, gwa_ref, ga_ref)):
                parts = jnp.dot(e_ref[...], w_ref[...], preferred_element_type=jnp.float32)
                n = g_ref.shape[0]
                g_ref[...] = parts[:n] + parts[n : 2 * n] + parts[2 * n :]
        if ring:
            if 1 <= step < A + 1:
                stage_xy(stages[step - 1])
            if 2 <= step:
                stage_d(stages[step - 2])
    for k in range(A):
        if ring:
            for name in ("c", "cx", "cy", "cdk", "cdv"):
                got[name, k].wait_recv()
        else:
            for m in v_peers:
                got[m, k].wait_recv()
    own_q.wait()
    for k in order:
        q_copies[k].wait()
        z_copies[k].wait_send()
    for copy in sent:
        copy.wait_send()


def gather(qkv, ev, ea, gwv, gwa, A, V):
    _, _, heads, rows, hd = qkv.shape
    slots = 9 if V == 8 else V
    return pl.pallas_call(
        functools.partial(gather_kernel, A, V, rows),
        out_shape=(
            jax.ShapeDtypeStruct((heads, A * rows, hd), qkv.dtype),
            jax.ShapeDtypeStruct((2, heads, V * A * rows, hd), qkv.dtype),
            jax.ShapeDtypeStruct((ev.shape[0] // 3, gwv.shape[1]), jnp.float32),
            jax.ShapeDtypeStruct((ea.shape[0] // 3, gwa.shape[1]), jnp.float32),
        ),
        in_specs=[pl.BlockSpec(memory_space=pl.ANY)] + [pl.BlockSpec(memory_space=pltpu.VMEM)] * 4,
        out_specs=(pl.BlockSpec(memory_space=pl.ANY),) * 2
        + (pl.BlockSpec(memory_space=pltpu.VMEM),) * 2,
        scratch_shapes=[
            pltpu.SemaphoreType.DMA((2,)),
            pltpu.SemaphoreType.DMA((A,)),
            pltpu.SemaphoreType.DMA((A,)),
            pltpu.SemaphoreType.DMA((A,)),
            pltpu.SemaphoreType.DMA((A,)),
            pltpu.SemaphoreType.DMA((slots, A)),
            pltpu.SemaphoreType.DMA((slots, A)),
        ],
        compiler_params=pltpu.CompilerParams(collective_id=0, has_side_effects=True),
        name="gather_heads",
    )(qkv, ev, ea, gwv, gwa)


def attend_kernel(A, vrows, arows, step_keys, q_ref, kv_ref, v_ref, vo_ref, ao_ref):
    q = q_ref[0]
    keys = kv_ref.shape[2]
    scale = math.log2(math.e) / math.sqrt(q.shape[1])
    top, total, acc = None, None, None
    for start in range(0, keys, step_keys):
        k = kv_ref[0, 0, pl.ds(start, step_keys), :]
        vv = v_ref[0, 0, pl.ds(start, step_keys), :]
        s = lax.dot_general(q, k, (((1,), (1,)), ((), ())), preferred_element_type=jnp.float32)
        new_top = jnp.max(s, axis=1, keepdims=True)
        if top is not None:
            new_top = jnp.maximum(new_top, top)
        w = jnp.exp2((s - new_top) * scale)
        part = jnp.sum(w, axis=1, keepdims=True)
        mixed = jnp.dot(w.astype(jnp.bfloat16), vv, preferred_element_type=jnp.float32)
        if top is None:
            total, acc = part, mixed
        else:
            f = jnp.exp2((top - new_top) * scale)
            total, acc = total * f + part, acc * f + mixed
        top = new_top
    o = acc / total
    rows = vrows + arows
    for i in range(A):
        vo_ref[pl.ds(i * vrows, vrows), :] = o[i * rows : i * rows + vrows].astype(vo_ref.dtype)
    ao_ref[...] = jnp.concatenate(
        [o[i * rows + vrows : (i + 1) * rows] for i in range(A)], axis=0
    ).astype(ao_ref.dtype)


def attend(q, kv, A, vrows, arows):
    heads, qrows, hd = q.shape
    keys = kv.shape[2]
    step_keys = keys if keys <= 2048 else 1792
    while keys % step_keys:
        step_keys -= 128
    return pl.pallas_call(
        functools.partial(attend_kernel, A, vrows, arows, step_keys),
        grid=(heads,),
        out_shape=(
            jax.ShapeDtypeStruct((A * vrows, heads * hd), q.dtype),
            jax.ShapeDtypeStruct((A * arows, heads * hd), q.dtype),
        ),
        in_specs=[
            pl.BlockSpec((1, qrows, hd), lambda h: (h, 0, 0)),
            pl.BlockSpec((1, 1, keys, hd), lambda h: (0, h, 0, 0)),
            pl.BlockSpec((1, 1, keys, hd), lambda h: (1, h, 0, 0)),
        ],
        out_specs=(
            pl.BlockSpec((A * vrows, hd), lambda h: (0, h)),
            pl.BlockSpec((A * arows, hd), lambda h: (0, h)),
        ),
        compiler_params=pltpu.CompilerParams(dimension_semantics=("arbitrary",)),
        name="attend_heads",
    )(q, kv, kv)


def project_kernel(
    A, nC, cw, vrows, arows,
    va_ref, aa_ref, wv_hbm, wa_hbm, xv_ref, xa_ref, gv_ref, ga_ref,
    vo_ref, ao_ref,
    wv, wa, own, up_in, dn_in, up_out, dn_out, w_sem, us, ur, ds_, dr,
):
    p = lax.axis_index("aseq")
    loads = []
    for c in range(nC):
        cols = pl.ds(c * cw, cw)
        one = pltpu.make_async_copy(wv_hbm.at[:, cols], wv.at[c], w_sem.at[0, c])
        two = pltpu.make_async_copy(wa_hbm.at[:, cols], wa.at[c], w_sem.at[1, c])
        one.start()
        two.start()
        loads.append((one, two))
    above = {"aseq": jnp.minimum(p + 1, A - 1)}
    below = {"aseq": jnp.maximum(p - 1, 0)}
    MESH = pl.DeviceIdType.MESH
    barrier = pltpu.get_barrier_semaphore()

    for k in range(1, A):
        peer = {"aseq": jnp.bitwise_xor(p, k)}
        pl.semaphore_signal(barrier, 1, device_id=peer, device_id_type=MESH)
    pl.semaphore_wait(barrier, A - 1)

    def up_copy(d, c):
        return pltpu.make_async_remote_copy(
            src_ref=up_out.at[d, c], dst_ref=up_in.at[d, c],
            send_sem=us.at[d, c], recv_sem=ur.at[d, c], device_id=above, device_id_type=MESH,
        )

    def dn_copy(d, c):
        return pltpu.make_async_remote_copy(
            src_ref=dn_out.at[d, c], dst_ref=dn_in.at[d, c],
            send_sem=ds_.at[d, c], recv_sem=dr.at[d, c], device_id=below, device_id_type=MESH,
        )

    def multiply(c):
        one, two = loads[c]
        one.wait()
        pv = jnp.dot(va_ref[...], wv[c], preferred_element_type=jnp.float32)
        two.wait()
        pa = jnp.dot(aa_ref[...], wa[c], preferred_element_type=jnp.float32)
        for d in range(A):
            own[d, c, pl.ds(0, vrows), :] = pv[d * vrows : (d + 1) * vrows]
            own[d, c, pl.ds(vrows, arows), :] = pa[d * arows : (d + 1) * arows]

        first_sends(0, c)

    def first_sends(i, c):
        @pl.when(p == 0)
        def _():
            up_out[A - 1 - i, c] = own[A - 1 - i, c].astype(up_out.dtype)
            up_copy(A - 1 - i, c).start()

        @pl.when(p == A - 1)
        def _():
            dn_out[i, c] = own[i, c].astype(dn_out.dtype)
            dn_copy(i, c).start()

    def relay(i, c):
        d = A - 1 - i

        @pl.when((p > 0) & (p < d))
        def _():
            up_copy(d, c).wait_recv()
            up_out[d, c] = (own[d, c] + up_in[d, c].astype(jnp.float32)).astype(up_out.dtype)
            up_copy(d, c).start()

        @pl.when((p < A - 1) & (p > i))
        def _():
            dn_copy(i, c).wait_recv()
            dn_out[i, c] = (own[i, c] + dn_in[i, c].astype(jnp.float32)).astype(dn_out.dtype)
            dn_copy(i, c).start()

    for c in range(nC):
        multiply(c)
    for i in range(1, A - 1):
        for c in range(nC):
            first_sends(i, c)
    for i in range(A - 1):
        for c in range(nC):
            relay(i, c)

    for c in range(nC):
        @pl.when(p > 0)
        def _():
            up_copy(p, c).wait_recv()
            own[p, c] = own[p, c] + up_in[p, c].astype(jnp.float32)

        @pl.when(p < A - 1)
        def _():
            dn_copy(p, c).wait_recv()
            own[p, c] = own[p, c] + dn_in[p, c].astype(jnp.float32)

        cols = pl.ds(c * cw, cw)
        gate = gv_ref[:, cols] if gv_ref.shape[0] == vrows else gv_ref[pl.ds(0, 1), cols]
        vo_ref[:, cols] = (
            xv_ref[:, cols].astype(jnp.float32) + gate * own[p, c, pl.ds(0, vrows), :]
        ).astype(vo_ref.dtype)
        ao_ref[:, cols] = (
            xa_ref[:, cols].astype(jnp.float32) + ga_ref[:, cols] * own[p, c, pl.ds(vrows, arows), :]
        ).astype(ao_ref.dtype)

    for c in range(nC):
        for d in range(A):
            @pl.when(p < d)
            def _():
                up_copy(d, c).wait_send()

            @pl.when(p > d)
            def _():
                dn_copy(d, c).wait_send()


def project(va, aa, wv, wa, xv, xa, gv, ga, A):
    vrows, width = xv.shape
    arows = xa.shape[0]
    inner = wv.shape[0]
    nC = 2
    cw = width // nC
    rows = vrows + arows
    vmem = pl.BlockSpec(memory_space=pltpu.VMEM)
    hbm = pl.BlockSpec(memory_space=pl.ANY)
    wire = pltpu.VMEM((A, nC, rows, cw), jnp.bfloat16)
    return pl.pallas_call(
        functools.partial(project_kernel, A, nC, cw, vrows, arows),
        out_shape=(
            jax.ShapeDtypeStruct(xv.shape, xv.dtype),
            jax.ShapeDtypeStruct(xa.shape, xa.dtype),
        ),
        in_specs=[vmem, vmem, hbm, hbm, vmem, vmem, vmem, vmem],
        out_specs=(vmem, vmem),
        scratch_shapes=[
            pltpu.VMEM((nC, inner, cw), wv.dtype),
            pltpu.VMEM((nC, inner, cw), wa.dtype),
            pltpu.VMEM((A, nC, rows, cw), jnp.float32),
            wire, wire, wire, wire,
            pltpu.SemaphoreType.DMA((2, nC)),
            pltpu.SemaphoreType.DMA((A, nC)),
            pltpu.SemaphoreType.DMA((A, nC)),
            pltpu.SemaphoreType.DMA((A, nC)),
            pltpu.SemaphoreType.DMA((A, nC)),
        ],
        compiler_params=pltpu.CompilerParams(
            collective_id=1, has_side_effects=True, vmem_limit_bytes=60 * 1024 * 1024
        ),
        name="project_sum",
    )(va, aa, wv, wa, xv, xa, gv, ga)


def fused_kernel(
    A, V, n_heads, nC, vrows, arows,
    vq_h, vk_h, vv_h, aq_h, ak_h, av_h, xv_h, xa_h, wv_h, wa_h, gwv_h, gwa_h, lane_h, swap_h,
    levels_h, video_pos_h, audio_pos_h,
    vo_ref, ao_ref,
    levels_ref, video_pos_ref, audio_pos_ref, raw_v, raw_a, flat, xv, xa, wv, wa, gwv, gwa, lane, swap,
    kvs, qs, kv, q, va, aa, own, up_in, dn_in, up_out, dn_out, gates,
    best, total, mixed,
    in_sem, sent, z_got, q_got, xy_got, d_got, core_got, sum_got,
):
    a = lax.axis_index("aseq")
    v = lax.axis_index("vseq")
    MESH = pl.DeviceIdType.MESH
    rows = vrows + arows
    heads, hd = raw_v.shape[2], raw_v.shape[3]
    group = heads // A
    G = group // n_heads
    cw = own.shape[3]
    f32, bf16 = jnp.float32, jnp.bfloat16

    def at_z(k):
        return {"aseq": jnp.bitwise_xor(a, k)}

    def at_v(m):
        return {"vseq": jnp.bitwise_xor(v, m)}

    barrier = pltpu.get_barrier_semaphore()
    for k in range(1, A):
        pl.semaphore_signal(barrier, 1, device_id=at_z(k), device_id_type=MESH)
    for m in (1, 2, 4):
        pl.semaphore_signal(barrier, 1, device_id=at_v(m), device_id_type=MESH)

    small = []
    for i, (src, dst) in enumerate(
        (
            (lane_h, lane), (swap_h, swap),
            (video_pos_h, video_pos_ref), (audio_pos_h, audio_pos_ref),
            (vk_h, raw_v.at[1]), (ak_h, raw_a.at[1]),
            (vv_h, raw_v.at[2]), (av_h, raw_a.at[2]),
            (vq_h, raw_v.at[0]), (aq_h, raw_a.at[0]),
            (xv_h, xv), (xa_h, xa), (gwv_h, gwv), (gwa_h, gwa), (levels_h, levels_ref),
            (wv_h, wv), (wa_h, wa),
        )
    ):
        small.append(pltpu.make_async_copy(src, dst, in_sem.at[i]))
    early = 10
    for copy in small[:early]:
        copy.start()

    for i in (0, 2, 3):
        small[i].wait()
    frame = v
    row = lax.broadcasted_iota(jnp.int32, (vrows, hd), 0)
    within = a * vrows + row
    at_h = lax.div(within, GRID_W)
    at_w = within - at_h * GRID_W
    place_t = video_pos_ref[frame].astype(f32)
    freq = lane[pl.ds(0, 1), :]
    sign = lane[pl.ds(1, 1), :]
    is_t, is_h, is_w = (lane[pl.ds(i, 1), :] for i in (2, 3, 4))
    video_place = place_t * is_t + at_h.astype(f32) * is_h + at_w.astype(f32) * is_w
    audio_row = lax.broadcasted_iota(jnp.int32, (arows, hd), 0)
    audio_at = jnp.zeros((arows, hd), f32)
    for i in range(arows):
        audio_at = jnp.where(audio_row == i, audio_pos_ref[i].astype(f32), audio_at)
    angle = jnp.concatenate([video_place, audio_at * is_t], axis=0) * freq
    cos, sin = jnp.cos(angle), jnp.sin(angle) * sign

    def flatten(which):
        n = vrows * heads
        flat[which, pl.ds(0, n), :] = raw_v[which].astype(f32).reshape(n, hd)
        flat[which, pl.ds(n, arows * heads), :] = raw_a[which].astype(f32).reshape(arows * heads, hd)

    def head_of(which, h):
        top = flat[which, pl.ds(h, vrows, stride=heads), :]
        low = flat[which, pl.ds(vrows * heads + h, arows, stride=heads), :]
        return jnp.concatenate([top, low], axis=0)

    def rotated(x):
        other = jnp.dot(x.astype(bf16), swap[...], preferred_element_type=f32)
        return (x * cos + other * sin).astype(bf16)

    def z_copy(g, k):
        part = pl.ds(g * 2 * n_heads, 2 * n_heads)
        return pltpu.make_async_remote_copy(
            src_ref=kvs.at[k - 1, part], dst_ref=kv.at[v, a, part],
            send_sem=sent.at[0], recv_sem=z_got.at[g, k], device_id=at_z(k), device_id_type=MESH,
        )

    def q_copy(g, k):
        part = pl.ds(g * n_heads, n_heads)
        return pltpu.make_async_remote_copy(
            src_ref=qs.at[k - 1, part], dst_ref=q.at[a, part],
            send_sem=sent.at[1], recv_sem=q_got.at[g], device_id=at_z(k), device_id_type=MESH,
        )

    lines = {
        "x": (xy_got, 0, None, 2), "y": (xy_got, 0, None, 4), "c": (core_got, 0, None, 1),
        "d1": (d_got, 2, 0, 4), "cx": (core_got, 2, None, 1),
        "d2": (d_got, 4, 1, 2), "cy": (core_got, 4, None, 1),
        "cd1": (core_got, 6, 0, 1), "cd2": (core_got, 6, 1, 1),
    }

    def forward(name, g, k):
        got, m, half, target = lines[name]
        if half is None:
            part = pl.ds(g * 2 * n_heads, 2 * n_heads)
        else:
            part = pl.ds(g * 2 * n_heads + half * n_heads, n_heads)
        slot = kv.at[jnp.bitwise_xor(v, m), jnp.bitwise_xor(a, k), part]
        pltpu.make_async_remote_copy(
            src_ref=slot, dst_ref=slot, send_sem=sent.at[2], recv_sem=got.at[g, k],
            device_id=at_v(target), device_id_type=MESH,
        ).start()

    def wait_for(ref, sem):
        pltpu.make_async_copy(ref, ref, sem).wait()

    def wait_blocks(n, sem):
        wait_for(kv.at[pl.ds(0, n), 0, pl.ds(0, 2 * n_heads)], sem)

    order = [j ^ (j >> 1) for j in range(A)]
    for i in (1, 4, 5, 6, 7):
        small[i].wait()
    flatten(1)
    flatten(2)

    def send_keys(g):
        for k in order[1:] + [0]:
            for i in range(n_heads):
                h = g * n_heads + i
                whole = jnp.bitwise_xor(a, k) * group + h
                key = rotated(head_of(1, whole))
                value = head_of(2, whole).astype(bf16)
                if k:
                    kvs[k - 1, 2 * h] = key
                    kvs[k - 1, 2 * h + 1] = value
                else:
                    kv[v, a, 2 * h] = key
                    kv[v, a, 2 * h + 1] = value
        if g == 0:
            pl.semaphore_wait(barrier, A + 2)
        for k in order[1:]:
            z_copy(g, k).start()
        if g == 0:
            for name in ("x", "y", "c"):
                forward(name, 0, 0)

    def send_queries(g):
        if g == 0:
            small[8].wait()
            small[9].wait()
            flatten(0)
        for k in order[1:] + [0]:
            for i in range(n_heads):
                h = g * n_heads + i
                query = rotated(head_of(0, jnp.bitwise_xor(a, k) * group + h))
                if k:
                    qs[k - 1, h] = query
                else:
                    q[a, h] = query
        for k in order[1:]:
            q_copy(g, k).start()

    for g in range(G):
        send_keys(g)
        if g:
            send_queries(g - 1)
    send_queries(G - 1)

    for copy in small[early:]:
        copy.start()

    scale = math.log2(math.e) / math.sqrt(hd)

    def attend(g, k, first, last):
        plane = jnp.bitwise_xor(a, k)

        @pl.when(first)
        def _():
            wait_for(q.at[pl.ds(0, A - 1), pl.ds(0, n_heads)], q_got.at[g])
            best[...] = jnp.full_like(best, -jnp.inf)
            total[...] = jnp.zeros_like(total)
            mixed[...] = jnp.zeros_like(mixed)

        hs = [g * n_heads + i for i in range(n_heads)]
        ss = [
            lax.dot_general(
                kv[:, plane, 2 * h].reshape(V * rows, hd), q[:, h].reshape(A * rows, hd),
                (((1,), (1,)), ((), ())), preferred_element_type=f32,
            )
            for h in hs
        ]
        befores = [best[i] for i in range(n_heads)]
        tops = [jnp.maximum(b, jnp.max(s, axis=0, keepdims=True)) for b, s in zip(befores, ss)]
        ws = [jnp.exp2((s - top) * scale) for s, top in zip(ss, tops)]
        fades = [jnp.exp2((b - top) * scale) for b, top in zip(befores, tops)]
        totals = [total[i] * fades[i] + jnp.sum(ws[i], axis=0, keepdims=True) for i in range(n_heads)]
        mixes = [
            mixed[i] * fades[i]
            + lax.dot_general(
                kv[:, plane, 2 * hs[i] + 1].reshape(V * rows, hd), ws[i].astype(bf16),
                (((0,), (0,)), ((), ())), preferred_element_type=f32,
            )
            for i in range(n_heads)
        ]
        for i in range(n_heads):
            best[i] = tops[i]
            total[i] = totals[i]
            mixed[i] = mixes[i]

        @pl.when(last)
        def _():
            for i in range(n_heads):
                o = (mixed[i] / total[i]).T
                cols = pl.ds(pl.multiple_of((g * n_heads + i) * hd, hd), hd)
                va[:, cols] = jnp.concatenate(
                    [o[p * rows : p * rows + vrows] for p in range(A)], axis=0
                ).astype(bf16)
                aa[:, cols] = jnp.concatenate(
                    [o[p * rows + vrows : (p + 1) * rows] for p in range(A)], axis=0
                ).astype(bf16)

    S = G * A
    lag_xy, lag_d, lag_att = 2, 5, 9

    def group_and_step(s):
        g = s // A
        j = s % A
        return g, jnp.bitwise_xor(j, j // 2)

    def step(s, carry):
        @pl.when(s < S)
        def _():
            g, k = group_and_step(s)

            @pl.when(k > 0)
            def _():
                z_copy(g, k).wait_recv()

            @pl.when(s > 0)
            def _():
                for name in ("x", "y", "c"):
                    forward(name, g, k)

        @pl.when((s >= lag_xy) & (s < S + lag_xy))
        def _():
            g, k = group_and_step(s - lag_xy)
            wait_blocks(2, xy_got.at[g, k])
            for name in ("d1", "d2", "cx", "cy"):
                forward(name, g, k)

        @pl.when((s >= lag_d) & (s < S + lag_d))
        def _():
            g, k = group_and_step(s - lag_d)
            wait_blocks(1, d_got.at[g, k])
            for name in ("cd1", "cd2"):
                forward(name, g, k)

        @pl.when(s >= lag_att)
        def _():
            g, k = group_and_step(s - lag_att)
            wait_blocks(4, core_got.at[g, k])
            j = (s - lag_att) % A
            attend(g, k, j == 0, j == A - 1)

        return carry

    lax.fori_loop(0, S + lag_att, step, 0)

    above = {"aseq": jnp.minimum(a + 1, A - 1)}
    below = {"aseq": jnp.maximum(a - 1, 0)}

    def up_copy(d, c):
        return pltpu.make_async_remote_copy(
            src_ref=up_out.at[d, c], dst_ref=up_in.at[d, c],
            send_sem=sent.at[3], recv_sem=sum_got.at[d + 1, c], device_id=above, device_id_type=MESH,
        )

    def dn_copy(d, c):
        return pltpu.make_async_remote_copy(
            src_ref=dn_out.at[d, c], dst_ref=dn_in.at[d, c],
            send_sem=sent.at[3], recv_sem=sum_got.at[d, c], device_id=below, device_id_type=MESH,
        )

    def first_sends(i, c):
        @pl.when(a == 0)
        def _():
            up_out[A - 1 - i, c] = own[A - 1 - i, c].astype(bf16)
            up_copy(A - 1 - i, c).start()

        @pl.when(a == A - 1)
        def _():
            dn_out[i, c] = own[i, c].astype(bf16)
            dn_copy(i, c).start()

    def multiply(c, carry):
        cols = pl.ds(pl.multiple_of(c * cw, 128), cw)
        pv = jnp.dot(va[...], wv[:, cols], preferred_element_type=f32)
        pa = jnp.dot(aa[...], wa[:, cols], preferred_element_type=f32)
        for d in range(A):
            own[d, c, pl.ds(0, vrows), :] = pv[d * vrows : (d + 1) * vrows]
            own[d, c, pl.ds(vrows, arows), :] = pa[d * arows : (d + 1) * arows]
        first_sends(0, c)
        return carry

    for copy in small[early:]:
        copy.wait()
    lax.fori_loop(0, nC, multiply, 0)

    def later_sends(c, carry):
        first_sends(1 + c // nC, c % nC)
        return carry

    lax.fori_loop(0, (A - 2) * nC, later_sends, 0)

    hop = 2

    def relay(t, carry):
        up = t - hop * jnp.maximum(a - 1, 0)
        dn = t - hop * jnp.maximum(A - 2 - a, 0)

        @pl.when((a > 0) & (up >= 0) & (up < (A - 1 - a) * nC))
        def _():
            d, c = A - 1 - up // nC, up % nC
            up_copy(d, c).wait_recv()
            up_out[d, c] = (own[d, c] + up_in[d, c].astype(f32)).astype(bf16)
            up_copy(d, c).start()

        @pl.when((a < A - 1) & (dn >= 0) & (dn < a * nC))
        def _():
            d, c = dn // nC, dn % nC
            dn_copy(d, c).wait_recv()
            dn_out[d, c] = (own[d, c] + dn_in[d, c].astype(f32)).astype(bf16)
            dn_copy(d, c).start()

        return carry

    level = (levels_ref[frame] + 1).astype(f32)
    frac = jnp.full((8, hd), level, f32) / LEVELS
    timestep = 1000.0 * flow_shift * frac / (1.0 + (flow_shift - 1.0) * frac)
    half_emb = gwv.shape[0] // 2
    turn = timestep * lane[pl.ds(5, 1), :]
    embedding = jnp.concatenate([jnp.cos(turn), jnp.sin(turn)], axis=1)
    high = embedding.astype(bf16).astype(f32)
    mid = (embedding - high).astype(bf16).astype(f32)
    low = embedding - high - mid
    erow = lax.broadcasted_iota(jnp.int32, embedding.shape, 0)
    split = jnp.where(erow == 0, high, jnp.where(erow == 1, mid, jnp.where(erow == 2, low, 0.0))).astype(bf16)
    for i, w_ref in enumerate((gwv, gwa)):
        parts = jnp.dot(split, w_ref[...], preferred_element_type=f32)
        gates[i] = jnp.broadcast_to(jnp.sum(parts, axis=0, keepdims=True), parts.shape)

    lax.fori_loop(0, (A - 2) * (nC + hop), relay, 0)

    def finish(c, carry):
        @pl.when(a > 0)
        def _():
            up_copy(a, c).wait_recv()
            own[a, c] = own[a, c] + up_in[a, c].astype(f32)

        @pl.when(a < A - 1)
        def _():
            dn_copy(a, c).wait_recv()
            own[a, c] = own[a, c] + dn_in[a, c].astype(f32)

        cols = pl.ds(pl.multiple_of(c * cw, 128), cw)
        vo_ref[:, cols] = (
            xv[:, cols].astype(f32) + gates[0, pl.ds(0, 1), cols] * own[a, c, pl.ds(0, vrows), :]
        ).astype(vo_ref.dtype)
        ao_ref[:, cols] = (
            xa[:, cols].astype(f32) + gates[1, pl.ds(0, 1), cols] * own[a, c, pl.ds(vrows, arows), :]
        ).astype(ao_ref.dtype)
        return carry

    lax.fori_loop(0, nC, finish, 0)

    wait_for(kvs, sent.at[0])
    wait_for(qs, sent.at[1])
    wait_for(kv.at[pl.ds(0, 7)], sent.at[2])
    wait_for(up_in.at[pl.ds(0, A - 1)], sent.at[3])


def lane_table(hd, half_emb):
    one_sixth = hd // 6
    first = hd - 4 * one_sixth
    table = np.zeros((8, hd), np.float64)
    start = 0
    for i, width in enumerate((first, 2 * one_sixth, 2 * one_sixth)):
        half = width // 2
        frequency = 10000.0 ** (-(np.arange(half) * 2.0) / width)
        table[0, start : start + width] = np.concatenate([frequency, frequency])
        table[1, start : start + width] = np.repeat([-1.0, 1.0], half)
        table[2 + i, start : start + width] = 1.0
        start += width
    table[5, :half_emb] = np.exp(-math.log(10000.0) * np.arange(half_emb) / half_emb)
    return jnp.asarray(table, jnp.float32)


def store_kernel(v_ref, a_ref, vo_ref, ao_ref, sem):
    one = pltpu.make_async_copy(v_ref, vo_ref, sem.at[0])
    two = pltpu.make_async_copy(a_ref, ao_ref, sem.at[1])
    one.start()
    two.start()
    one.wait()
    two.wait()


def fused(
    video_q, video_k, video_v, audio_q, audio_k, audio_v, video_x, audio_x,
    video_out_w, audio_out_w, video_gate_w, audio_gate_w, levels, video_pos, audio_pos, A, V,
):
    vrows, heads, hd = video_q.shape
    arows = audio_q.shape[0]
    rows = vrows + arows
    group = heads // A
    inner, width = video_out_w.shape
    n_heads = 2
    G = group // n_heads
    nC = 4
    cw = width // nC
    bf16, f32 = jnp.bfloat16, jnp.float32
    anywhere = pl.BlockSpec(memory_space=pl.ANY)
    vmem = pl.BlockSpec(memory_space=pltpu.VMEM)
    wire = pltpu.VMEM((A, nC, rows, cw), bf16)
    dma = pltpu.SemaphoreType.DMA
    temb = video_gate_w.shape[0]
    vo, ao = pl.pallas_call(
        functools.partial(fused_kernel, A, V, n_heads, nC, vrows, arows),
        out_shape=(pltpu.VMEM(video_x.shape, video_x.dtype), pltpu.VMEM(audio_x.shape, audio_x.dtype)),
        in_specs=[anywhere] * 17,
        out_specs=(vmem, vmem),
        scratch_shapes=[
            pltpu.SMEM(levels.shape, levels.dtype),
            pltpu.SMEM(video_pos.shape, video_pos.dtype),
            pltpu.SMEM(audio_pos.shape, audio_pos.dtype),
            pltpu.VMEM((3, vrows, heads, hd), bf16),
            pltpu.VMEM((3, arows, heads, hd), bf16),
            pltpu.VMEM((3, rows * heads, hd), f32),
            pltpu.VMEM(video_x.shape, bf16),
            pltpu.VMEM(audio_x.shape, bf16),
            pltpu.VMEM((inner, width), bf16),
            pltpu.VMEM((inner, width), bf16),
            pltpu.VMEM((temb, width), bf16),
            pltpu.VMEM((temb, width), bf16),
            pltpu.VMEM((8, hd), f32),
            pltpu.VMEM((hd, hd), bf16),
            pltpu.VMEM((A - 1, 2 * group, rows, hd), bf16),
            pltpu.VMEM((A - 1, group, rows, hd), bf16),
            pltpu.VMEM((V, A, 2 * group, rows, hd), bf16),
            pltpu.VMEM((A, group, rows, hd), bf16),
            pltpu.VMEM((A * vrows, group * hd), bf16),
            pltpu.VMEM((A * arows, group * hd), bf16),
            pltpu.VMEM((A, nC, rows, cw), f32),
            wire, wire, wire, wire,
            pltpu.VMEM((2, 8, width), f32),
            pltpu.VMEM((n_heads, 1, A * rows), f32),
            pltpu.VMEM((n_heads, 1, A * rows), f32),
            pltpu.VMEM((n_heads, hd, A * rows), f32),
            dma((17,)), dma((4,)), dma((G, A)), dma((G,)), dma((G, A)), dma((G, A)), dma((G, A)), dma((A + 1, nC)),
        ],
        compiler_params=pltpu.CompilerParams(
            collective_id=2, has_side_effects=True, vmem_limit_bytes=60 * 1024 * 1024
        ),
        name="fused_attention",
    )(
        video_q, video_k, video_v, audio_q, audio_k, audio_v, video_x, audio_x,
        video_out_w, audio_out_w, video_gate_w, audio_gate_w,
        lane_table(hd, temb // 2), swap_matrix(hd), levels, video_pos, audio_pos,
    )
    return pl.pallas_call(
        store_kernel,
        out_shape=(
            jax.ShapeDtypeStruct(video_x.shape, video_x.dtype),
            jax.ShapeDtypeStruct(audio_x.shape, audio_x.dtype),
        ),
        in_specs=[vmem, vmem],
        out_specs=(anywhere, anywhere),
        scratch_shapes=[dma((2,))],
        name="store_result",
    )(pltpu.with_memory_space_constraint(vo, pltpu.VMEM), pltpu.with_memory_space_constraint(ao, pltpu.VMEM))


def local(
    video_q, video_k, video_v, audio_q, audio_k, audio_v, video_x, audio_x,
    video_out_w, audio_out_w, video_gate_w, audio_gate_w, levels, video_pos, audio_pos,
):
    A, V = lax.axis_size("aseq"), lax.axis_size("vseq")
    vrows, heads, hd = video_q.shape
    arows = audio_q.shape[0]
    rows = vrows + arows
    frames = video_pos.shape[0]
    if V == 8 and V == frames and A == 4 and heads % (2 * A) == 0 and hd == video_gate_w.shape[0] // 2:
        return fused(
            video_q, video_k, video_v, audio_q, audio_k, audio_v, video_x, audio_x,
            video_out_w, audio_out_w, video_gate_w, audio_gate_w, levels, video_pos, audio_pos, A, V,
        )
    rank = lax.axis_index(("vseq", "aseq"))
    frame_tokens = vrows * A * V // frames
    token = rank * vrows + jnp.arange(vrows, dtype=jnp.int32)
    frame_of = token // frame_tokens
    within = token % frame_tokens
    frame_ids = jnp.arange(frames, dtype=jnp.int32)
    video_hot = frame_of[:, None] == frame_ids[None, :]
    place_t = jnp.sum(jnp.where(video_hot, video_pos[None, :], 0), axis=1)
    zero = jnp.zeros_like(audio_pos)
    cos, sin = rope_tables(
        hd,
        jnp.concatenate([place_t, audio_pos]),
        jnp.concatenate([within // GRID_W, zero]),
        jnp.concatenate([within % GRID_W, zero]),
    )
    swap = swap_matrix(hd)

    def heads_first(video, audio):
        return jnp.swapaxes(jnp.concatenate([video, audio], axis=0), 0, 1)

    def rotate(x):
        other = jnp.dot(x, swap, preferred_element_type=jnp.float32)
        return (x.astype(jnp.float32) * cos[None] + other * sin[None]).astype(jnp.bfloat16)

    group = heads // A
    qkv = jnp.stack(
        [
            rotate(heads_first(video_q, audio_q)).reshape(A, group, rows, hd),
            rotate(heads_first(video_k, audio_k)).reshape(A, group, rows, hd),
            heads_first(video_v, audio_v).reshape(A, group, rows, hd),
        ],
        axis=1,
    )
    audio_frame = jnp.sum((video_pos[None, :] <= audio_pos[:, None]).astype(jnp.int32), axis=1) - 1
    audio_hot = audio_frame[:, None] == frame_ids[None, :]
    embedding = embedding_of(levels, video_gate_w.shape[0] // 2)

    def split_rows(hot):
        mine = jnp.sum(jnp.where(hot[:, :, None], embedding[None], 0.0), axis=1)
        high = mine.astype(jnp.bfloat16)
        rest = mine - high.astype(jnp.float32)
        mid = rest.astype(jnp.bfloat16)
        low = (rest - mid.astype(jnp.float32)).astype(jnp.bfloat16)
        return jnp.concatenate([high, mid, low], axis=0)

    one_frame = frame_tokens % vrows == 0
    ev = split_rows(video_hot[:8] if one_frame else video_hot)
    ea = split_rows(audio_hot)
    q, kv, gv, ga = gather(qkv, ev, ea, video_gate_w, audio_gate_w, A, V)
    va, aa = attend(q, kv, A, vrows, arows)
    return project(va, aa, video_out_w, audio_out_w, video_x, audio_x, gv, ga, A)


def solution(mesh):
    tokens = P(("vseq", "aseq"), None, None)
    wide = P(("vseq", "aseq"), None)
    return jax.shard_map(
        local,
        mesh=mesh,
        in_specs=(
            tokens, tokens, tokens, tokens, tokens, tokens, wide, wide,
            P("aseq", None), P("aseq", None), P(), P(), P(), P(), P(("vseq", "aseq")),
        ),
        out_specs=(wide, wide),
        check_vma=False,
    )
```

```python
import functools
import math

import jax
import jax.numpy as jnp
import numpy as np
from jax import lax
from jax.experimental import pallas as pl
from jax.experimental.pallas import tpu as pltpu
from jax.sharding import PartitionSpec as P

GRID_W = 32
LEVELS = 1000
flow_shift = 5.0


def rope_tables(head_dim, place_t, place_h, place_w):
    one_sixth = head_dim // 6
    first = head_dim - 4 * one_sixth
    cos_cols, sin_cols = [], []
    for width, places in ((first, place_t), (2 * one_sixth, place_h), (2 * one_sixth, place_w)):
        half = width // 2
        frequency = 10000.0 ** (-(jnp.arange(half, dtype=jnp.float32) * 2.0) / width)
        angles = places.astype(jnp.float32)[:, None] * frequency[None, :]
        cos_part, sin_part = jnp.cos(angles), jnp.sin(angles)
        cos_cols += [cos_part, cos_part]
        sin_cols += [-sin_part, sin_part]
    return jnp.concatenate(cos_cols, axis=1), jnp.concatenate(sin_cols, axis=1)


def swap_matrix(head_dim):
    one_sixth = head_dim // 6
    first = head_dim - 4 * one_sixth
    source = []
    start = 0
    for width in (first, 2 * one_sixth, 2 * one_sixth):
        half = width // 2
        source += list(range(start + half, start + width)) + list(range(start, start + half))
        start += width
    return jnp.asarray(np.arange(head_dim)[:, None] == np.array(source)[None, :], jnp.bfloat16)


def embedding_of(levels, half_emb):
    level_frac = (levels.astype(jnp.float32) + 1.0) / LEVELS
    timestep = 1000.0 * flow_shift * level_frac / (1.0 + (flow_shift - 1.0) * level_frac)
    frequency = jnp.exp(-math.log(10000.0) * jnp.arange(half_emb, dtype=jnp.float32) / half_emb)
    angles = timestep[:, None] * frequency[None, :]
    return jnp.concatenate([jnp.cos(angles), jnp.sin(angles)], axis=1)


def gather_kernel(
    A, V, rows, qkv_ref, ev_ref, ea_ref, gwv_ref, gwa_ref, q_out, kv_out, gv_ref, ga_ref, loc_sem, zs, zr, qs, qr, fs, fr
):
    a = lax.axis_index("aseq")
    v = lax.axis_index("vseq")

    def at_z(k):
        return {"aseq": jnp.bitwise_xor(a, k)}

    def at_v(m):
        return {"vseq": jnp.bitwise_xor(v, m)}

    ring = V == 8
    v_peers = (1, 2, 4) if ring else tuple(range(1, V))
    barrier = pltpu.get_barrier_semaphore()
    for k in range(1, A):
        pl.semaphore_signal(barrier, 1, device_id=at_z(k), device_id_type=pl.DeviceIdType.MESH)
    for m in v_peers:
        pl.semaphore_signal(barrier, 1, device_id=at_v(m), device_id_type=pl.DeviceIdType.MESH)
    pl.semaphore_wait(barrier, A - 1 + len(v_peers))

    def spot(m, k, which=None):
        at = (jnp.bitwise_xor(v, m) * A + jnp.bitwise_xor(a, k)) * rows
        at = pl.ds(pl.multiple_of(at, 8), rows)
        if which is None:
            return kv_out.at[:, :, at, :]
        return kv_out.at[pl.ds(which, 1), :, at, :]

    def q_spot():
        return q_out.at[:, pl.ds(pl.multiple_of(a * rows, 8), rows), :]

    def send(src, dst, ssem, rsem, device):
        copy = pltpu.make_async_remote_copy(
            src_ref=src, dst_ref=dst, send_sem=ssem, recv_sem=rsem,
            device_id=device, device_id_type=pl.DeviceIdType.MESH,
        )
        copy.start()
        return copy

    own_kv = pltpu.make_async_copy(qkv_ref.at[a, pl.ds(1, 2)], spot(0, 0), loc_sem.at[0])
    own_kv.start()
    own_q = pltpu.make_async_copy(qkv_ref.at[a, 0], q_spot(), loc_sem.at[1])
    own_q.start()
    order = [1] + list(range(A - 1, 1, -1))
    z_copies, q_copies = {}, {}
    for k in order:
        z_copies[k] = send(
            qkv_ref.at[jnp.bitwise_xor(a, k), pl.ds(1, 2)], spot(0, 0), zs.at[k], zr.at[k], at_z(k)
        )
    sent = []

    def forward(m, k, which, slot, target):
        copy = send(spot(m, k, which), spot(m, k, which), fs.at[slot, k], fr.at[slot, k], at_v(target))
        sent.append(copy)
        return copy

    got = {}

    def stage_z(k):
        if k == 0:
            own_kv.wait()
        else:
            z_copies[k].wait_recv()
        if ring:
            got["x", k] = forward(0, k, None, 0, 2)
            got["y", k] = forward(0, k, None, 1, 4)
            got["c", k] = forward(0, k, None, 2, 1)
        else:
            for m in v_peers:
                got[m, k] = forward(0, k, None, m, m)

    def stage_xy(k):
        got["x", k].wait_recv()
        got["dk", k] = forward(2, k, 0, 3, 4)
        got["cx", k] = forward(2, k, None, 4, 1)
        got["y", k].wait_recv()
        got["dv", k] = forward(4, k, 1, 5, 2)
        got["cy", k] = forward(4, k, None, 6, 1)

    def stage_d(k):
        got["dk", k].wait_recv()
        got["cdk", k] = forward(6, k, 0, 7, 1)
        got["dv", k].wait_recv()
        got["cdv", k] = forward(6, k, 1, 8, 1)

    stages = [0] + order
    for step in range(A + 2):
        if step < A:
            stage_z(stages[step])
        if step == 0:
            for k in order:
                q_copies[k] = send(
                    qkv_ref.at[jnp.bitwise_xor(a, k), 0], q_spot(), qs.at[k], qr.at[k], at_z(k)
                )
            for e_ref, w_ref, g_ref in ((ev_ref, gwv_ref, gv_ref), (ea_ref, gwa_ref, ga_ref)):
                parts = jnp.dot(e_ref[...], w_ref[...], preferred_element_type=jnp.float32)
                n = g_ref.shape[0]
                g_ref[...] = parts[:n] + parts[n : 2 * n] + parts[2 * n :]
        if ring:
            if 1 <= step < A + 1:
                stage_xy(stages[step - 1])
            if 2 <= step:
                stage_d(stages[step - 2])
    for k in range(A):
        if ring:
            for name in ("c", "cx", "cy", "cdk", "cdv"):
                got[name, k].wait_recv()
        else:
            for m in v_peers:
                got[m, k].wait_recv()
    own_q.wait()
    for k in order:
        q_copies[k].wait()
        z_copies[k].wait_send()
    for copy in sent:
        copy.wait_send()


def gather(qkv, ev, ea, gwv, gwa, A, V):
    _, _, heads, rows, hd = qkv.shape
    slots = 9 if V == 8 else V
    return pl.pallas_call(
        functools.partial(gather_kernel, A, V, rows),
        out_shape=(
            jax.ShapeDtypeStruct((heads, A * rows, hd), qkv.dtype),
            jax.ShapeDtypeStruct((2, heads, V * A * rows, hd), qkv.dtype),
            jax.ShapeDtypeStruct((ev.shape[0] // 3, gwv.shape[1]), jnp.float32),
            jax.ShapeDtypeStruct((ea.shape[0] // 3, gwa.shape[1]), jnp.float32),
        ),
        in_specs=[pl.BlockSpec(memory_space=pl.ANY)] + [pl.BlockSpec(memory_space=pltpu.VMEM)] * 4,
        out_specs=(pl.BlockSpec(memory_space=pl.ANY),) * 2
        + (pl.BlockSpec(memory_space=pltpu.VMEM),) * 2,
        scratch_shapes=[
            pltpu.SemaphoreType.DMA((2,)),
            pltpu.SemaphoreType.DMA((A,)),
            pltpu.SemaphoreType.DMA((A,)),
            pltpu.SemaphoreType.DMA((A,)),
            pltpu.SemaphoreType.DMA((A,)),
            pltpu.SemaphoreType.DMA((slots, A)),
            pltpu.SemaphoreType.DMA((slots, A)),
        ],
        compiler_params=pltpu.CompilerParams(collective_id=0, has_side_effects=True),
        name="gather_heads",
    )(qkv, ev, ea, gwv, gwa)


def attend_kernel(A, vrows, arows, step_keys, q_ref, kv_ref, v_ref, vo_ref, ao_ref):
    q = q_ref[0]
    keys = kv_ref.shape[2]
    scale = math.log2(math.e) / math.sqrt(q.shape[1])
    top, total, acc = None, None, None
    for start in range(0, keys, step_keys):
        k = kv_ref[0, 0, pl.ds(start, step_keys), :]
        vv = v_ref[0, 0, pl.ds(start, step_keys), :]
        s = lax.dot_general(q, k, (((1,), (1,)), ((), ())), preferred_element_type=jnp.float32)
        new_top = jnp.max(s, axis=1, keepdims=True)
        if top is not None:
            new_top = jnp.maximum(new_top, top)
        w = jnp.exp2((s - new_top) * scale)
        part = jnp.sum(w, axis=1, keepdims=True)
        mixed = jnp.dot(w.astype(jnp.bfloat16), vv, preferred_element_type=jnp.float32)
        if top is None:
            total, acc = part, mixed
        else:
            f = jnp.exp2((top - new_top) * scale)
            total, acc = total * f + part, acc * f + mixed
        top = new_top
    o = acc / total
    rows = vrows + arows
    for i in range(A):
        vo_ref[pl.ds(i * vrows, vrows), :] = o[i * rows : i * rows + vrows].astype(vo_ref.dtype)
    ao_ref[...] = jnp.concatenate(
        [o[i * rows + vrows : (i + 1) * rows] for i in range(A)], axis=0
    ).astype(ao_ref.dtype)


def attend(q, kv, A, vrows, arows):
    heads, qrows, hd = q.shape
    keys = kv.shape[2]
    step_keys = keys if keys <= 2048 else 1792
    while keys % step_keys:
        step_keys -= 128
    return pl.pallas_call(
        functools.partial(attend_kernel, A, vrows, arows, step_keys),
        grid=(heads,),
        out_shape=(
            jax.ShapeDtypeStruct((A * vrows, heads * hd), q.dtype),
            jax.ShapeDtypeStruct((A * arows, heads * hd), q.dtype),
        ),
        in_specs=[
            pl.BlockSpec((1, qrows, hd), lambda h: (h, 0, 0)),
            pl.BlockSpec((1, 1, keys, hd), lambda h: (0, h, 0, 0)),
            pl.BlockSpec((1, 1, keys, hd), lambda h: (1, h, 0, 0)),
        ],
        out_specs=(
            pl.BlockSpec((A * vrows, hd), lambda h: (0, h)),
            pl.BlockSpec((A * arows, hd), lambda h: (0, h)),
        ),
        compiler_params=pltpu.CompilerParams(dimension_semantics=("arbitrary",)),
        name="attend_heads",
    )(q, kv, kv)


def project_kernel(
    A, nC, cw, vrows, arows,
    va_ref, aa_ref, wv_hbm, wa_hbm, xv_ref, xa_ref, gv_ref, ga_ref,
    vo_ref, ao_ref,
    wv, wa, own, up_in, dn_in, up_out, dn_out, w_sem, us, ur, ds_, dr,
):
    p = lax.axis_index("aseq")
    loads = []
    for c in range(nC):
        cols = pl.ds(c * cw, cw)
        one = pltpu.make_async_copy(wv_hbm.at[:, cols], wv.at[c], w_sem.at[0, c])
        two = pltpu.make_async_copy(wa_hbm.at[:, cols], wa.at[c], w_sem.at[1, c])
        one.start()
        two.start()
        loads.append((one, two))
    above = {"aseq": jnp.minimum(p + 1, A - 1)}
    below = {"aseq": jnp.maximum(p - 1, 0)}
    MESH = pl.DeviceIdType.MESH
    barrier = pltpu.get_barrier_semaphore()

    for k in range(1, A):
        peer = {"aseq": jnp.bitwise_xor(p, k)}
        pl.semaphore_signal(barrier, 1, device_id=peer, device_id_type=MESH)
    pl.semaphore_wait(barrier, A - 1)

    def up_copy(d, c):
        return pltpu.make_async_remote_copy(
            src_ref=up_out.at[d, c], dst_ref=up_in.at[d, c],
            send_sem=us.at[d, c], recv_sem=ur.at[d, c], device_id=above, device_id_type=MESH,
        )

    def dn_copy(d, c):
        return pltpu.make_async_remote_copy(
            src_ref=dn_out.at[d, c], dst_ref=dn_in.at[d, c],
            send_sem=ds_.at[d, c], recv_sem=dr.at[d, c], device_id=below, device_id_type=MESH,
        )

    def multiply(c):
        one, two = loads[c]
        one.wait()
        pv = jnp.dot(va_ref[...], wv[c], preferred_element_type=jnp.float32)
        two.wait()
        pa = jnp.dot(aa_ref[...], wa[c], preferred_element_type=jnp.float32)
        for d in range(A):
            own[d, c, pl.ds(0, vrows), :] = pv[d * vrows : (d + 1) * vrows]
            own[d, c, pl.ds(vrows, arows), :] = pa[d * arows : (d + 1) * arows]

        first_sends(0, c)

    def first_sends(i, c):
        @pl.when(p == 0)
        def _():
            up_out[A - 1 - i, c] = own[A - 1 - i, c].astype(up_out.dtype)
            up_copy(A - 1 - i, c).start()

        @pl.when(p == A - 1)
        def _():
            dn_out[i, c] = own[i, c].astype(dn_out.dtype)
            dn_copy(i, c).start()

    def relay(i, c):
        d = A - 1 - i

        @pl.when((p > 0) & (p < d))
        def _():
            up_copy(d, c).wait_recv()
            up_out[d, c] = (own[d, c] + up_in[d, c].astype(jnp.float32)).astype(up_out.dtype)
            up_copy(d, c).start()

        @pl.when((p < A - 1) & (p > i))
        def _():
            dn_copy(i, c).wait_recv()
            dn_out[i, c] = (own[i, c] + dn_in[i, c].astype(jnp.float32)).astype(dn_out.dtype)
            dn_copy(i, c).start()

    for c in range(nC):
        multiply(c)
    for i in range(1, A - 1):
        for c in range(nC):
            first_sends(i, c)
    for i in range(A - 1):
        for c in range(nC):
            relay(i, c)

    for c in range(nC):
        @pl.when(p > 0)
        def _():
            up_copy(p, c).wait_recv()
            own[p, c] = own[p, c] + up_in[p, c].astype(jnp.float32)

        @pl.when(p < A - 1)
        def _():
            dn_copy(p, c).wait_recv()
            own[p, c] = own[p, c] + dn_in[p, c].astype(jnp.float32)

        cols = pl.ds(c * cw, cw)
        gate = gv_ref[:, cols] if gv_ref.shape[0] == vrows else gv_ref[pl.ds(0, 1), cols]
        vo_ref[:, cols] = (
            xv_ref[:, cols].astype(jnp.float32) + gate * own[p, c, pl.ds(0, vrows), :]
        ).astype(vo_ref.dtype)
        ao_ref[:, cols] = (
            xa_ref[:, cols].astype(jnp.float32) + ga_ref[:, cols] * own[p, c, pl.ds(vrows, arows), :]
        ).astype(ao_ref.dtype)

    for c in range(nC):
        for d in range(A):
            @pl.when(p < d)
            def _():
                up_copy(d, c).wait_send()

            @pl.when(p > d)
            def _():
                dn_copy(d, c).wait_send()


def project(va, aa, wv, wa, xv, xa, gv, ga, A):
    vrows, width = xv.shape
    arows = xa.shape[0]
    inner = wv.shape[0]
    nC = 2
    cw = width // nC
    rows = vrows + arows
    vmem = pl.BlockSpec(memory_space=pltpu.VMEM)
    hbm = pl.BlockSpec(memory_space=pl.ANY)
    wire = pltpu.VMEM((A, nC, rows, cw), jnp.bfloat16)
    return pl.pallas_call(
        functools.partial(project_kernel, A, nC, cw, vrows, arows),
        out_shape=(
            jax.ShapeDtypeStruct(xv.shape, xv.dtype),
            jax.ShapeDtypeStruct(xa.shape, xa.dtype),
        ),
        in_specs=[vmem, vmem, hbm, hbm, vmem, vmem, vmem, vmem],
        out_specs=(vmem, vmem),
        scratch_shapes=[
            pltpu.VMEM((nC, inner, cw), wv.dtype),
            pltpu.VMEM((nC, inner, cw), wa.dtype),
            pltpu.VMEM((A, nC, rows, cw), jnp.float32),
            wire, wire, wire, wire,
            pltpu.SemaphoreType.DMA((2, nC)),
            pltpu.SemaphoreType.DMA((A, nC)),
            pltpu.SemaphoreType.DMA((A, nC)),
            pltpu.SemaphoreType.DMA((A, nC)),
            pltpu.SemaphoreType.DMA((A, nC)),
        ],
        compiler_params=pltpu.CompilerParams(
            collective_id=1, has_side_effects=True, vmem_limit_bytes=60 * 1024 * 1024
        ),
        name="project_sum",
    )(va, aa, wv, wa, xv, xa, gv, ga)


def fused_kernel(
    A, V, n_heads, nC, vrows, arows,
    vq_h, vk_h, vv_h, aq_h, ak_h, av_h, xv_h, xa_h, wv_h, wa_h, gwv_h, gwa_h, lane_h, swap_h,
    levels_h, video_pos_h, audio_pos_h,
    vo_ref, ao_ref,
    levels_ref, video_pos_ref, audio_pos_ref, raw_v, raw_a, flat, xv, xa, wv, wa, gwv, gwa, lane, swap,
    kvs, qs, kv, q, va, aa, own, up_in, dn_in, up_out, dn_out, gates,
    best, total, mixed,
    in_sem, sent, z_got, q_got, xy_got, d_got, core_got, sum_got,
):
    a = lax.axis_index("aseq")
    v = lax.axis_index("vseq")
    MESH = pl.DeviceIdType.MESH
    rows = vrows + arows
    heads, hd = raw_v.shape[2], raw_v.shape[3]
    group = heads // A
    G = group // n_heads
    cw = own.shape[3]
    f32, bf16 = jnp.float32, jnp.bfloat16

    def at_z(k):
        return {"aseq": jnp.bitwise_xor(a, k)}

    def at_v(m):
        return {"vseq": jnp.bitwise_xor(v, m)}

    barrier = pltpu.get_barrier_semaphore()
    for k in range(1, A):
        pl.semaphore_signal(barrier, 1, device_id=at_z(k), device_id_type=MESH)
    for m in (1, 2, 4):
        pl.semaphore_signal(barrier, 1, device_id=at_v(m), device_id_type=MESH)

    small = []
    for i, (src, dst) in enumerate(
        (
            (lane_h, lane), (swap_h, swap),
            (video_pos_h, video_pos_ref), (audio_pos_h, audio_pos_ref),
            (vk_h, raw_v.at[1]), (ak_h, raw_a.at[1]),
            (vv_h, raw_v.at[2]), (av_h, raw_a.at[2]),
            (vq_h, raw_v.at[0]), (aq_h, raw_a.at[0]),
            (xv_h, xv), (xa_h, xa), (gwv_h, gwv), (gwa_h, gwa), (levels_h, levels_ref),
            (wv_h, wv), (wa_h, wa),
        )
    ):
        small.append(pltpu.make_async_copy(src, dst, in_sem.at[i]))
    early = 10
    for copy in small[:early]:
        copy.start()

    for i in (0, 2, 3):
        small[i].wait()
    frame = v
    row = lax.broadcasted_iota(jnp.int32, (vrows, hd), 0)
    within = a * vrows + row
    at_h = lax.div(within, GRID_W)
    at_w = within - at_h * GRID_W
    place_t = video_pos_ref[frame].astype(f32)
    freq = lane[pl.ds(0, 1), :]
    sign = lane[pl.ds(1, 1), :]
    is_t, is_h, is_w = (lane[pl.ds(i, 1), :] for i in (2, 3, 4))
    video_place = place_t * is_t + at_h.astype(f32) * is_h + at_w.astype(f32) * is_w
    audio_row = lax.broadcasted_iota(jnp.int32, (arows, hd), 0)
    audio_at = jnp.zeros((arows, hd), f32)
    for i in range(arows):
        audio_at = jnp.where(audio_row == i, audio_pos_ref[i].astype(f32), audio_at)
    angle = jnp.concatenate([video_place, audio_at * is_t], axis=0) * freq
    cos, sin = jnp.cos(angle), jnp.sin(angle) * sign

    def flatten(which):
        n = vrows * heads
        flat[which, pl.ds(0, n), :] = raw_v[which].astype(f32).reshape(n, hd)
        flat[which, pl.ds(n, arows * heads), :] = raw_a[which].astype(f32).reshape(arows * heads, hd)

    def head_of(which, h):
        top = flat[which, pl.ds(h, vrows, stride=heads), :]
        low = flat[which, pl.ds(vrows * heads + h, arows, stride=heads), :]
        return jnp.concatenate([top, low], axis=0)

    def rotated(x):
        other = jnp.dot(x.astype(bf16), swap[...], preferred_element_type=f32)
        return (x * cos + other * sin).astype(bf16)

    def z_copy(g, k):
        part = pl.ds(g * 2 * n_heads, 2 * n_heads)
        return pltpu.make_async_remote_copy(
            src_ref=kvs.at[k - 1, part], dst_ref=kv.at[v, a, part],
            send_sem=sent.at[0], recv_sem=z_got.at[g, k], device_id=at_z(k), device_id_type=MESH,
        )

    def q_copy(g, k):
        part = pl.ds(g * n_heads, n_heads)
        return pltpu.make_async_remote_copy(
            src_ref=qs.at[k - 1, part], dst_ref=q.at[a, part],
            send_sem=sent.at[1], recv_sem=q_got.at[g], device_id=at_z(k), device_id_type=MESH,
        )

    lines = {
        "x": (xy_got, 0, None, 2), "y": (xy_got, 0, None, 4), "c": (core_got, 0, None, 1),
        "d1": (d_got, 2, 0, 4), "cx": (core_got, 2, None, 1),
        "d2": (d_got, 4, 1, 2), "cy": (core_got, 4, None, 1),
        "cd1": (core_got, 6, 0, 1), "cd2": (core_got, 6, 1, 1),
    }

    def forward(name, g, k):
        got, m, half, target = lines[name]
        if half is None:
            part = pl.ds(g * 2 * n_heads, 2 * n_heads)
        else:
            part = pl.ds(g * 2 * n_heads + half * n_heads, n_heads)
        slot = kv.at[jnp.bitwise_xor(v, m), jnp.bitwise_xor(a, k), part]
        pltpu.make_async_remote_copy(
            src_ref=slot, dst_ref=slot, send_sem=sent.at[2], recv_sem=got.at[g, k],
            device_id=at_v(target), device_id_type=MESH,
        ).start()

    def wait_for(ref, sem):
        pltpu.make_async_copy(ref, ref, sem).wait()

    def wait_blocks(n, sem):
        wait_for(kv.at[pl.ds(0, n), 0, pl.ds(0, 2 * n_heads)], sem)

    order = [j ^ (j >> 1) for j in range(A)]
    for i in (1, 4, 5, 6, 7):
        small[i].wait()
    flatten(1)
    flatten(2)

    far = jnp.bitwise_xor(jnp.where(a < A // 2, A - 1, 0), a)
    near = jnp.bitwise_xor(far, 1)
    away = [far, 1, near]

    def send_keys(g):
        for k in order[1:] + [0]:
            for i in range(n_heads):
                h = g * n_heads + i
                whole = jnp.bitwise_xor(a, k) * group + h
                key = rotated(head_of(1, whole))
                value = head_of(2, whole).astype(bf16)
                if k:
                    kvs[k - 1, 2 * h] = key
                    kvs[k - 1, 2 * h + 1] = value
                else:
                    kv[v, a, 2 * h] = key
                    kv[v, a, 2 * h + 1] = value
        if g == 0:
            pl.semaphore_wait(barrier, A + 2)
        for k in away:
            z_copy(g, k).start()
        for name in ("x", "y", "c"):
            forward(name, g, 0)

    def send_queries(g):
        if g == 0:
            small[8].wait()
            small[9].wait()
            flatten(0)
        for k in order[1:] + [0]:
            for i in range(n_heads):
                h = g * n_heads + i
                query = rotated(head_of(0, jnp.bitwise_xor(a, k) * group + h))
                if k:
                    qs[k - 1, h] = query
                else:
                    q[a, h] = query
        for k in away:
            q_copy(g, k).start()

    for g in range(G):
        send_keys(g)
        if g:
            send_queries(g - 1)
    send_queries(G - 1)

    for copy in small[early:]:
        copy.start()

    scale = math.log2(math.e) / math.sqrt(hd)

    def attend(g, k, first, last):
        plane = jnp.bitwise_xor(a, k)

        @pl.when(first)
        def _():
            wait_for(q.at[pl.ds(0, A - 1), pl.ds(0, n_heads)], q_got.at[g])
            best[...] = jnp.full_like(best, -jnp.inf)
            total[...] = jnp.zeros_like(total)
            mixed[...] = jnp.zeros_like(mixed)

        hs = [g * n_heads + i for i in range(n_heads)]
        ss = [
            lax.dot_general(
                kv[:, plane, 2 * h].reshape(V * rows, hd), q[:, h].reshape(A * rows, hd),
                (((1,), (1,)), ((), ())), preferred_element_type=f32,
            )
            for h in hs
        ]
        befores = [best[i] for i in range(n_heads)]
        tops = [jnp.maximum(b, jnp.max(s, axis=0, keepdims=True)) for b, s in zip(befores, ss)]
        ws = [jnp.exp2((s - top) * scale) for s, top in zip(ss, tops)]
        fades = [jnp.exp2((b - top) * scale) for b, top in zip(befores, tops)]
        totals = [total[i] * fades[i] + jnp.sum(ws[i], axis=0, keepdims=True) for i in range(n_heads)]
        mixes = [
            mixed[i] * fades[i]
            + lax.dot_general(
                kv[:, plane, 2 * hs[i] + 1].reshape(V * rows, hd), ws[i].astype(bf16),
                (((0,), (0,)), ((), ())), preferred_element_type=f32,
            )
            for i in range(n_heads)
        ]
        for i in range(n_heads):
            best[i] = tops[i]
            total[i] = totals[i]
            mixed[i] = mixes[i]

        @pl.when(last)
        def _():
            for i in range(n_heads):
                o = (mixed[i] / total[i]).T
                cols = pl.ds(pl.multiple_of((g * n_heads + i) * hd, hd), hd)
                va[:, cols] = jnp.concatenate(
                    [o[p * rows : p * rows + vrows] for p in range(A)], axis=0
                ).astype(bf16)
                aa[:, cols] = jnp.concatenate(
                    [o[p * rows + vrows : (p + 1) * rows] for p in range(A)], axis=0
                ).astype(bf16)

    S = G * A
    lag_xy, lag_d, lag_att = 2, 5, 9

    def group_and_step(s):
        g = s // A
        j = s % A
        return g, jnp.bitwise_xor(j, j // 2)

    def step(s, carry):
        @pl.when(s < S)
        def _():
            g, k = group_and_step(s)

            @pl.when(k > 0)
            def _():
                z_copy(g, k).wait_recv()
                for name in ("x", "y", "c"):
                    forward(name, g, k)

        @pl.when((s >= lag_xy) & (s < S + lag_xy))
        def _():
            g, k = group_and_step(s - lag_xy)
            wait_blocks(2, xy_got.at[g, k])
            for name in ("d1", "d2", "cx", "cy"):
                forward(name, g, k)

        @pl.when((s >= lag_d) & (s < S + lag_d))
        def _():
            g, k = group_and_step(s - lag_d)
            wait_blocks(1, d_got.at[g, k])
            for name in ("cd1", "cd2"):
                forward(name, g, k)

        @pl.when(s >= lag_att)
        def _():
            g, k = group_and_step(s - lag_att)
            wait_blocks(4, core_got.at[g, k])
            j = (s - lag_att) % A
            attend(g, k, j == 0, j == A - 1)

        return carry

    lax.fori_loop(0, S + lag_att, step, 0)

    above = {"aseq": jnp.minimum(a + 1, A - 1)}
    below = {"aseq": jnp.maximum(a - 1, 0)}

    def up_copy(d, c):
        return pltpu.make_async_remote_copy(
            src_ref=up_out.at[d, c], dst_ref=up_in.at[d, c],
            send_sem=sent.at[3], recv_sem=sum_got.at[d + 1, c], device_id=above, device_id_type=MESH,
        )

    def dn_copy(d, c):
        return pltpu.make_async_remote_copy(
            src_ref=dn_out.at[d, c], dst_ref=dn_in.at[d, c],
            send_sem=sent.at[3], recv_sem=sum_got.at[d, c], device_id=below, device_id_type=MESH,
        )

    def first_sends(i, c):
        @pl.when(a == 0)
        def _():
            up_out[A - 1 - i, c] = own[A - 1 - i, c].astype(bf16)
            up_copy(A - 1 - i, c).start()

        @pl.when(a == A - 1)
        def _():
            dn_out[i, c] = own[i, c].astype(bf16)
            dn_copy(i, c).start()

    def multiply(c, carry):
        cols = pl.ds(pl.multiple_of(c * cw, 128), cw)
        pv = jnp.dot(va[...], wv[:, cols], preferred_element_type=f32)
        pa = jnp.dot(aa[...], wa[:, cols], preferred_element_type=f32)
        for d in range(A):
            own[d, c, pl.ds(0, vrows), :] = pv[d * vrows : (d + 1) * vrows]
            own[d, c, pl.ds(vrows, arows), :] = pa[d * arows : (d + 1) * arows]
        first_sends(0, c)
        return carry

    for copy in small[early:]:
        copy.wait()
    lax.fori_loop(0, nC, multiply, 0)

    def later_sends(c, carry):
        first_sends(1 + c // nC, c % nC)
        return carry

    lax.fori_loop(0, (A - 2) * nC, later_sends, 0)

    hop = 2

    def relay(t, carry):
        up = t - hop * jnp.maximum(a - 1, 0)
        dn = t - hop * jnp.maximum(A - 2 - a, 0)

        @pl.when((a > 0) & (up >= 0) & (up < (A - 1 - a) * nC))
        def _():
            d, c = A - 1 - up // nC, up % nC
            up_copy(d, c).wait_recv()
            up_out[d, c] = (own[d, c] + up_in[d, c].astype(f32)).astype(bf16)
            up_copy(d, c).start()

        @pl.when((a < A - 1) & (dn >= 0) & (dn < a * nC))
        def _():
            d, c = dn // nC, dn % nC
            dn_copy(d, c).wait_recv()
            dn_out[d, c] = (own[d, c] + dn_in[d, c].astype(f32)).astype(bf16)
            dn_copy(d, c).start()

        return carry

    level = (levels_ref[frame] + 1).astype(f32)
    frac = jnp.full((8, hd), level, f32) / LEVELS
    timestep = 1000.0 * flow_shift * frac / (1.0 + (flow_shift - 1.0) * frac)
    half_emb = gwv.shape[0] // 2
    turn = timestep * lane[pl.ds(5, 1), :]
    embedding = jnp.concatenate([jnp.cos(turn), jnp.sin(turn)], axis=1)
    high = embedding.astype(bf16).astype(f32)
    mid = (embedding - high).astype(bf16).astype(f32)
    low = embedding - high - mid
    erow = lax.broadcasted_iota(jnp.int32, embedding.shape, 0)
    split = jnp.where(erow == 0, high, jnp.where(erow == 1, mid, jnp.where(erow == 2, low, 0.0))).astype(bf16)
    for i, w_ref in enumerate((gwv, gwa)):
        parts = jnp.dot(split, w_ref[...], preferred_element_type=f32)
        gates[i] = jnp.broadcast_to(jnp.sum(parts, axis=0, keepdims=True), parts.shape)

    lax.fori_loop(0, (A - 2) * (nC + hop), relay, 0)

    def finish(c, carry):
        @pl.when(a > 0)
        def _():
            up_copy(a, c).wait_recv()
            own[a, c] = own[a, c] + up_in[a, c].astype(f32)

        @pl.when(a < A - 1)
        def _():
            dn_copy(a, c).wait_recv()
            own[a, c] = own[a, c] + dn_in[a, c].astype(f32)

        cols = pl.ds(pl.multiple_of(c * cw, 128), cw)
        vo_ref[:, cols] = (
            xv[:, cols].astype(f32) + gates[0, pl.ds(0, 1), cols] * own[a, c, pl.ds(0, vrows), :]
        ).astype(vo_ref.dtype)
        ao_ref[:, cols] = (
            xa[:, cols].astype(f32) + gates[1, pl.ds(0, 1), cols] * own[a, c, pl.ds(vrows, arows), :]
        ).astype(ao_ref.dtype)
        return carry

    lax.fori_loop(0, nC, finish, 0)

    wait_for(kvs, sent.at[0])
    wait_for(qs, sent.at[1])
    wait_for(kv.at[pl.ds(0, 7)], sent.at[2])
    wait_for(up_in.at[pl.ds(0, A - 1)], sent.at[3])


def lane_table(hd, half_emb):
    one_sixth = hd // 6
    first = hd - 4 * one_sixth
    table = np.zeros((8, hd), np.float64)
    start = 0
    for i, width in enumerate((first, 2 * one_sixth, 2 * one_sixth)):
        half = width // 2
        frequency = 10000.0 ** (-(np.arange(half) * 2.0) / width)
        table[0, start : start + width] = np.concatenate([frequency, frequency])
        table[1, start : start + width] = np.repeat([-1.0, 1.0], half)
        table[2 + i, start : start + width] = 1.0
        start += width
    table[5, :half_emb] = np.exp(-math.log(10000.0) * np.arange(half_emb) / half_emb)
    return jnp.asarray(table, jnp.float32)


def store_kernel(v_ref, a_ref, vo_ref, ao_ref, sem):
    one = pltpu.make_async_copy(v_ref, vo_ref, sem.at[0])
    two = pltpu.make_async_copy(a_ref, ao_ref, sem.at[1])
    one.start()
    two.start()
    one.wait()
    two.wait()


def fused(
    video_q, video_k, video_v, audio_q, audio_k, audio_v, video_x, audio_x,
    video_out_w, audio_out_w, video_gate_w, audio_gate_w, levels, video_pos, audio_pos, A, V,
):
    vrows, heads, hd = video_q.shape
    arows = audio_q.shape[0]
    rows = vrows + arows
    group = heads // A
    inner, width = video_out_w.shape
    n_heads = 2
    G = group // n_heads
    nC = 4
    cw = width // nC
    bf16, f32 = jnp.bfloat16, jnp.float32
    anywhere = pl.BlockSpec(memory_space=pl.ANY)
    vmem = pl.BlockSpec(memory_space=pltpu.VMEM)
    wire = pltpu.VMEM((A, nC, rows, cw), bf16)
    dma = pltpu.SemaphoreType.DMA
    temb = video_gate_w.shape[0]
    vo, ao = pl.pallas_call(
        functools.partial(fused_kernel, A, V, n_heads, nC, vrows, arows),
        out_shape=(pltpu.VMEM(video_x.shape, video_x.dtype), pltpu.VMEM(audio_x.shape, audio_x.dtype)),
        in_specs=[anywhere] * 17,
        out_specs=(vmem, vmem),
        scratch_shapes=[
            pltpu.SMEM(levels.shape, levels.dtype),
            pltpu.SMEM(video_pos.shape, video_pos.dtype),
            pltpu.SMEM(audio_pos.shape, audio_pos.dtype),
            pltpu.VMEM((3, vrows, heads, hd), bf16),
            pltpu.VMEM((3, arows, heads, hd), bf16),
            pltpu.VMEM((3, rows * heads, hd), f32),
            pltpu.VMEM(video_x.shape, bf16),
            pltpu.VMEM(audio_x.shape, bf16),
            pltpu.VMEM((inner, width), bf16),
            pltpu.VMEM((inner, width), bf16),
            pltpu.VMEM((temb, width), bf16),
            pltpu.VMEM((temb, width), bf16),
            pltpu.VMEM((8, hd), f32),
            pltpu.VMEM((hd, hd), bf16),
            pltpu.VMEM((A - 1, 2 * group, rows, hd), bf16),
            pltpu.VMEM((A - 1, group, rows, hd), bf16),
            pltpu.VMEM((V, A, 2 * group, rows, hd), bf16),
            pltpu.VMEM((A, group, rows, hd), bf16),
            pltpu.VMEM((A * vrows, group * hd), bf16),
            pltpu.VMEM((A * arows, group * hd), bf16),
            pltpu.VMEM((A, nC, rows, cw), f32),
            wire, wire, wire, wire,
            pltpu.VMEM((2, 8, width), f32),
            pltpu.VMEM((n_heads, 1, A * rows), f32),
            pltpu.VMEM((n_heads, 1, A * rows), f32),
            pltpu.VMEM((n_heads, hd, A * rows), f32),
            dma((17,)), dma((4,)), dma((G, A)), dma((G,)), dma((G, A)), dma((G, A)), dma((G, A)), dma((A + 1, nC)),
        ],
        compiler_params=pltpu.CompilerParams(
            collective_id=2, has_side_effects=True, vmem_limit_bytes=60 * 1024 * 1024
        ),
        name="fused_attention",
    )(
        video_q, video_k, video_v, audio_q, audio_k, audio_v, video_x, audio_x,
        video_out_w, audio_out_w, video_gate_w, audio_gate_w,
        lane_table(hd, temb // 2), swap_matrix(hd), levels, video_pos, audio_pos,
    )
    return pl.pallas_call(
        store_kernel,
        out_shape=(
            jax.ShapeDtypeStruct(video_x.shape, video_x.dtype),
            jax.ShapeDtypeStruct(audio_x.shape, audio_x.dtype),
        ),
        in_specs=[vmem, vmem],
        out_specs=(anywhere, anywhere),
        scratch_shapes=[dma((2,))],
        name="store_result",
    )(pltpu.with_memory_space_constraint(vo, pltpu.VMEM), pltpu.with_memory_space_constraint(ao, pltpu.VMEM))


def local(
    video_q, video_k, video_v, audio_q, audio_k, audio_v, video_x, audio_x,
    video_out_w, audio_out_w, video_gate_w, audio_gate_w, levels, video_pos, audio_pos,
):
    A, V = lax.axis_size("aseq"), lax.axis_size("vseq")
    vrows, heads, hd = video_q.shape
    arows = audio_q.shape[0]
    rows = vrows + arows
    frames = video_pos.shape[0]
    if V == 8 and V == frames and A == 4 and heads % (2 * A) == 0 and hd == video_gate_w.shape[0] // 2:
        return fused(
            video_q, video_k, video_v, audio_q, audio_k, audio_v, video_x, audio_x,
            video_out_w, audio_out_w, video_gate_w, audio_gate_w, levels, video_pos, audio_pos, A, V,
        )
    rank = lax.axis_index(("vseq", "aseq"))
    frame_tokens = vrows * A * V // frames
    token = rank * vrows + jnp.arange(vrows, dtype=jnp.int32)
    frame_of = token // frame_tokens
    within = token % frame_tokens
    frame_ids = jnp.arange(frames, dtype=jnp.int32)
    video_hot = frame_of[:, None] == frame_ids[None, :]
    place_t = jnp.sum(jnp.where(video_hot, video_pos[None, :], 0), axis=1)
    zero = jnp.zeros_like(audio_pos)
    cos, sin = rope_tables(
        hd,
        jnp.concatenate([place_t, audio_pos]),
        jnp.concatenate([within // GRID_W, zero]),
        jnp.concatenate([within % GRID_W, zero]),
    )
    swap = swap_matrix(hd)

    def heads_first(video, audio):
        return jnp.swapaxes(jnp.concatenate([video, audio], axis=0), 0, 1)

    def rotate(x):
        other = jnp.dot(x, swap, preferred_element_type=jnp.float32)
        return (x.astype(jnp.float32) * cos[None] + other * sin[None]).astype(jnp.bfloat16)

    group = heads // A
    qkv = jnp.stack(
        [
            rotate(heads_first(video_q, audio_q)).reshape(A, group, rows, hd),
            rotate(heads_first(video_k, audio_k)).reshape(A, group, rows, hd),
            heads_first(video_v, audio_v).reshape(A, group, rows, hd),
        ],
        axis=1,
    )
    audio_frame = jnp.sum((video_pos[None, :] <= audio_pos[:, None]).astype(jnp.int32), axis=1) - 1
    audio_hot = audio_frame[:, None] == frame_ids[None, :]
    embedding = embedding_of(levels, video_gate_w.shape[0] // 2)

    def split_rows(hot):
        mine = jnp.sum(jnp.where(hot[:, :, None], embedding[None], 0.0), axis=1)
        high = mine.astype(jnp.bfloat16)
        rest = mine - high.astype(jnp.float32)
        mid = rest.astype(jnp.bfloat16)
        low = (rest - mid.astype(jnp.float32)).astype(jnp.bfloat16)
        return jnp.concatenate([high, mid, low], axis=0)

    one_frame = frame_tokens % vrows == 0
    ev = split_rows(video_hot[:8] if one_frame else video_hot)
    ea = split_rows(audio_hot)
    q, kv, gv, ga = gather(qkv, ev, ea, video_gate_w, audio_gate_w, A, V)
    va, aa = attend(q, kv, A, vrows, arows)
    return project(va, aa, video_out_w, audio_out_w, video_x, audio_x, gv, ga, A)


def solution(mesh):
    tokens = P(("vseq", "aseq"), None, None)
    wide = P(("vseq", "aseq"), None)
    return jax.shard_map(
        local,
        mesh=mesh,
        in_specs=(
            tokens, tokens, tokens, tokens, tokens, tokens, wide, wide,
            P("aseq", None), P("aseq", None), P(), P(), P(), P(), P(("vseq", "aseq")),
        ),
        out_specs=(wide, wide),
        check_vma=False,
    )
```

```python
import functools
import math

import jax
import jax.numpy as jnp
import numpy as np
from jax import lax
from jax.experimental import pallas as pl
from jax.experimental.pallas import tpu as pltpu
from jax.sharding import PartitionSpec as P

GRID_W = 32
LEVELS = 1000
flow_shift = 5.0


def rope_tables(head_dim, place_t, place_h, place_w):
    one_sixth = head_dim // 6
    first = head_dim - 4 * one_sixth
    cos_cols, sin_cols = [], []
    for width, places in ((first, place_t), (2 * one_sixth, place_h), (2 * one_sixth, place_w)):
        half = width // 2
        frequency = 10000.0 ** (-(jnp.arange(half, dtype=jnp.float32) * 2.0) / width)
        angles = places.astype(jnp.float32)[:, None] * frequency[None, :]
        cos_part, sin_part = jnp.cos(angles), jnp.sin(angles)
        cos_cols += [cos_part, cos_part]
        sin_cols += [-sin_part, sin_part]
    return jnp.concatenate(cos_cols, axis=1), jnp.concatenate(sin_cols, axis=1)


def swap_matrix(head_dim):
    one_sixth = head_dim // 6
    first = head_dim - 4 * one_sixth
    source = []
    start = 0
    for width in (first, 2 * one_sixth, 2 * one_sixth):
        half = width // 2
        source += list(range(start + half, start + width)) + list(range(start, start + half))
        start += width
    return jnp.asarray(np.arange(head_dim)[:, None] == np.array(source)[None, :], jnp.bfloat16)


def embedding_of(levels, half_emb):
    level_frac = (levels.astype(jnp.float32) + 1.0) / LEVELS
    timestep = 1000.0 * flow_shift * level_frac / (1.0 + (flow_shift - 1.0) * level_frac)
    frequency = jnp.exp(-math.log(10000.0) * jnp.arange(half_emb, dtype=jnp.float32) / half_emb)
    angles = timestep[:, None] * frequency[None, :]
    return jnp.concatenate([jnp.cos(angles), jnp.sin(angles)], axis=1)


def gather_kernel(
    A, V, rows, qkv_ref, ev_ref, ea_ref, gwv_ref, gwa_ref, q_out, kv_out, gv_ref, ga_ref, loc_sem, zs, zr, qs, qr, fs, fr
):
    a = lax.axis_index("aseq")
    v = lax.axis_index("vseq")

    def at_z(k):
        return {"aseq": jnp.bitwise_xor(a, k)}

    def at_v(m):
        return {"vseq": jnp.bitwise_xor(v, m)}

    ring = V == 8
    v_peers = (1, 2, 4) if ring else tuple(range(1, V))
    barrier = pltpu.get_barrier_semaphore()
    for k in range(1, A):
        pl.semaphore_signal(barrier, 1, device_id=at_z(k), device_id_type=pl.DeviceIdType.MESH)
    for m in v_peers:
        pl.semaphore_signal(barrier, 1, device_id=at_v(m), device_id_type=pl.DeviceIdType.MESH)
    pl.semaphore_wait(barrier, A - 1 + len(v_peers))

    def spot(m, k, which=None):
        at = (jnp.bitwise_xor(v, m) * A + jnp.bitwise_xor(a, k)) * rows
        at = pl.ds(pl.multiple_of(at, 8), rows)
        if which is None:
            return kv_out.at[:, :, at, :]
        return kv_out.at[pl.ds(which, 1), :, at, :]

    def q_spot():
        return q_out.at[:, pl.ds(pl.multiple_of(a * rows, 8), rows), :]

    def send(src, dst, ssem, rsem, device):
        copy = pltpu.make_async_remote_copy(
            src_ref=src, dst_ref=dst, send_sem=ssem, recv_sem=rsem,
            device_id=device, device_id_type=pl.DeviceIdType.MESH,
        )
        copy.start()
        return copy

    own_kv = pltpu.make_async_copy(qkv_ref.at[a, pl.ds(1, 2)], spot(0, 0), loc_sem.at[0])
    own_kv.start()
    own_q = pltpu.make_async_copy(qkv_ref.at[a, 0], q_spot(), loc_sem.at[1])
    own_q.start()
    order = [1] + list(range(A - 1, 1, -1))
    z_copies, q_copies = {}, {}
    for k in order:
        z_copies[k] = send(
            qkv_ref.at[jnp.bitwise_xor(a, k), pl.ds(1, 2)], spot(0, 0), zs.at[k], zr.at[k], at_z(k)
        )
    sent = []

    def forward(m, k, which, slot, target):
        copy = send(spot(m, k, which), spot(m, k, which), fs.at[slot, k], fr.at[slot, k], at_v(target))
        sent.append(copy)
        return copy

    got = {}

    def stage_z(k):
        if k == 0:
            own_kv.wait()
        else:
            z_copies[k].wait_recv()
        if ring:
            got["x", k] = forward(0, k, None, 0, 2)
            got["y", k] = forward(0, k, None, 1, 4)
            got["c", k] = forward(0, k, None, 2, 1)
        else:
            for m in v_peers:
                got[m, k] = forward(0, k, None, m, m)

    def stage_xy(k):
        got["x", k].wait_recv()
        got["dk", k] = forward(2, k, 0, 3, 4)
        got["cx", k] = forward(2, k, None, 4, 1)
        got["y", k].wait_recv()
        got["dv", k] = forward(4, k, 1, 5, 2)
        got["cy", k] = forward(4, k, None, 6, 1)

    def stage_d(k):
        got["dk", k].wait_recv()
        got["cdk", k] = forward(6, k, 0, 7, 1)
        got["dv", k].wait_recv()
        got["cdv", k] = forward(6, k, 1, 8, 1)

    stages = [0] + order
    for step in range(A + 2):
        if step < A:
            stage_z(stages[step])
        if step == 0:
            for k in order:
                q_copies[k] = send(
                    qkv_ref.at[jnp.bitwise_xor(a, k), 0], q_spot(), qs.at[k], qr.at[k], at_z(k)
                )
            for e_ref, w_ref, g_ref in ((ev_ref, gwv_ref, gv_ref), (ea_ref, gwa_ref, ga_ref)):
                parts = jnp.dot(e_ref[...], w_ref[...], preferred_element_type=jnp.float32)
                n = g_ref.shape[0]
                g_ref[...] = parts[:n] + parts[n : 2 * n] + parts[2 * n :]
        if ring:
            if 1 <= step < A + 1:
                stage_xy(stages[step - 1])
            if 2 <= step:
                stage_d(stages[step - 2])
    for k in range(A):
        if ring:
            for name in ("c", "cx", "cy", "cdk", "cdv"):
                got[name, k].wait_recv()
        else:
            for m in v_peers:
                got[m, k].wait_recv()
    own_q.wait()
    for k in order:
        q_copies[k].wait()
        z_copies[k].wait_send()
    for copy in sent:
        copy.wait_send()


def gather(qkv, ev, ea, gwv, gwa, A, V):
    _, _, heads, rows, hd = qkv.shape
    slots = 9 if V == 8 else V
    return pl.pallas_call(
        functools.partial(gather_kernel, A, V, rows),
        out_shape=(
            jax.ShapeDtypeStruct((heads, A * rows, hd), qkv.dtype),
            jax.ShapeDtypeStruct((2, heads, V * A * rows, hd), qkv.dtype),
            jax.ShapeDtypeStruct((ev.shape[0] // 3, gwv.shape[1]), jnp.float32),
            jax.ShapeDtypeStruct((ea.shape[0] // 3, gwa.shape[1]), jnp.float32),
        ),
        in_specs=[pl.BlockSpec(memory_space=pl.ANY)] + [pl.BlockSpec(memory_space=pltpu.VMEM)] * 4,
        out_specs=(pl.BlockSpec(memory_space=pl.ANY),) * 2
        + (pl.BlockSpec(memory_space=pltpu.VMEM),) * 2,
        scratch_shapes=[
            pltpu.SemaphoreType.DMA((2,)),
            pltpu.SemaphoreType.DMA((A,)),
            pltpu.SemaphoreType.DMA((A,)),
            pltpu.SemaphoreType.DMA((A,)),
            pltpu.SemaphoreType.DMA((A,)),
            pltpu.SemaphoreType.DMA((slots, A)),
            pltpu.SemaphoreType.DMA((slots, A)),
        ],
        compiler_params=pltpu.CompilerParams(collective_id=0, has_side_effects=True),
        name="gather_heads",
    )(qkv, ev, ea, gwv, gwa)


def attend_kernel(A, vrows, arows, step_keys, q_ref, kv_ref, v_ref, vo_ref, ao_ref):
    q = q_ref[0]
    keys = kv_ref.shape[2]
    scale = math.log2(math.e) / math.sqrt(q.shape[1])
    top, total, acc = None, None, None
    for start in range(0, keys, step_keys):
        k = kv_ref[0, 0, pl.ds(start, step_keys), :]
        vv = v_ref[0, 0, pl.ds(start, step_keys), :]
        s = lax.dot_general(q, k, (((1,), (1,)), ((), ())), preferred_element_type=jnp.float32)
        new_top = jnp.max(s, axis=1, keepdims=True)
        if top is not None:
            new_top = jnp.maximum(new_top, top)
        w = jnp.exp2((s - new_top) * scale)
        part = jnp.sum(w, axis=1, keepdims=True)
        mixed = jnp.dot(w.astype(jnp.bfloat16), vv, preferred_element_type=jnp.float32)
        if top is None:
            total, acc = part, mixed
        else:
            f = jnp.exp2((top - new_top) * scale)
            total, acc = total * f + part, acc * f + mixed
        top = new_top
    o = acc / total
    rows = vrows + arows
    for i in range(A):
        vo_ref[pl.ds(i * vrows, vrows), :] = o[i * rows : i * rows + vrows].astype(vo_ref.dtype)
    ao_ref[...] = jnp.concatenate(
        [o[i * rows + vrows : (i + 1) * rows] for i in range(A)], axis=0
    ).astype(ao_ref.dtype)


def attend(q, kv, A, vrows, arows):
    heads, qrows, hd = q.shape
    keys = kv.shape[2]
    step_keys = keys if keys <= 2048 else 1792
    while keys % step_keys:
        step_keys -= 128
    return pl.pallas_call(
        functools.partial(attend_kernel, A, vrows, arows, step_keys),
        grid=(heads,),
        out_shape=(
            jax.ShapeDtypeStruct((A * vrows, heads * hd), q.dtype),
            jax.ShapeDtypeStruct((A * arows, heads * hd), q.dtype),
        ),
        in_specs=[
            pl.BlockSpec((1, qrows, hd), lambda h: (h, 0, 0)),
            pl.BlockSpec((1, 1, keys, hd), lambda h: (0, h, 0, 0)),
            pl.BlockSpec((1, 1, keys, hd), lambda h: (1, h, 0, 0)),
        ],
        out_specs=(
            pl.BlockSpec((A * vrows, hd), lambda h: (0, h)),
            pl.BlockSpec((A * arows, hd), lambda h: (0, h)),
        ),
        compiler_params=pltpu.CompilerParams(dimension_semantics=("arbitrary",)),
        name="attend_heads",
    )(q, kv, kv)


def project_kernel(
    A, nC, cw, vrows, arows,
    va_ref, aa_ref, wv_hbm, wa_hbm, xv_ref, xa_ref, gv_ref, ga_ref,
    vo_ref, ao_ref,
    wv, wa, own, up_in, dn_in, up_out, dn_out, w_sem, us, ur, ds_, dr,
):
    p = lax.axis_index("aseq")
    loads = []
    for c in range(nC):
        cols = pl.ds(c * cw, cw)
        one = pltpu.make_async_copy(wv_hbm.at[:, cols], wv.at[c], w_sem.at[0, c])
        two = pltpu.make_async_copy(wa_hbm.at[:, cols], wa.at[c], w_sem.at[1, c])
        one.start()
        two.start()
        loads.append((one, two))
    above = {"aseq": jnp.minimum(p + 1, A - 1)}
    below = {"aseq": jnp.maximum(p - 1, 0)}
    MESH = pl.DeviceIdType.MESH
    barrier = pltpu.get_barrier_semaphore()

    for k in range(1, A):
        peer = {"aseq": jnp.bitwise_xor(p, k)}
        pl.semaphore_signal(barrier, 1, device_id=peer, device_id_type=MESH)
    pl.semaphore_wait(barrier, A - 1)

    def up_copy(d, c):
        return pltpu.make_async_remote_copy(
            src_ref=up_out.at[d, c], dst_ref=up_in.at[d, c],
            send_sem=us.at[d, c], recv_sem=ur.at[d, c], device_id=above, device_id_type=MESH,
        )

    def dn_copy(d, c):
        return pltpu.make_async_remote_copy(
            src_ref=dn_out.at[d, c], dst_ref=dn_in.at[d, c],
            send_sem=ds_.at[d, c], recv_sem=dr.at[d, c], device_id=below, device_id_type=MESH,
        )

    def multiply(c):
        one, two = loads[c]
        one.wait()
        pv = jnp.dot(va_ref[...], wv[c], preferred_element_type=jnp.float32)
        two.wait()
        pa = jnp.dot(aa_ref[...], wa[c], preferred_element_type=jnp.float32)
        for d in range(A):
            own[d, c, pl.ds(0, vrows), :] = pv[d * vrows : (d + 1) * vrows]
            own[d, c, pl.ds(vrows, arows), :] = pa[d * arows : (d + 1) * arows]

        first_sends(0, c)

    def first_sends(i, c):
        @pl.when(p == 0)
        def _():
            up_out[A - 1 - i, c] = own[A - 1 - i, c].astype(up_out.dtype)
            up_copy(A - 1 - i, c).start()

        @pl.when(p == A - 1)
        def _():
            dn_out[i, c] = own[i, c].astype(dn_out.dtype)
            dn_copy(i, c).start()

    def relay(i, c):
        d = A - 1 - i

        @pl.when((p > 0) & (p < d))
        def _():
            up_copy(d, c).wait_recv()
            up_out[d, c] = (own[d, c] + up_in[d, c].astype(jnp.float32)).astype(up_out.dtype)
            up_copy(d, c).start()

        @pl.when((p < A - 1) & (p > i))
        def _():
            dn_copy(i, c).wait_recv()
            dn_out[i, c] = (own[i, c] + dn_in[i, c].astype(jnp.float32)).astype(dn_out.dtype)
            dn_copy(i, c).start()

    for c in range(nC):
        multiply(c)
    for i in range(1, A - 1):
        for c in range(nC):
            first_sends(i, c)
    for i in range(A - 1):
        for c in range(nC):
            relay(i, c)

    for c in range(nC):
        @pl.when(p > 0)
        def _():
            up_copy(p, c).wait_recv()
            own[p, c] = own[p, c] + up_in[p, c].astype(jnp.float32)

        @pl.when(p < A - 1)
        def _():
            dn_copy(p, c).wait_recv()
            own[p, c] = own[p, c] + dn_in[p, c].astype(jnp.float32)

        cols = pl.ds(c * cw, cw)
        gate = gv_ref[:, cols] if gv_ref.shape[0] == vrows else gv_ref[pl.ds(0, 1), cols]
        vo_ref[:, cols] = (
            xv_ref[:, cols].astype(jnp.float32) + gate * own[p, c, pl.ds(0, vrows), :]
        ).astype(vo_ref.dtype)
        ao_ref[:, cols] = (
            xa_ref[:, cols].astype(jnp.float32) + ga_ref[:, cols] * own[p, c, pl.ds(vrows, arows), :]
        ).astype(ao_ref.dtype)

    for c in range(nC):
        for d in range(A):
            @pl.when(p < d)
            def _():
                up_copy(d, c).wait_send()

            @pl.when(p > d)
            def _():
                dn_copy(d, c).wait_send()


def project(va, aa, wv, wa, xv, xa, gv, ga, A):
    vrows, width = xv.shape
    arows = xa.shape[0]
    inner = wv.shape[0]
    nC = 2
    cw = width // nC
    rows = vrows + arows
    vmem = pl.BlockSpec(memory_space=pltpu.VMEM)
    hbm = pl.BlockSpec(memory_space=pl.ANY)
    wire = pltpu.VMEM((A, nC, rows, cw), jnp.bfloat16)
    return pl.pallas_call(
        functools.partial(project_kernel, A, nC, cw, vrows, arows),
        out_shape=(
            jax.ShapeDtypeStruct(xv.shape, xv.dtype),
            jax.ShapeDtypeStruct(xa.shape, xa.dtype),
        ),
        in_specs=[vmem, vmem, hbm, hbm, vmem, vmem, vmem, vmem],
        out_specs=(vmem, vmem),
        scratch_shapes=[
            pltpu.VMEM((nC, inner, cw), wv.dtype),
            pltpu.VMEM((nC, inner, cw), wa.dtype),
            pltpu.VMEM((A, nC, rows, cw), jnp.float32),
            wire, wire, wire, wire,
            pltpu.SemaphoreType.DMA((2, nC)),
            pltpu.SemaphoreType.DMA((A, nC)),
            pltpu.SemaphoreType.DMA((A, nC)),
            pltpu.SemaphoreType.DMA((A, nC)),
            pltpu.SemaphoreType.DMA((A, nC)),
        ],
        compiler_params=pltpu.CompilerParams(
            collective_id=1, has_side_effects=True, vmem_limit_bytes=60 * 1024 * 1024
        ),
        name="project_sum",
    )(va, aa, wv, wa, xv, xa, gv, ga)


def fused_kernel(
    A, V, n_heads, nC, vrows, arows,
    vq_h, vk_h, vv_h, aq_h, ak_h, av_h, xv_h, xa_h, wv_h, wa_h, gwv_h, gwa_h, lane_h, swap_h,
    levels_h, video_pos_h, audio_pos_h,
    vo_ref, ao_ref,
    levels_ref, video_pos_ref, audio_pos_ref, raw_v, raw_a, flat, xv, xa, wv, wa, gwv, gwa, lane, swap,
    kvs, qs, kv, q, va, aa, own, up_in, dn_in, up_out, dn_out, gates,
    best, total, mixed,
    in_sem, sent, z_got, q_got, xy_got, d_got, core_got, sum_got,
):
    a = lax.axis_index("aseq")
    v = lax.axis_index("vseq")
    MESH = pl.DeviceIdType.MESH
    rows = vrows + arows
    heads, hd = raw_v.shape[2], raw_v.shape[3]
    group = heads // A
    G = group // n_heads
    cw = own.shape[3]
    f32, bf16 = jnp.float32, jnp.bfloat16

    def at_z(k):
        return {"aseq": jnp.bitwise_xor(a, k)}

    def at_v(m):
        return {"vseq": jnp.bitwise_xor(v, m)}

    barrier = pltpu.get_barrier_semaphore()
    for k in range(1, A):
        pl.semaphore_signal(barrier, 1, device_id=at_z(k), device_id_type=MESH)
    for m in (1, 2, 4):
        pl.semaphore_signal(barrier, 1, device_id=at_v(m), device_id_type=MESH)

    small = []
    for i, (src, dst) in enumerate(
        (
            (lane_h, lane), (swap_h, swap),
            (video_pos_h, video_pos_ref), (audio_pos_h, audio_pos_ref),
            (vk_h, raw_v.at[1]), (ak_h, raw_a.at[1]),
            (vv_h, raw_v.at[2]), (av_h, raw_a.at[2]),
            (vq_h, raw_v.at[0]), (aq_h, raw_a.at[0]),
            (xv_h, xv), (xa_h, xa), (gwv_h, gwv), (gwa_h, gwa), (levels_h, levels_ref),
            (wv_h, wv), (wa_h, wa),
        )
    ):
        small.append(pltpu.make_async_copy(src, dst, in_sem.at[i]))
    early = 10
    for i in (4, 5, 6, 7, 0, 2, 3, 1, 8, 9):
        small[i].start()

    for i in (0, 2, 3):
        small[i].wait()
    frame = v
    row = lax.broadcasted_iota(jnp.int32, (vrows, hd), 0)
    within = a * vrows + row
    at_h = lax.div(within, GRID_W)
    at_w = within - at_h * GRID_W
    place_t = video_pos_ref[frame].astype(f32)
    freq = lane[pl.ds(0, 1), :]
    sign = lane[pl.ds(1, 1), :]
    is_t, is_h, is_w = (lane[pl.ds(i, 1), :] for i in (2, 3, 4))
    video_place = place_t * is_t + at_h.astype(f32) * is_h + at_w.astype(f32) * is_w
    audio_row = lax.broadcasted_iota(jnp.int32, (arows, hd), 0)
    audio_at = jnp.zeros((arows, hd), f32)
    for i in range(arows):
        audio_at = jnp.where(audio_row == i, audio_pos_ref[i].astype(f32), audio_at)
    angle = jnp.concatenate([video_place, audio_at * is_t], axis=0) * freq
    cos, sin = jnp.cos(angle), jnp.sin(angle) * sign

    def flatten(which):
        n = vrows * heads
        flat[which, pl.ds(0, n), :] = raw_v[which].astype(f32).reshape(n, hd)
        flat[which, pl.ds(n, arows * heads), :] = raw_a[which].astype(f32).reshape(arows * heads, hd)

    def head_of(which, h):
        top = flat[which, pl.ds(h, vrows, stride=heads), :]
        low = flat[which, pl.ds(vrows * heads + h, arows, stride=heads), :]
        return jnp.concatenate([top, low], axis=0)

    def rotated(x):
        other = jnp.dot(x.astype(bf16), swap[...], preferred_element_type=f32)
        return (x * cos + other * sin).astype(bf16)

    def z_copy(g, k):
        part = pl.ds(g * 2 * n_heads, 2 * n_heads)
        return pltpu.make_async_remote_copy(
            src_ref=kvs.at[k - 1, part], dst_ref=kv.at[v, a, part],
            send_sem=sent.at[0], recv_sem=z_got.at[g, k - 1], device_id=at_z(k), device_id_type=MESH,
        )

    def q_copy(g, k):
        part = pl.ds(g * n_heads, n_heads)
        return pltpu.make_async_remote_copy(
            src_ref=qs.at[k - 1, part], dst_ref=q.at[a, part],
            send_sem=sent.at[1], recv_sem=q_got.at[g], device_id=at_z(k), device_id_type=MESH,
        )

    lines = {
        "x": (xy_got, 0, None, 2), "y": (xy_got, 0, None, 4), "c": (core_got, 0, None, 1),
        "d1": (d_got, 2, 0, 4), "cx": (core_got, 2, None, 1),
        "d2": (d_got, 4, 1, 2), "cy": (core_got, 4, None, 1),
        "cd1": (core_got, 6, 0, 1), "cd2": (core_got, 6, 1, 1),
    }

    def forward(name, g, k):
        got, m, half, target = lines[name]
        if half is None:
            part = pl.ds(g * 2 * n_heads, 2 * n_heads)
        else:
            part = pl.ds(g * 2 * n_heads + half * n_heads, n_heads)
        slot = kv.at[jnp.bitwise_xor(v, m), jnp.bitwise_xor(a, k), part]
        pltpu.make_async_remote_copy(
            src_ref=slot, dst_ref=slot, send_sem=sent.at[2], recv_sem=got.at[g, k],
            device_id=at_v(target), device_id_type=MESH,
        ).start()

    def wait_for(ref, sem):
        pltpu.make_async_copy(ref, ref, sem).wait()

    def wait_blocks(n, sem):
        wait_for(kv.at[pl.ds(0, n), 0, pl.ds(0, 2 * n_heads)], sem)

    order = [j ^ (j >> 1) for j in range(A)]
    for i in (1, 4, 5, 6, 7):
        small[i].wait()
    flatten(1)
    flatten(2)

    far = jnp.bitwise_xor(jnp.where(a < A // 2, A - 1, 0), a)
    near = jnp.bitwise_xor(far, 1)
    away = [far, 1, near]

    def send_keys(g):
        for k in order[1:] + [0]:
            for i in range(n_heads):
                h = g * n_heads + i
                whole = jnp.bitwise_xor(a, k) * group + h
                key = rotated(head_of(1, whole))
                value = head_of(2, whole).astype(bf16)
                if k:
                    kvs[k - 1, 2 * h] = key
                    kvs[k - 1, 2 * h + 1] = value
                else:
                    kv[v, a, 2 * h] = key
                    kv[v, a, 2 * h + 1] = value
        if g == 0:
            pl.semaphore_wait(barrier, A + 2)
        for k in away:
            z_copy(g, k).start()
        for name in ("x", "y", "c"):
            forward(name, g, 0)

    def send_queries(g):
        if g == 0:
            small[8].wait()
            small[9].wait()
            flatten(0)
        for k in order[1:] + [0]:
            for i in range(n_heads):
                h = g * n_heads + i
                query = rotated(head_of(0, jnp.bitwise_xor(a, k) * group + h))
                if k:
                    qs[k - 1, h] = query
                else:
                    q[a, h] = query
        for k in away:
            q_copy(g, k).start()

    for g in range(G):
        send_keys(g)
        if g:
            send_queries(g - 1)
    send_queries(G - 1)

    for copy in small[early:]:
        copy.start()

    scale = math.log2(math.e) / math.sqrt(hd)

    def attend(g, k, first, last):
        plane = jnp.bitwise_xor(a, k)

        @pl.when(first)
        def _():
            wait_for(q.at[pl.ds(0, A - 1), pl.ds(0, n_heads)], q_got.at[g])
            best[...] = jnp.full_like(best, -jnp.inf)
            total[...] = jnp.zeros_like(total)
            mixed[...] = jnp.zeros_like(mixed)

        hs = [g * n_heads + i for i in range(n_heads)]
        ss = [
            lax.dot_general(
                kv[:, plane, 2 * h].reshape(V * rows, hd), q[:, h].reshape(A * rows, hd),
                (((1,), (1,)), ((), ())), preferred_element_type=f32,
            )
            for h in hs
        ]
        befores = [best[i] for i in range(n_heads)]
        tops = [jnp.maximum(b, jnp.max(s, axis=0, keepdims=True)) for b, s in zip(befores, ss)]
        ws = [jnp.exp2((s - top) * scale) for s, top in zip(ss, tops)]
        fades = [jnp.exp2((b - top) * scale) for b, top in zip(befores, tops)]
        totals = [total[i] * fades[i] + jnp.sum(ws[i], axis=0, keepdims=True) for i in range(n_heads)]
        mixes = [
            mixed[i] * fades[i]
            + lax.dot_general(
                kv[:, plane, 2 * hs[i] + 1].reshape(V * rows, hd), ws[i].astype(bf16),
                (((0,), (0,)), ((), ())), preferred_element_type=f32,
            )
            for i in range(n_heads)
        ]
        for i in range(n_heads):
            best[i] = tops[i]
            total[i] = totals[i]
            mixed[i] = mixes[i]

        @pl.when(last)
        def _():
            for i in range(n_heads):
                o = (mixed[i] / total[i]).T
                cols = pl.ds(pl.multiple_of((g * n_heads + i) * hd, hd), hd)
                va[:, cols] = jnp.concatenate(
                    [o[p * rows : p * rows + vrows] for p in range(A)], axis=0
                ).astype(bf16)
                aa[:, cols] = jnp.concatenate(
                    [o[p * rows + vrows : (p + 1) * rows] for p in range(A)], axis=0
                ).astype(bf16)

    S = G * A
    lag_xy, lag_d, lag_att = 2, 5, 9

    def group_and_step(s):
        g = s // A
        j = s % A
        return g, jnp.bitwise_xor(j, j // 2)

    def step(s, carry):
        @pl.when(s < S)
        def _():
            g, k = group_and_step(s)

            @pl.when(k > 0)
            def _():
                z_copy(g, k).wait_recv()
                for name in ("x", "y", "c"):
                    forward(name, g, k)

        @pl.when((s >= lag_xy) & (s < S + lag_xy))
        def _():
            g, k = group_and_step(s - lag_xy)
            wait_blocks(2, xy_got.at[g, k])
            for name in ("d1", "d2", "cx", "cy"):
                forward(name, g, k)

        @pl.when((s >= lag_d) & (s < S + lag_d))
        def _():
            g, k = group_and_step(s - lag_d)
            wait_blocks(1, d_got.at[g, k])
            for name in ("cd1", "cd2"):
                forward(name, g, k)

        @pl.when(s >= lag_att)
        def _():
            g, k = group_and_step(s - lag_att)
            wait_blocks(4, core_got.at[g, k])
            j = (s - lag_att) % A
            attend(g, k, j == 0, j == A - 1)

        return carry

    lax.fori_loop(0, S + lag_att, step, 0)

    above = {"aseq": jnp.minimum(a + 1, A - 1)}
    below = {"aseq": jnp.maximum(a - 1, 0)}

    def up_copy(d, c):
        return pltpu.make_async_remote_copy(
            src_ref=up_out.at[d, c], dst_ref=up_in.at[d, c],
            send_sem=sent.at[3], recv_sem=sum_got.at[d + 1, c], device_id=above, device_id_type=MESH,
        )

    def dn_copy(d, c):
        return pltpu.make_async_remote_copy(
            src_ref=dn_out.at[d, c], dst_ref=dn_in.at[d, c],
            send_sem=sent.at[3], recv_sem=sum_got.at[d, c], device_id=below, device_id_type=MESH,
        )

    def first_sends(i, c):
        @pl.when(a == 0)
        def _():
            up_out[A - 1 - i, c] = own[A - 1 - i, c].astype(bf16)
            up_copy(A - 1 - i, c).start()

        @pl.when(a == A - 1)
        def _():
            dn_out[i, c] = own[i, c].astype(bf16)
            dn_copy(i, c).start()

    def multiply(c, carry):
        cols = pl.ds(pl.multiple_of(c * cw, 128), cw)
        pv = jnp.dot(va[...], wv[:, cols], preferred_element_type=f32)
        pa = jnp.dot(aa[...], wa[:, cols], preferred_element_type=f32)
        for d in range(A):
            own[d, c, pl.ds(0, vrows), :] = pv[d * vrows : (d + 1) * vrows]
            own[d, c, pl.ds(vrows, arows), :] = pa[d * arows : (d + 1) * arows]
        first_sends(0, c)
        return carry

    for copy in small[early:]:
        copy.wait()
    lax.fori_loop(0, nC, multiply, 0)

    def later_sends(c, carry):
        first_sends(1 + c // nC, c % nC)
        return carry

    lax.fori_loop(0, (A - 2) * nC, later_sends, 0)

    hop = 2

    def relay(t, carry):
        up = t - hop * jnp.maximum(a - 1, 0)
        dn = t - hop * jnp.maximum(A - 2 - a, 0)

        @pl.when((a > 0) & (up >= 0) & (up < (A - 1 - a) * nC))
        def _():
            d, c = A - 1 - up // nC, up % nC
            up_copy(d, c).wait_recv()
            up_out[d, c] = (own[d, c] + up_in[d, c].astype(f32)).astype(bf16)
            up_copy(d, c).start()

        @pl.when((a < A - 1) & (dn >= 0) & (dn < a * nC))
        def _():
            d, c = dn // nC, dn % nC
            dn_copy(d, c).wait_recv()
            dn_out[d, c] = (own[d, c] + dn_in[d, c].astype(f32)).astype(bf16)
            dn_copy(d, c).start()

        return carry

    level = (levels_ref[frame] + 1).astype(f32)
    frac = jnp.full((8, hd), level, f32) / LEVELS
    timestep = 1000.0 * flow_shift * frac / (1.0 + (flow_shift - 1.0) * frac)
    half_emb = gwv.shape[0] // 2
    turn = timestep * lane[pl.ds(5, 1), :]
    embedding = jnp.concatenate([jnp.cos(turn), jnp.sin(turn)], axis=1)
    high = embedding.astype(bf16).astype(f32)
    mid = (embedding - high).astype(bf16).astype(f32)
    low = embedding - high - mid
    erow = lax.broadcasted_iota(jnp.int32, embedding.shape, 0)
    split = jnp.where(erow == 0, high, jnp.where(erow == 1, mid, jnp.where(erow == 2, low, 0.0))).astype(bf16)
    for i, w_ref in enumerate((gwv, gwa)):
        parts = jnp.dot(split, w_ref[...], preferred_element_type=f32)
        gates[i] = jnp.broadcast_to(jnp.sum(parts, axis=0, keepdims=True), parts.shape)

    lax.fori_loop(0, (A - 2) * (nC + hop), relay, 0)

    def finish(c, carry):
        @pl.when(a > 0)
        def _():
            up_copy(a, c).wait_recv()
            own[a, c] = own[a, c] + up_in[a, c].astype(f32)

        @pl.when(a < A - 1)
        def _():
            dn_copy(a, c).wait_recv()
            own[a, c] = own[a, c] + dn_in[a, c].astype(f32)

        cols = pl.ds(pl.multiple_of(c * cw, 128), cw)
        vo_ref[:, cols] = (
            xv[:, cols].astype(f32) + gates[0, pl.ds(0, 1), cols] * own[a, c, pl.ds(0, vrows), :]
        ).astype(vo_ref.dtype)
        ao_ref[:, cols] = (
            xa[:, cols].astype(f32) + gates[1, pl.ds(0, 1), cols] * own[a, c, pl.ds(vrows, arows), :]
        ).astype(ao_ref.dtype)
        return carry

    lax.fori_loop(0, nC, finish, 0)

    wait_for(kvs, sent.at[0])
    wait_for(qs, sent.at[1])
    wait_for(kv.at[pl.ds(0, 7)], sent.at[2])
    wait_for(up_in.at[pl.ds(0, A - 1)], sent.at[3])


def lane_table(hd, half_emb):
    one_sixth = hd // 6
    first = hd - 4 * one_sixth
    table = np.zeros((8, hd), np.float64)
    start = 0
    for i, width in enumerate((first, 2 * one_sixth, 2 * one_sixth)):
        half = width // 2
        frequency = 10000.0 ** (-(np.arange(half) * 2.0) / width)
        table[0, start : start + width] = np.concatenate([frequency, frequency])
        table[1, start : start + width] = np.repeat([-1.0, 1.0], half)
        table[2 + i, start : start + width] = 1.0
        start += width
    table[5, :half_emb] = np.exp(-math.log(10000.0) * np.arange(half_emb) / half_emb)
    return jnp.asarray(table, jnp.float32)


def store_kernel(v_ref, a_ref, vo_ref, ao_ref, sem):
    one = pltpu.make_async_copy(v_ref, vo_ref, sem.at[0])
    two = pltpu.make_async_copy(a_ref, ao_ref, sem.at[1])
    one.start()
    two.start()
    one.wait()
    two.wait()


def fused(
    video_q, video_k, video_v, audio_q, audio_k, audio_v, video_x, audio_x,
    video_out_w, audio_out_w, video_gate_w, audio_gate_w, levels, video_pos, audio_pos, A, V,
):
    vrows, heads, hd = video_q.shape
    arows = audio_q.shape[0]
    rows = vrows + arows
    group = heads // A
    inner, width = video_out_w.shape
    n_heads = 2
    G = group // n_heads
    nC = 4
    cw = width // nC
    bf16, f32 = jnp.bfloat16, jnp.float32
    anywhere = pl.BlockSpec(memory_space=pl.ANY)
    vmem = pl.BlockSpec(memory_space=pltpu.VMEM)
    wire = pltpu.VMEM((A, nC, rows, cw), bf16)
    dma = pltpu.SemaphoreType.DMA
    temb = video_gate_w.shape[0]
    vo, ao = pl.pallas_call(
        functools.partial(fused_kernel, A, V, n_heads, nC, vrows, arows),
        out_shape=(pltpu.VMEM(video_x.shape, video_x.dtype), pltpu.VMEM(audio_x.shape, audio_x.dtype)),
        in_specs=[anywhere] * 17,
        out_specs=(vmem, vmem),
        scratch_shapes=[
            pltpu.SMEM(levels.shape, levels.dtype),
            pltpu.SMEM(video_pos.shape, video_pos.dtype),
            pltpu.SMEM(audio_pos.shape, audio_pos.dtype),
            pltpu.VMEM((3, vrows, heads, hd), bf16),
            pltpu.VMEM((3, arows, heads, hd), bf16),
            pltpu.VMEM((3, rows * heads, hd), f32),
            pltpu.VMEM(video_x.shape, bf16),
            pltpu.VMEM(audio_x.shape, bf16),
            pltpu.VMEM((inner, width), bf16),
            pltpu.VMEM((inner, width), bf16),
            pltpu.VMEM((temb, width), bf16),
            pltpu.VMEM((temb, width), bf16),
            pltpu.VMEM((8, hd), f32),
            pltpu.VMEM((hd, hd), bf16),
            pltpu.VMEM((A - 1, 2 * group, rows, hd), bf16),
            pltpu.VMEM((A - 1, group, rows, hd), bf16),
            pltpu.VMEM((V, A, 2 * group, rows, hd), bf16),
            pltpu.VMEM((A, group, rows, hd), bf16),
            pltpu.VMEM((A * vrows, group * hd), bf16),
            pltpu.VMEM((A * arows, group * hd), bf16),
            pltpu.VMEM((A, nC, rows, cw), f32),
            wire, wire, wire, wire,
            pltpu.VMEM((2, 8, width), f32),
            pltpu.VMEM((n_heads, 1, A * rows), f32),
            pltpu.VMEM((n_heads, 1, A * rows), f32),
            pltpu.VMEM((n_heads, hd, A * rows), f32),
            dma((17,)), dma((4,)), dma((G, A - 1)), dma((G,)), dma((G, A)), dma((G, A)), dma((G, A)), dma((A + 1, nC)),
        ],
        compiler_params=pltpu.CompilerParams(
            collective_id=2, has_side_effects=True, vmem_limit_bytes=60 * 1024 * 1024
        ),
        name="fused_attention",
    )(
        video_q, video_k, video_v, audio_q, audio_k, audio_v, video_x, audio_x,
        video_out_w, audio_out_w, video_gate_w, audio_gate_w,
        lane_table(hd, temb // 2), swap_matrix(hd), levels, video_pos, audio_pos,
    )
    return pl.pallas_call(
        store_kernel,
        out_shape=(
            jax.ShapeDtypeStruct(video_x.shape, video_x.dtype),
            jax.ShapeDtypeStruct(audio_x.shape, audio_x.dtype),
        ),
        in_specs=[vmem, vmem],
        out_specs=(anywhere, anywhere),
        scratch_shapes=[dma((2,))],
        name="store_result",
    )(pltpu.with_memory_space_constraint(vo, pltpu.VMEM), pltpu.with_memory_space_constraint(ao, pltpu.VMEM))


def local(
    video_q, video_k, video_v, audio_q, audio_k, audio_v, video_x, audio_x,
    video_out_w, audio_out_w, video_gate_w, audio_gate_w, levels, video_pos, audio_pos,
):
    A, V = lax.axis_size("aseq"), lax.axis_size("vseq")
    vrows, heads, hd = video_q.shape
    arows = audio_q.shape[0]
    rows = vrows + arows
    frames = video_pos.shape[0]
    if V == 8 and V == frames and A == 4 and heads % (2 * A) == 0 and hd == video_gate_w.shape[0] // 2:
        return fused(
            video_q, video_k, video_v, audio_q, audio_k, audio_v, video_x, audio_x,
            video_out_w, audio_out_w, video_gate_w, audio_gate_w, levels, video_pos, audio_pos, A, V,
        )
    rank = lax.axis_index(("vseq", "aseq"))
    frame_tokens = vrows * A * V // frames
    token = rank * vrows + jnp.arange(vrows, dtype=jnp.int32)
    frame_of = token // frame_tokens
    within = token % frame_tokens
    frame_ids = jnp.arange(frames, dtype=jnp.int32)
    video_hot = frame_of[:, None] == frame_ids[None, :]
    place_t = jnp.sum(jnp.where(video_hot, video_pos[None, :], 0), axis=1)
    zero = jnp.zeros_like(audio_pos)
    cos, sin = rope_tables(
        hd,
        jnp.concatenate([place_t, audio_pos]),
        jnp.concatenate([within // GRID_W, zero]),
        jnp.concatenate([within % GRID_W, zero]),
    )
    swap = swap_matrix(hd)

    def heads_first(video, audio):
        return jnp.swapaxes(jnp.concatenate([video, audio], axis=0), 0, 1)

    def rotate(x):
        other = jnp.dot(x, swap, preferred_element_type=jnp.float32)
        return (x.astype(jnp.float32) * cos[None] + other * sin[None]).astype(jnp.bfloat16)

    group = heads // A
    qkv = jnp.stack(
        [
            rotate(heads_first(video_q, audio_q)).reshape(A, group, rows, hd),
            rotate(heads_first(video_k, audio_k)).reshape(A, group, rows, hd),
            heads_first(video_v, audio_v).reshape(A, group, rows, hd),
        ],
        axis=1,
    )
    audio_frame = jnp.sum((video_pos[None, :] <= audio_pos[:, None]).astype(jnp.int32), axis=1) - 1
    audio_hot = audio_frame[:, None] == frame_ids[None, :]
    embedding = embedding_of(levels, video_gate_w.shape[0] // 2)

    def split_rows(hot):
        mine = jnp.sum(jnp.where(hot[:, :, None], embedding[None], 0.0), axis=1)
        high = mine.astype(jnp.bfloat16)
        rest = mine - high.astype(jnp.float32)
        mid = rest.astype(jnp.bfloat16)
        low = (rest - mid.astype(jnp.float32)).astype(jnp.bfloat16)
        return jnp.concatenate([high, mid, low], axis=0)

    one_frame = frame_tokens % vrows == 0
    ev = split_rows(video_hot[:8] if one_frame else video_hot)
    ea = split_rows(audio_hot)
    q, kv, gv, ga = gather(qkv, ev, ea, video_gate_w, audio_gate_w, A, V)
    va, aa = attend(q, kv, A, vrows, arows)
    return project(va, aa, video_out_w, audio_out_w, video_x, audio_x, gv, ga, A)


def solution(mesh):
    tokens = P(("vseq", "aseq"), None, None)
    wide = P(("vseq", "aseq"), None)
    return jax.shard_map(
        local,
        mesh=mesh,
        in_specs=(
            tokens, tokens, tokens, tokens, tokens, tokens, wide, wide,
            P("aseq", None), P("aseq", None), P(), P(), P(), P(), P(("vseq", "aseq")),
        ),
        out_specs=(wide, wide),
        check_vma=False,
    )
```
